32 devices in a mesh: table: 16 (over z, y, x), narrow: 2 (over core).
Axes of the slice: x: 2, y: 2, z: 4, core: 2. Of those that a mesh axis runs over, the one named last changes fastest.
Arguments:
- table_rows: bfloat16 [16384, 256], P('table'), may hold values from -3 to 3
- accum: float32 [16384], P('table'), may hold values from 1 to 100
- factor_down: bfloat16 [2048, 256], P('narrow'), may hold values from -0.125 to 0.125
- factor_up: bfloat16 [2048, 256], P('narrow'), may hold values from -0.375 to 0.375
- cross_bias: float32 [2048], replicated, may hold values from -3 to 3
- out_weight: bfloat16 [2048], replicated, may hold values from -0.125 to 0.125
- target: float32 [4096], P(('table', 'narrow')), may hold values from 0 to 1
- bag_rows: int32 [512, 512], P(('table', 'narrow')), may hold values from -1 to 1023, as said below
- slot_target: int32 [512, 128], P(('table', 'narrow')), may hold values from -1 to 1023, as said below
Outputs:
- logits: float32 [4096], P(('table', 'narrow'))
- down_grad: float32 [2048, 256], P('narrow')
- up_grad: float32 [2048, 256], P('narrow')
- new_rows: bfloat16 [16384, 256], P('table')
- new_accum: float32 [16384], P(('table', 'narrow'))
The draws below stay inside these ranges and needn't reach their ends.
Inputs may be any that keep to these rules, and one draw needn't show every extreme that they name: `slot_target`: for each source device (its 16 rows): every bag 0 .. 1023 is named by exactly one slot and the other slots hold -1; in every draw each source device has one window all of whose 128 slots are used. `bag_rows`: A used slot holds 1 to 4 rows of the window first and -1 after them; an unused slot holds -1 only; each source device has a slot with 4 lookups.
All inputs are finite; a program needn't handle non-finite values.
Results may differ from the reference program's by a relative error of at most 0.0077.
Values may be sent and summed in bfloat16 or wider, within the bound.
No kernel may reach another device: no remote copies, remote signals or barrier semaphores. Data moves between devices by JAX's collectives and lax.ppermute only.
A program may use at most 64 MiB of HBM per device.

```python
import math
import jax
import jax.numpy as jnp
from jax import lax

E = 256
FEAT = 8
R = 256
HOT = 4
B_DEV = 128
ROW_DEV = 1024
POOLS = 128
X = 2048
BATCH = 4096
ROWS = 16384
N_TABLE = 16
N_NARROW = 2


def layout(key):
    sources = N_TABLE * N_NARROW
    slot_count = N_TABLE * POOLS
    bag_count = B_DEV * FEAT
    base = jax.random.fold_in(key, 11)
    keys = jax.random.split(base, 6)
    levels = jax.random.randint(keys[0], (sources, N_TABLE), 0, 4)
    crowded = jax.random.randint(keys[1], (sources, 1), 0, N_TABLE)
    window_ids = lax.broadcasted_iota(jnp.int32, (sources, N_TABLE), 1)
    levels = jnp.where(window_ids == crowded, 12, levels)
    jitter = jax.random.randint(keys[2], (sources, N_TABLE, POOLS), 0, 256)
    slot_ids = lax.broadcasted_iota(jnp.int32, (sources, N_TABLE, POOLS), 1) * POOLS + lax.broadcasted_iota(jnp.int32, (sources, N_TABLE, POOLS), 2)
    scores = ((levels[:, :, None] * 64 + jitter) * slot_count + slot_ids).reshape(sources, slot_count)
    chosen = lax.top_k(scores, bag_count)[1].astype(jnp.int32)

    def shuffled(one_key):
        return jax.random.permutation(one_key, bag_count)
    orders = jax.vmap(shuffled)(jax.random.split(keys[3], sources)).astype(jnp.int32)
    source_index = lax.broadcasted_iota(jnp.int32, (sources, bag_count), 0)
    targets = jnp.full((sources, slot_count), -1, jnp.int32).at[source_index, chosen].set(orders)
    slot_iota = lax.broadcasted_iota(jnp.int32, (sources, slot_count), 1)
    leading = slot_iota == chosen[:, :1]
    lengths = jax.random.randint(keys[4], (sources, slot_count), 1, HOT + 1)
    lengths = jnp.where(leading, HOT, lengths)
    lengths = jnp.where(targets >= 0, lengths, 0)
    picks = jax.random.randint(keys[5], (sources, slot_count, HOT), 0, ROW_DEV)
    lookup_iota = lax.broadcasted_iota(jnp.int32, (sources, slot_count, HOT), 2)
    picks = jnp.where(leading[:, :, None] & (lookup_iota == 0), ROW_DEV - 1, picks)
    row_ids = jnp.where(lookup_iota < lengths[:, :, None], picks, -1)
    return (row_ids.reshape(sources * N_TABLE, POOLS * HOT), targets.reshape(sources * N_TABLE, POOLS))


def draw_bag_rows(key, part):
    return layout(key)[0]


def draw_slot_target(key, part):
    return layout(key)[1]


def steps_of(key, extent, pieces, least, largest):
    def one(axis_at, blocks):
        steps = jax.random.uniform(jax.random.fold_in(jax.random.fold_in(key, 6), axis_at), (blocks,), jnp.float32, least / len(pieces), largest / len(pieces))
        return jnp.repeat(jnp.exp(steps), extent[axis_at] // blocks).reshape((-1,) + (1,) * (len(extent) - axis_at - 1))

    loudness = one(*pieces[0])
    for cut in pieces[1:]:
        loudness = loudness * one(*cut)
    return loudness


def gaussian(key, extent, width, limit, cuts=(), held_as=jnp.bfloat16):
    gain = steps_of(key, extent, cuts, -0.22, 0.18) if cuts else 1.0
    values = jax.random.normal(key, extent, jnp.float32) * width * gain
    return jnp.minimum(jnp.maximum(values, -limit), limit).astype(held_as)


def setup_inputs(seed: int = 0) -> dict:
    splits = jax.random.split(jax.random.key(seed), 10)
    table_rows = gaussian(splits[0], (ROWS, E), 0.5, 3.0, ((0, 16),))
    accum = jnp.clip(jnp.exp(math.log(100.0) - 4.6051702 * jax.random.uniform(splits[1], (ROWS,), jnp.float32) ** steps_of(splits[1], (ROWS,), ((0, 16),), -0.2, 0.2)), 1.0, 100.0)
    factor_down = gaussian(splits[2], (X, R), X ** -0.5, 0.125, ((0, 2),))
    factor_up = gaussian(splits[3], (X, R), R ** -0.5, 0.375, ((0, 2),))
    cross_bias = gaussian(splits[4], (X,), 0.5, 3.0, (), jnp.float32)
    out_weight = gaussian(splits[5], (X,), X ** -0.5, 0.125)
    target = jnp.clip(1.0 * jax.random.uniform(splits[6], (BATCH,), jnp.float32) ** steps_of(splits[6], (BATCH,), ((0, 32),), -0.2, 0.2), 0.0, 1.0)
    bag_rows = draw_bag_rows(jax.random.fold_in(splits[9], 71), 0)
    slot_target = draw_slot_target(jax.random.fold_in(splits[9], 71), 0)
    return {"table_rows": table_rows, "accum": accum, "factor_down": factor_down, "factor_up": factor_up, "cross_bias": cross_bias, "out_weight": out_weight, "target": target, "bag_rows": bag_rows, "slot_target": slot_target}


LEARN_RATE = 0.2
LOSS_SCALE = 32.0
ADA_EPS = 1e-06

def reference(table_rows, accum, factor_down, factor_up, cross_bias, out_weight, target, bag_rows, slot_target):
    sources = N_TABLE * N_NARROW
    bag_count = B_DEV * FEAT
    windows = table_rows.reshape(N_TABLE, ROW_DEV, E)
    rows_all = bag_rows.reshape(sources, N_TABLE, POOLS, HOT)
    targets_all = slot_target.reshape(sources, N_TABLE * POOLS)
    labels_all = target.reshape(sources, B_DEV)
    weight_f = out_weight.astype(jnp.float32)
    window_ids = jnp.arange(N_TABLE, dtype=jnp.int32)[:, None, None]

    def pick_rows(window, picks):
        return window[picks]

    def one_source(carried, source):
        dense_sum, row_sum = carried
        row_ids = lax.dynamic_index_in_dim(rows_all, source, 0, keepdims=False)
        is_live = row_ids >= 0
        safe_rows = jnp.where(is_live, row_ids, 0)
        picked = jax.vmap(pick_rows)(windows, safe_rows).astype(jnp.float32)
        pool_sums = lax.optimization_barrier(jnp.sum(jnp.where(is_live[..., None], picked, 0.0), axis=2)).astype(jnp.bfloat16)
        slot_goal = lax.dynamic_index_in_dim(targets_all, source, 0, keepdims=False)
        segment_ids = jnp.where(slot_goal >= 0, slot_goal, bag_count)
        placed = jax.ops.segment_sum(pool_sums.reshape(N_TABLE * POOLS, E).astype(jnp.float32), segment_ids, num_segments=bag_count + 1)
        pooled_feats = placed[:bag_count].astype(jnp.bfloat16).reshape(B_DEV, FEAT * E)
        hidden = jnp.dot(pooled_feats, factor_down, preferred_element_type=jnp.float32).astype(jnp.bfloat16)
        cross_out = jnp.dot(hidden, factor_up.T, preferred_element_type=jnp.float32)
        feats_f = pooled_feats.astype(jnp.float32)
        shifted = cross_out + cross_bias
        mixed_out = feats_f * shifted + feats_f
        logits = lax.optimization_barrier(jnp.sum(mixed_out * weight_f, axis=1))
        labels = lax.dynamic_index_in_dim(labels_all, source, 0, keepdims=False)
        dlogit = LOSS_SCALE * (jax.nn.sigmoid(logits) - labels)
        dmixed = dlogit[:, None] * weight_f
        dcross = (dmixed * feats_f).astype(jnp.bfloat16)
        dhidden = jnp.dot(dcross, factor_up, preferred_element_type=jnp.float32).astype(jnp.bfloat16)
        back_term = jnp.dot(dhidden, factor_down.T, preferred_element_type=jnp.float32)
        dpooled = (dmixed * (shifted + 1.0) + back_term).astype(jnp.bfloat16)
        grad_down = jnp.dot(pooled_feats.T, dhidden, preferred_element_type=jnp.float32)
        grad_up = jnp.dot(dcross.T, hidden, preferred_element_type=jnp.float32)
        partial_value = jnp.concatenate([grad_down, grad_up], axis=1)
        partial_value = lax.optimization_barrier(partial_value.astype(jnp.bfloat16)).astype(jnp.float32)
        bag_grads = dpooled.reshape(bag_count, E)
        slot_grads = jnp.where((slot_goal >= 0)[:, None], bag_grads[jnp.where(slot_goal >= 0, slot_goal, 0)], jnp.zeros((), jnp.bfloat16))
        contrib = jnp.where(is_live[..., None], slot_grads.reshape(N_TABLE, POOLS, 1, E).astype(jnp.float32), 0.0)
        row_sum = row_sum.at[window_ids, safe_rows].add(contrib)
        return ((dense_sum + partial_value, row_sum), logits)
    start = (jnp.zeros((X, 2 * R), jnp.float32), jnp.zeros((N_TABLE, ROW_DEV, E), jnp.float32))
    (dense_sum, row_sum), logits = lax.scan(one_source, start, jnp.arange(sources, dtype=jnp.int32))
    dense_sum = dense_sum * (1.0 / math.sqrt(BATCH))
    row_grad = row_sum.reshape(ROWS, E)
    new_accum = accum + lax.optimization_barrier(jnp.mean(row_grad * row_grad, axis=1))
    new_rows = (table_rows.astype(jnp.float32) - LEARN_RATE * row_grad * lax.rsqrt(new_accum + ADA_EPS)[:, None]).astype(jnp.bfloat16)
    return (logits.reshape(BATCH), dense_sum[:, :R], dense_sum[:, R:], new_rows, new_accum)
```

```python
import math

import jax
import jax.numpy as jnp
from jax import lax
from jax.sharding import PartitionSpec as P

FEAT = 8
HOT = 4


LEARN_RATE = 0.2
LOSS_SCALE = 32.0
ADA_EPS = 1e-06


def transposed_dot(left, right):
    return lax.dot_general(
        left, right, (((0,), (0,)), ((), ())), preferred_element_type=jnp.float32
    )


def rows_dot(left, right):
    return lax.dot_general(
        left, right, (((1,), (1,)), ((), ())), preferred_element_type=jnp.float32
    )


def group_levels(size):
    levels = []
    stride = 1
    while size % 4 == 0:
        levels.append((stride, 4))
        stride, size = stride * 4, size // 4
    if size > 1:
        levels.append((stride, size))
    return levels


def partner_index(index, stride, group, step):
    place = (index // stride) % group
    if group & (group - 1) == 0:
        other = place ^ step
    else:
        other = (place + step) % group
    return index + (other - place) * stride


def sent_from(axis, stride, group, step):
    size = lax.axis_size(axis)
    return [(partner_index(i, stride, group, step), i) for i in range(size)]


def scatter_sum(blocks, axis, levels):
    index = lax.axis_index(axis)
    for stride, group in levels:
        rows = blocks.shape[0] // group
        place = (index // stride) % group
        total = lax.dynamic_slice_in_dim(blocks, place * rows, rows, 0).astype(jnp.float32)
        for step in range(1, group):
            pairs = sent_from(axis, stride, group, step)
            if group & (group - 1) == 0:
                goal = place ^ step
            else:
                goal = (place + group - step) % group
            outgoing = lax.dynamic_slice_in_dim(blocks, goal * rows, rows, 0)
            total = total + lax.ppermute(outgoing, axis, pairs).astype(jnp.float32)
        blocks = total.astype(jnp.bfloat16)
    return blocks


def gather_blocks(block, axis, levels):
    index = lax.axis_index(axis)
    for stride, group in reversed(levels):
        rows = block.shape[0]
        place = (index // stride) % group
        whole = jnp.zeros((group * rows,) + block.shape[1:], block.dtype)
        whole = lax.dynamic_update_slice_in_dim(whole, block, place * rows, 0)
        for step in range(1, group):
            origin = partner_index(index, stride, group, step)
            came = lax.ppermute(block, axis, sent_from(axis, stride, group, step))
            spot = (origin // stride) % group
            whole = lax.dynamic_update_slice_in_dim(whole, came, spot * rows, 0)
        block = whole
    return block


def local(
    table_rows, accum, factor_down, factor_up, cross_bias, out_weight, target, bag_rows, slot_target
):
    tables = lax.axis_size("table")
    narrows = lax.axis_size("narrow")
    row_dev, emb_width = table_rows.shape
    pools_per = slot_target.shape[1]
    samples = target.shape[0]
    bag_count = samples * FEAT
    slot_count = tables * pools_per
    asked = lax.all_to_all(bag_rows, "table", split_axis=0, concat_axis=0, tiled=True)
    lookup_ids = asked.reshape(slot_count, HOT)
    positions = lax.broadcasted_iota(jnp.int32, (1, row_dev), 1)
    counts = jnp.zeros((slot_count, row_dev), jnp.bfloat16)
    for lookup in range(HOT):
        counts = counts + (lookup_ids[:, lookup : lookup + 1] == positions).astype(jnp.bfloat16)
    pool_sums = jnp.dot(counts, table_rows, preferred_element_type=jnp.float32)
    pool_out = pool_sums.astype(jnp.bfloat16).reshape(tables, pools_per, emb_width)
    arrived = lax.all_to_all(pool_out, "table", split_axis=0, concat_axis=0, tiled=True).reshape(
        slot_count, emb_width
    )
    bag_index = lax.broadcasted_iota(jnp.int32, (bag_count, 1), 0)
    placing = (slot_target.reshape(1, slot_count) == bag_index).astype(jnp.bfloat16)
    pooled_feats = (
        jnp.dot(placing, arrived, preferred_element_type=jnp.float32)
        .astype(jnp.bfloat16)
        .reshape(samples, FEAT * emb_width)
    )
    narrow_levels = group_levels(narrows)
    table_levels = group_levels(tables)
    down_full = gather_blocks(factor_down, "narrow", narrow_levels)
    up_full = gather_blocks(factor_up, "narrow", narrow_levels)
    hidden = jnp.dot(pooled_feats, down_full, preferred_element_type=jnp.float32).astype(
        jnp.bfloat16
    )
    cross_out = rows_dot(hidden, up_full)
    feats_f = pooled_feats.astype(jnp.float32)
    shifted = cross_out + cross_bias
    mixed_out = feats_f * shifted + feats_f
    weight_f = out_weight.astype(jnp.float32)
    logits = jnp.sum(mixed_out * weight_f, axis=1)
    dlogit = LOSS_SCALE * (jax.nn.sigmoid(logits) - target)
    dmixed = dlogit[:, None] * weight_f
    dcross = (dmixed * feats_f).astype(jnp.bfloat16)
    dhidden = jnp.dot(dcross, up_full, preferred_element_type=jnp.float32).astype(jnp.bfloat16)
    back_term = rows_dot(dhidden, down_full)
    dpooled = (dmixed * (shifted + 1.0) + back_term).astype(jnp.bfloat16)
    grad_terms = jnp.concatenate(
        [transposed_dot(pooled_feats, dhidden), transposed_dot(dcross, hidden)], axis=1
    ).astype(jnp.bfloat16)
    narrow_sum = scatter_sum(grad_terms, "narrow", narrow_levels)
    table_sum = scatter_sum(narrow_sum, "table", table_levels)
    grand_total = gather_blocks(table_sum, "table", table_levels).astype(jnp.float32)
    batch_all = samples * tables * narrows
    grand_total = grand_total * (1.0 / math.sqrt(batch_all))
    rank_size = factor_down.shape[1]
    down_grad = grand_total[:, :rank_size]
    up_grad = grand_total[:, rank_size:]
    bag_grads = dpooled.reshape(bag_count, emb_width)
    slot_grads = (
        transposed_dot(placing, bag_grads)
        .astype(jnp.bfloat16)
        .reshape(tables, pools_per, emb_width)
    )
    returned = lax.all_to_all(slot_grads, "table", split_axis=0, concat_axis=0, tiled=True).reshape(
        slot_count, emb_width
    )
    local_grad = transposed_dot(counts, returned)
    narrow_index = lax.axis_index("narrow")
    share_size = row_dev // narrows
    sent_grad = local_grad.astype(jnp.bfloat16)
    if narrows == 2:
        other_grad = lax.ppermute(sent_grad, "narrow", sent_from("narrow", 1, 2, 1))
        row_grad = sent_grad.astype(jnp.float32) + other_grad.astype(jnp.float32)
    else:
        share = scatter_sum(sent_grad, "narrow", narrow_levels)
        row_grad = gather_blocks(share, "narrow", narrow_levels).astype(jnp.float32)
    accum_all = accum + jnp.mean(row_grad * row_grad, axis=1)
    new_rows = (
        table_rows.astype(jnp.float32)
        - LEARN_RATE * row_grad * lax.rsqrt(accum_all + ADA_EPS)[:, None]
    ).astype(jnp.bfloat16)
    new_accum = lax.dynamic_slice_in_dim(accum_all, narrow_index * share_size, share_size, 0)
    return (logits, down_grad, up_grad, new_rows, new_accum)


def solution(mesh):
    in_specs = (
        P("table", None),
        P("table"),
        P("narrow", None),
        P("narrow", None),
        P(),
        P(),
        P(("table", "narrow")),
        P(("table", "narrow"), None),
        P(("table", "narrow"), None),
    )
    out_specs = (
        P(("table", "narrow")),
        P("narrow", None),
        P("narrow", None),
        P("table", None),
        P(("table", "narrow")),
    )
    return jax.shard_map(local, mesh=mesh, in_specs=in_specs, out_specs=out_specs, check_vma=False)
```

```python
import math

import jax
import jax.numpy as jnp
from jax import lax
from jax.experimental import pallas as pl
from jax.experimental.pallas import tpu as pltpu
from jax.sharding import PartitionSpec as P

FEAT = 8
HOT = 4


LEARN_RATE = 0.2
LOSS_SCALE = 32.0
ADA_EPS = 1e-06


SLOTS = 128
VMEM_BYTES = 48 * 1024 * 1024


def matmul(left, right):
    return jnp.dot(left, right, preferred_element_type=jnp.float32)


def transposed_dot(left, right):
    return lax.dot_general(
        left, right, (((0,), (0,)), ((), ())), preferred_element_type=jnp.float32
    )


def rows_dot(left, right):
    return lax.dot_general(
        left, right, (((1,), (1,)), ((), ())), preferred_element_type=jnp.float32
    )


def kernel_call(kernel, out_shape, cost, scratch=()):
    flops, moved = cost
    return pl.pallas_call(
        kernel,
        out_shape=out_shape,
        scratch_shapes=scratch,
        compiler_params=pltpu.CompilerParams(vmem_limit_bytes=VMEM_BYTES),
        cost_estimate=pl.CostEstimate(flops=flops, bytes_accessed=moved, transcendentals=0),
    )


def split_ids(ids):
    shifted = ids + 1
    high = lax.shift_right_logical(shifted, 5).astype(jnp.float32).astype(jnp.bfloat16)
    low = (shifted & 31).astype(jnp.float32).astype(jnp.bfloat16)
    return high, low


def lookup_choice():
    shape = (HOT * SLOTS, HOT * SLOTS)
    row = lax.broadcasted_iota(jnp.int32, shape, 0)
    column = lax.broadcasted_iota(jnp.int32, shape, 1)
    wanted = (row & (SLOTS - 1)) * HOT + lax.shift_right_logical(row, 7)
    return jnp.where(wanted == column, 1.0, 0.0).astype(jnp.bfloat16)


def pool_kernel(ids_ref, rows_ref, out_ref):
    blocks = ids_ref.shape[0]
    high, low = split_ids(ids_ref[...])
    choice = lookup_choice()
    columns = (rows_dot(choice, high) * 32.0 + rows_dot(choice, low) - 1.0).astype(jnp.int32)
    rows = rows_ref[...]
    position = lax.broadcasted_iota(jnp.int32, (SLOTS, rows.shape[0]), 1)
    for block in range(blocks):
        counts = jnp.zeros((SLOTS, rows.shape[0]), jnp.float32)
        for lookup in range(HOT):
            column = columns[lookup * SLOTS : (lookup + 1) * SLOTS, block : block + 1]
            counts = counts + jnp.where(column == position, 1.0, 0.0)
        sums = matmul(counts.astype(jnp.bfloat16), rows)
        out_ref[block * SLOTS : (block + 1) * SLOTS, :] = sums.astype(jnp.bfloat16)


def pool_lookups(ids, rows):
    blocks = ids.shape[0]
    flops = 2 * blocks * SLOTS * rows.size
    return kernel_call(
        pool_kernel,
        jax.ShapeDtypeStruct((blocks * SLOTS, rows.shape[1]), jnp.bfloat16),
        (flops, 2 * rows.size + 2 * blocks * SLOTS * rows.shape[1]),
    )(ids, rows)


def counts_kernel(ids_ref, out_ref):
    blocks = ids_ref.shape[0]
    row_dev = out_ref.shape[0]
    high, low = split_ids(ids_ref[...])
    choice = lookup_choice()
    lines = (rows_dot(high, choice) * 32.0 + rows_dot(low, choice) - 1.0).astype(jnp.int32)
    position = lax.broadcasted_iota(jnp.int32, (row_dev, SLOTS), 0)
    for block in range(blocks):
        counts = jnp.zeros((row_dev, SLOTS), jnp.float32)
        for lookup in range(HOT):
            line = lines[block : block + 1, lookup * SLOTS : (lookup + 1) * SLOTS]
            counts = counts + jnp.where(line == position, 1.0, 0.0)
        out_ref[:, block * SLOTS : (block + 1) * SLOTS] = counts.astype(jnp.bfloat16)


def lookup_counts(ids, row_dev):
    slot_count = ids.size // HOT
    return kernel_call(
        counts_kernel,
        jax.ShapeDtypeStruct((row_dev, slot_count), jnp.bfloat16),
        (8 * row_dev * slot_count, 2 * row_dev * slot_count),
    )(ids)


def diagonal(size):
    row = lax.broadcasted_iota(jnp.int32, (size, size), 0)
    return row == lax.broadcasted_iota(jnp.int32, (size, size), 1)


def as_column(line):
    return jnp.sum(jnp.where(diagonal(line.shape[1]), line, 0.0), axis=1, keepdims=True)


def as_line(column):
    return jnp.sum(jnp.where(diagonal(column.shape[0]), column, 0.0), axis=0, keepdims=True)


def dense_kernel(
    place_ref,
    unplace_ref,
    arrived_ref,
    down_ref,
    up_ref,
    bias_ref,
    weight_ref,
    target_ref,
    logits_ref,
    slot_ref,
    terms_ref,
):
    samples = target_ref.shape[1]
    width, rank = down_ref.shape
    emb = width // FEAT
    arrived = arrived_ref[...]
    features = [slice(f * emb, (f + 1) * emb) for f in range(FEAT)]
    pooled = [
        matmul(place_ref[f * samples : (f + 1) * samples, :], arrived).astype(jnp.bfloat16)
        for f in range(FEAT)
    ]
    hidden = jnp.zeros((samples, rank), jnp.float32)
    for f, part in enumerate(features):
        hidden = hidden + matmul(pooled[f], down_ref[part, :])
    hidden = hidden.astype(jnp.bfloat16)
    shifted = []
    summed = jnp.zeros((samples, emb), jnp.float32)
    for f, part in enumerate(features):
        shifted.append(rows_dot(hidden, up_ref[part, :]) + bias_ref[:, part])
        feats = pooled[f].astype(jnp.float32)
        summed = summed + (feats * shifted[f] + feats) * weight_ref[:, part].astype(jnp.float32)
    logits = jnp.sum(summed, axis=1, keepdims=True)
    logits_ref[...] = as_line(logits)
    dlogit = LOSS_SCALE * (jax.nn.sigmoid(logits) - as_column(target_ref[...]))
    dcross = []
    dhidden = jnp.zeros((samples, rank), jnp.float32)
    for f, part in enumerate(features):
        dmixed = dlogit * weight_ref[:, part].astype(jnp.float32)
        dcross.append((dmixed * pooled[f].astype(jnp.float32)).astype(jnp.bfloat16))
        dhidden = dhidden + matmul(dcross[f], up_ref[part, :])
    dhidden = dhidden.astype(jnp.bfloat16)
    dpooled = []
    for f, part in enumerate(features):
        dmixed = dlogit * weight_ref[:, part].astype(jnp.float32)
        back_term = rows_dot(dhidden, down_ref[part, :])
        dpooled.append((dmixed * (shifted[f] + 1.0) + back_term).astype(jnp.bfloat16))
        terms_ref[part, :rank] = transposed_dot(pooled[f], dhidden).astype(jnp.bfloat16)
        terms_ref[part, rank:] = transposed_dot(dcross[f], hidden).astype(jnp.bfloat16)
    bag_grads = jnp.concatenate(dpooled, axis=0)
    for start in range(0, slot_ref.shape[0], 256):
        picked = matmul(unplace_ref[start : start + 256, :], bag_grads)
        slot_ref[start : start + 256, :] = picked.astype(jnp.bfloat16)


def dense_step(place, unplace, arrived, down_full, up_full, bias, weight, target):
    samples = target.shape[0]
    slot_count, emb = arrived.shape
    width, rank = down_full.shape
    flops = 4 * slot_count * samples * width + 12 * samples * width * rank
    moved = 4 * place.size + 4 * arrived.size + 8 * down_full.size
    logits, slot_grads, terms = kernel_call(
        dense_kernel,
        (
            jax.ShapeDtypeStruct((1, samples), jnp.float32),
            jax.ShapeDtypeStruct((slot_count, emb), jnp.bfloat16),
            jax.ShapeDtypeStruct((width, 2 * rank), jnp.bfloat16),
        ),
        (flops, moved),
    )(
        place,
        unplace,
        arrived,
        down_full,
        up_full,
        bias.reshape(1, width),
        weight.reshape(1, width),
        target.reshape(1, samples),
    )
    return logits.reshape(samples), slot_grads, terms


def update_kernel(share_ref, rows_ref, mine_ref, other_ref, accum_ref, rows_out_ref, accum_out_ref):
    chunks = accum_ref.shape[0]
    per_share = accum_out_ref.shape[0]
    for chunk in range(chunks):
        part = slice(chunk * SLOTS, (chunk + 1) * SLOTS)
        row_grad = mine_ref[part, :].astype(jnp.float32) + other_ref[part, :].astype(jnp.float32)
        squares = jnp.mean(row_grad * row_grad, axis=1, keepdims=True)
        accum = as_column(accum_ref[chunk : chunk + 1, :]) + squares
        step = LEARN_RATE * row_grad * lax.rsqrt(accum + ADA_EPS)
        rows_out_ref[part, :] = (rows_ref[part, :].astype(jnp.float32) - step).astype(jnp.bfloat16)

        @pl.when(share_ref[0] == chunk // per_share)
        def _():
            accum_out_ref[chunk % per_share : chunk % per_share + 1, :] = as_line(accum)


def update_rows(share, rows, mine, other, accum, narrows):
    row_dev, emb = rows.shape
    chunks = row_dev // SLOTS
    vmem = pl.BlockSpec(memory_space=pltpu.VMEM)
    new_rows, new_accum = pl.pallas_call(
        update_kernel,
        in_specs=[pl.BlockSpec(memory_space=pltpu.SMEM), vmem, vmem, vmem, vmem],
        out_shape=(
            jax.ShapeDtypeStruct((row_dev, emb), jnp.bfloat16),
            jax.ShapeDtypeStruct((chunks // narrows, SLOTS), jnp.float32),
        ),
        compiler_params=pltpu.CompilerParams(vmem_limit_bytes=VMEM_BYTES),
        cost_estimate=pl.CostEstimate(
            flops=8 * rows.size, bytes_accessed=8 * rows.size, transcendentals=row_dev
        ),
    )(share.reshape(1), rows, mine, other, accum.reshape(chunks, SLOTS))
    return new_rows, new_accum.reshape(row_dev // narrows)


def group_levels(size):
    levels = []
    stride = 1
    while size % 4 == 0:
        levels.append((stride, 4))
        stride, size = stride * 4, size // 4
    if size > 1:
        levels.append((stride, size))
    return levels


def partner_index(index, stride, group, step):
    place = (index // stride) % group
    if group & (group - 1) == 0:
        other = place ^ step
    else:
        other = (place + step) % group
    return index + (other - place) * stride


def sent_from(axis, stride, group, step):
    size = lax.axis_size(axis)
    return [(partner_index(i, stride, group, step), i) for i in range(size)]


def scatter_sum(blocks, axis, levels):
    index = lax.axis_index(axis)
    for stride, group in levels:
        rows = blocks.shape[0] // group
        place = (index // stride) % group
        total = lax.dynamic_slice_in_dim(blocks, place * rows, rows, 0).astype(jnp.float32)
        for step in range(1, group):
            pairs = sent_from(axis, stride, group, step)
            if group & (group - 1) == 0:
                goal = place ^ step
            else:
                goal = (place + group - step) % group
            outgoing = lax.dynamic_slice_in_dim(blocks, goal * rows, rows, 0)
            total = total + lax.ppermute(outgoing, axis, pairs).astype(jnp.float32)
        blocks = total.astype(jnp.bfloat16)
    return blocks


def gather_blocks(block, axis, levels):
    index = lax.axis_index(axis)
    for stride, group in reversed(levels):
        rows = block.shape[0]
        place = (index // stride) % group
        whole = jnp.zeros((group * rows,) + block.shape[1:], block.dtype)
        whole = lax.dynamic_update_slice_in_dim(whole, block, place * rows, 0)
        for step in range(1, group):
            origin = partner_index(index, stride, group, step)
            came = lax.ppermute(block, axis, sent_from(axis, stride, group, step))
            spot = (origin // stride) % group
            whole = lax.dynamic_update_slice_in_dim(whole, came, spot * rows, 0)
        block = whole
    return block


def local(
    table_rows, accum, factor_down, factor_up, cross_bias, out_weight, target, bag_rows, slot_target
):
    tables = lax.axis_size("table")
    narrows = lax.axis_size("narrow")
    row_dev, emb_width = table_rows.shape
    pools_per = slot_target.shape[1]
    samples = target.shape[0]
    bag_count = samples * FEAT
    slot_count = tables * pools_per
    narrow_levels = group_levels(narrows)
    table_levels = group_levels(tables)
    down_full = gather_blocks(factor_down, "narrow", narrow_levels)
    up_full = gather_blocks(factor_up, "narrow", narrow_levels)
    asked = lax.all_to_all(bag_rows, "table", split_axis=0, concat_axis=0, tiled=True)
    lookup_ids = asked.reshape(slot_count // SLOTS, SLOTS * HOT)
    pool_out = pool_lookups(lookup_ids, table_rows).reshape(tables, pools_per, emb_width)
    arrived = lax.all_to_all(pool_out, "table", split_axis=0, concat_axis=0, tiled=True).reshape(
        slot_count, emb_width
    )
    order = jnp.arange(bag_count, dtype=jnp.int32)
    order = (order % samples) * FEAT + order // samples
    goals = slot_target.reshape(1, slot_count)
    place = (goals == order[:, None]).astype(jnp.bfloat16)
    unplace = (goals.reshape(slot_count, 1) == order[None, :]).astype(jnp.bfloat16)
    logits, slot_grads, grad_terms = dense_step(
        place, unplace, arrived, down_full, up_full, cross_bias, out_weight, target
    )
    narrow_sum = scatter_sum(grad_terms, "narrow", narrow_levels)
    returned = lax.all_to_all(
        slot_grads.reshape(tables, pools_per, emb_width),
        "table",
        split_axis=0,
        concat_axis=0,
        tiled=True,
    ).reshape(slot_count, emb_width)
    table_sum = scatter_sum(narrow_sum, "table", table_levels)
    sent_grad = matmul(lookup_counts(lookup_ids, row_dev), returned).astype(jnp.bfloat16)
    table_sum, sent_grad = lax.optimization_barrier((table_sum, sent_grad))
    grand_total = gather_blocks(table_sum, "table", table_levels).astype(jnp.float32)
    batch_all = samples * tables * narrows
    grand_total = grand_total * (1.0 / math.sqrt(batch_all))
    rank_size = factor_down.shape[1]
    down_grad = grand_total[:, :rank_size]
    up_grad = grand_total[:, rank_size:]
    if narrows == 2:
        mine = sent_grad
        other = lax.ppermute(sent_grad, "narrow", sent_from("narrow", 1, 2, 1))
    else:
        share = scatter_sum(sent_grad, "narrow", narrow_levels)
        mine = gather_blocks(share, "narrow", narrow_levels)
        other = jnp.zeros_like(mine)
    new_rows, new_accum = update_rows(
        lax.axis_index("narrow"), table_rows, mine, other, accum, narrows
    )
    return (logits, down_grad, up_grad, new_rows, new_accum)


def solution(mesh):
    in_specs = (
        P("table", None),
        P("table"),
        P("narrow", None),
        P("narrow", None),
        P(),
        P(),
        P(("table", "narrow")),
        P(("table", "narrow"), None),
        P(("table", "narrow"), None),
    )
    out_specs = (
        P(("table", "narrow")),
        P("narrow", None),
        P("narrow", None),
        P("table", None),
        P(("table", "narrow")),
    )
    return jax.shard_map(local, mesh=mesh, in_specs=in_specs, out_specs=out_specs, check_vma=False)
```

```python
import functools
import math

import jax
import jax.numpy as jnp
from jax import lax
from jax.experimental import pallas as pl
from jax.experimental.pallas import tpu as pltpu
from jax.sharding import PartitionSpec as P

FEAT = 8
HOT = 4


LEARN_RATE = 0.2
LOSS_SCALE = 32.0
ADA_EPS = 1e-06


SLOTS = 128
VMEM_BYTES = 48 * 1024 * 1024


def matmul(left, right):
    return jnp.dot(left, right, preferred_element_type=jnp.float32)


def transposed_dot(left, right):
    return lax.dot_general(
        left, right, (((0,), (0,)), ((), ())), preferred_element_type=jnp.float32
    )


def rows_dot(left, right):
    return lax.dot_general(
        left, right, (((1,), (1,)), ((), ())), preferred_element_type=jnp.float32
    )


def kernel_call(kernel, out_shape, cost, scratch=(), flags=0, operands=0):
    flops, moved = cost
    smem = pl.BlockSpec(memory_space=pltpu.SMEM)
    vmem = pl.BlockSpec(memory_space=pltpu.VMEM)
    return pl.pallas_call(
        kernel,
        in_specs=[smem] * flags + [vmem] * operands,
        out_shape=out_shape,
        scratch_shapes=scratch,
        compiler_params=pltpu.CompilerParams(vmem_limit_bytes=VMEM_BYTES),
        cost_estimate=pl.CostEstimate(flops=flops, bytes_accessed=moved, transcendentals=0),
    )


def split_ids(ids):
    shifted = ids + 1
    high = lax.shift_right_logical(shifted, 5).astype(jnp.float32).astype(jnp.bfloat16)
    low = (shifted & 31).astype(jnp.float32).astype(jnp.bfloat16)
    return high, low


def lookup_choice():
    shape = (HOT * SLOTS, HOT * SLOTS)
    row = lax.broadcasted_iota(jnp.int32, shape, 0)
    column = lax.broadcasted_iota(jnp.int32, shape, 1)
    wanted = (row & (SLOTS - 1)) * HOT + lax.shift_right_logical(row, 7)
    return jnp.where(wanted == column, 1.0, 0.0).astype(jnp.bfloat16)


def joined(digits):
    high, low = digits
    return (high * 32.0 + low - 1.0).astype(jnp.int32)


def ones_where(mask):
    return jnp.where(mask, jnp.asarray(1, jnp.bfloat16), jnp.asarray(0, jnp.bfloat16))


def pool_kernel(offset, swap_ref, ids_ref, first_ref, second_ref, out_ref, counts_ref):
    blocks = ids_ref.shape[0]
    half = first_ref.shape[0]
    high, low = split_ids(ids_ref[:, offset : offset + HOT * SLOTS])
    choice = lookup_choice()
    columns = joined((rows_dot(choice, high), rows_dot(choice, low))).astype(jnp.int16)
    position = lax.broadcasted_iota(jnp.int32, (SLOTS, 2 * half), 1)
    shifted = position + swap_ref[0] * half
    position = jnp.where(shifted >= 2 * half, shifted - 2 * half, shifted).astype(jnp.int16)
    for block in range(blocks):
        counts = None
        for lookup in range(HOT):
            column = columns[lookup * SLOTS : (lookup + 1) * SLOTS, block : block + 1]
            found = ones_where(column == position)
            counts = found if counts is None else counts + found
        counts_ref[block * SLOTS : (block + 1) * SLOTS, :] = counts
    sums = matmul(counts_ref[:, :half], first_ref[...])
    sums = sums + matmul(counts_ref[:, half:], second_ref[...])
    out_ref[...] = sums.astype(jnp.bfloat16)


def pool_lookups(ids, offset, swap, first, second):
    blocks = ids.shape[0]
    half, width = first.shape
    slots = blocks * SLOTS
    return kernel_call(
        functools.partial(pool_kernel, offset),
        jax.ShapeDtypeStruct((slots, width), jnp.bfloat16),
        (4 * slots * half * width, 4 * half * width + 2 * slots * width),
        [pltpu.VMEM((slots, 2 * half), jnp.bfloat16)],
        flags=1,
        operands=3,
    )(swap, ids, first, second)


def counts_kernel(ids_ref, out_ref):
    blocks = ids_ref.shape[0]
    row_dev = out_ref.shape[0]
    tile = 64
    high, low = split_ids(ids_ref[...])
    choice = lookup_choice()
    lines = joined((rows_dot(high, choice), rows_dot(low, choice)))
    position = lax.broadcasted_iota(jnp.int32, (tile, SLOTS), 0).astype(jnp.int16)
    for block in range(blocks):
        spread = []
        for lookup in range(HOT):
            line = lines[block : block + 1, lookup * SLOTS : (lookup + 1) * SLOTS]
            spread.append(jnp.broadcast_to(line, (tile, SLOTS)).astype(jnp.int16))
        for start in range(0, row_dev, tile):
            counts = None
            for lookup in range(HOT):
                found = ones_where(spread[lookup] - jnp.asarray(start, jnp.int16) == position)
                counts = found if counts is None else counts + found
            out_ref[start : start + tile, block * SLOTS : (block + 1) * SLOTS] = counts


def lookup_counts(ids, row_dev):
    slot_count = ids.size // HOT
    return kernel_call(
        counts_kernel,
        jax.ShapeDtypeStruct((row_dev, slot_count), jnp.bfloat16),
        (8 * row_dev * slot_count, 2 * row_dev * slot_count),
        operands=1,
    )(ids)


def diagonal(size):
    row = lax.broadcasted_iota(jnp.int32, (size, size), 0)
    return row == lax.broadcasted_iota(jnp.int32, (size, size), 1)


def as_column(line):
    return jnp.sum(jnp.where(diagonal(line.shape[1]), line, 0.0), axis=1, keepdims=True)


def as_line(column):
    return jnp.sum(jnp.where(diagonal(column.shape[0]), column, 0.0), axis=0, keepdims=True)


def dense_kernel(
    swap_ref,
    goals_ref,
    near_ref,
    far_ref,
    down_a_ref,
    down_b_ref,
    up_a_ref,
    up_b_ref,
    bias_ref,
    weight_ref,
    target_ref,
    logits_ref,
    grads_ref,
    kept_ref,
    sent_ref,
    place_ref,
    wide_ref,
    cross_ref,
    down_ref,
    up_ref,
):
    samples = target_ref.shape[1]
    width, rank = down_ref.shape
    emb = width // FEAT
    slots = near_ref.shape[0]
    half = width // 2
    swapped = swap_ref[0] == 1
    down_ref[:half, :] = jnp.where(swapped, down_b_ref[...], down_a_ref[...])
    down_ref[half:, :] = jnp.where(swapped, down_a_ref[...], down_b_ref[...])
    up_ref[:half, :] = jnp.where(swapped, up_b_ref[...], up_a_ref[...])
    up_ref[half:, :] = jnp.where(swapped, up_a_ref[...], up_b_ref[...])
    features = [slice(f * emb, (f + 1) * emb) for f in range(FEAT)]
    chunk = 512
    first_bag = lax.broadcasted_iota(jnp.int32, (samples, chunk), 0) * FEAT
    for start in range(0, goals_ref.shape[1], chunk):
        line = goals_ref[:, start : start + chunk]
        nth = (jnp.broadcast_to(line, (samples, chunk)) - first_bag).astype(jnp.int16)
        for f in range(FEAT):
            place_ref[f * samples : (f + 1) * samples, start : start + chunk] = ones_where(
                nth == jnp.asarray(f, jnp.int16)
            )
    pooled = matmul(place_ref[:, :slots], near_ref[...])
    pooled = (pooled + matmul(place_ref[:, slots:], far_ref[...])).astype(jnp.bfloat16)
    for f, part in enumerate(features):
        wide_ref[:, part] = pooled[f * samples : (f + 1) * samples, :]
    hidden = matmul(wide_ref[...], down_ref[...]).astype(jnp.bfloat16)
    summed = jnp.zeros((samples, emb), jnp.float32)
    for part in features:
        shifted = rows_dot(hidden, up_ref[part, :]) + bias_ref[:, part]
        cross_ref[:, part] = shifted
        feats = wide_ref[:, part].astype(jnp.float32)
        summed = summed + (feats * shifted + feats) * weight_ref[:, part].astype(jnp.float32)
    logits = jnp.sum(summed, axis=1, keepdims=True)
    logits_ref[...] = as_line(logits)
    dlogit = LOSS_SCALE * (jax.nn.sigmoid(logits) - as_column(target_ref[...]))
    dcross = []
    for part in features:
        dmixed = dlogit * weight_ref[:, part].astype(jnp.float32)
        dcross.append((dmixed * wide_ref[:, part].astype(jnp.float32)).astype(jnp.bfloat16))
    dhidden = matmul(jnp.concatenate(dcross, axis=1), up_ref[...]).astype(jnp.bfloat16)
    for f, part in enumerate(features):
        dmixed = dlogit * weight_ref[:, part].astype(jnp.float32)
        back_term = rows_dot(dhidden, down_ref[part, :])
        grads = dmixed * (cross_ref[:, part] + 1.0) + back_term
        grads_ref[f * samples : (f + 1) * samples, :] = grads.astype(jnp.bfloat16)
    for f, part in enumerate(features):
        down_term = transposed_dot(wide_ref[:, part], dhidden).astype(jnp.bfloat16)
        up_term = transposed_dot(dcross[f], hidden).astype(jnp.bfloat16)
        spot = slice((f * emb) % half, (f * emb) % half + emb)
        keep = swapped if f * emb >= half else jnp.logical_not(swapped)

        @pl.when(keep)
        def _():
            kept_ref[spot, :rank] = down_term
            kept_ref[spot, rank:] = up_term

        @pl.when(jnp.logical_not(keep))
        def _():
            sent_ref[spot, :rank] = down_term
            sent_ref[spot, rank:] = up_term


def dense_step(swap, goals, near, far, downs, ups, bias, weight, target):
    samples = target.shape[0]
    slots, emb = near.shape
    width, rank = 2 * downs[0].shape[0], downs[0].shape[1]
    flops = 4 * slots * samples * width + 12 * samples * width * rank
    logits, grads, kept, sent = kernel_call(
        dense_kernel,
        (
            jax.ShapeDtypeStruct((1, samples), jnp.float32),
            jax.ShapeDtypeStruct((samples * FEAT, emb), jnp.bfloat16),
            jax.ShapeDtypeStruct((width // 2, 2 * rank), jnp.bfloat16),
            jax.ShapeDtypeStruct((width // 2, 2 * rank), jnp.bfloat16),
        ),
        (flops, 4 * near.size + 8 * width * rank),
        [
            pltpu.VMEM((samples * FEAT, 2 * slots), jnp.bfloat16),
            pltpu.VMEM((samples, width), jnp.bfloat16),
            pltpu.VMEM((samples, width), jnp.float32),
            pltpu.VMEM((width, rank), jnp.bfloat16),
            pltpu.VMEM((width, rank), jnp.bfloat16),
        ],
        flags=1,
        operands=10,
    )(
        swap,
        goals.reshape(1, 2 * slots),
        near,
        far,
        *downs,
        *ups,
        bias.reshape(1, width),
        weight.reshape(1, width),
        target.reshape(1, samples),
    )
    return logits.reshape(samples), grads, kept, sent


def return_kernel(goals_ref, grads_ref, out_ref, pick_ref):
    blocks = goals_ref.shape[0]
    bags = grads_ref.shape[0]
    samples = bags // FEAT
    high, low = split_ids(goals_ref[...])
    unit = ones_where(diagonal(SLOTS))
    columns = joined((rows_dot(unit, high), rows_dot(unit, low))).astype(jnp.int16)
    place = lax.broadcasted_iota(jnp.int32, (SLOTS, bags), 1)
    order = ((place % samples) * FEAT + place // samples).astype(jnp.int16)
    for block in range(blocks):
        pick_ref[block * SLOTS : (block + 1) * SLOTS, :] = ones_where(
            columns[:, block : block + 1] == order
        )
    out_ref[...] = matmul(pick_ref[...], grads_ref[...]).astype(jnp.bfloat16)


def return_grads(goals, grads):
    bags, emb = grads.shape
    slot_count = goals.size
    return kernel_call(
        return_kernel,
        jax.ShapeDtypeStruct((slot_count, emb), jnp.bfloat16),
        (2 * slot_count * bags * emb, 2 * grads.size + 2 * slot_count * emb),
        [pltpu.VMEM((slot_count, bags), jnp.bfloat16)],
        operands=2,
    )(goals.reshape(slot_count // SLOTS, SLOTS), grads)


def update_kernel(share_ref, rows_ref, mine_ref, other_ref, accum_ref, rows_out_ref, accum_out_ref):
    chunks = accum_ref.shape[0]
    per_share = accum_out_ref.shape[0]
    for chunk in range(chunks):
        part = slice(chunk * SLOTS, (chunk + 1) * SLOTS)
        row_grad = mine_ref[part, :].astype(jnp.float32) + other_ref[part, :].astype(jnp.float32)
        squares = jnp.mean(row_grad * row_grad, axis=1, keepdims=True)
        accum = as_column(accum_ref[chunk : chunk + 1, :]) + squares
        step = LEARN_RATE * row_grad * lax.rsqrt(accum + ADA_EPS)
        rows_out_ref[part, :] = (rows_ref[part, :].astype(jnp.float32) - step).astype(jnp.bfloat16)

        @pl.when(share_ref[0] == chunk // per_share)
        def _():
            accum_out_ref[chunk % per_share : chunk % per_share + 1, :] = as_line(accum)


def update_rows(share, rows, mine, other, accum, narrows):
    row_dev, emb = rows.shape
    chunks = row_dev // SLOTS
    new_rows, new_accum = kernel_call(
        update_kernel,
        (
            jax.ShapeDtypeStruct((row_dev, emb), jnp.bfloat16),
            jax.ShapeDtypeStruct((chunks // narrows, SLOTS), jnp.float32),
        ),
        (8 * rows.size, 8 * rows.size),
        flags=1,
        operands=4,
    )(share, rows, mine, other, accum.reshape(chunks, SLOTS))
    return new_rows, new_accum.reshape(row_dev // narrows)


def group_levels(size):
    levels = []
    stride = 1
    while size % 4 == 0:
        levels.append((stride, 4))
        stride, size = stride * 4, size // 4
    if size > 1:
        levels.append((stride, size))
    return levels


def partner_index(index, stride, group, step):
    place = (index // stride) % group
    if group & (group - 1) == 0:
        other = place ^ step
    else:
        other = (place + step) % group
    return index + (other - place) * stride


def sent_from(axis, stride, group, step):
    size = lax.axis_size(axis)
    return [(partner_index(i, stride, group, step), i) for i in range(size)]


def scatter_sum(blocks, axis, levels):
    index = lax.axis_index(axis)
    for stride, group in levels:
        rows = blocks.shape[0] // group
        place = (index // stride) % group
        total = lax.dynamic_slice_in_dim(blocks, place * rows, rows, 0).astype(jnp.float32)
        for step in range(1, group):
            pairs = sent_from(axis, stride, group, step)
            if group & (group - 1) == 0:
                goal = place ^ step
            else:
                goal = (place + group - step) % group
            outgoing = lax.dynamic_slice_in_dim(blocks, goal * rows, rows, 0)
            total = total + lax.ppermute(outgoing, axis, pairs).astype(jnp.float32)
        blocks = total.astype(jnp.bfloat16)
    return blocks


def gather_blocks(block, axis, levels):
    index = lax.axis_index(axis)
    for stride, group in reversed(levels):
        rows = block.shape[0]
        place = (index // stride) % group
        whole = jnp.zeros((group * rows,) + block.shape[1:], block.dtype)
        whole = lax.dynamic_update_slice_in_dim(whole, block, place * rows, 0)
        for step in range(1, group):
            origin = partner_index(index, stride, group, step)
            came = lax.ppermute(block, axis, sent_from(axis, stride, group, step))
            spot = (origin // stride) % group
            whole = lax.dynamic_update_slice_in_dim(whole, came, spot * rows, 0)
        block = whole
    return block


def local(
    table_rows, accum, factor_down, factor_up, cross_bias, out_weight, target, bag_rows, slot_target
):
    tables = lax.axis_size("table")
    narrows = lax.axis_size("narrow")
    row_dev, emb_width = table_rows.shape
    pools_per = slot_target.shape[1]
    samples = target.shape[0]
    bag_count = samples * FEAT
    slot_count = tables * pools_per
    narrow_levels = group_levels(narrows)
    table_levels = group_levels(tables)
    table_index = lax.axis_index("table")
    narrow_index = lax.axis_index("narrow")
    near_count = tables // 2
    far_half = table_index // near_count
    halves = [list(range(near_count)), list(range(near_count, tables))]
    across = [(i, (i + near_count) % tables) for i in range(tables)]
    paired = narrows == 2
    swap = (narrow_index if paired else narrow_index * 0).reshape(1)

    def near_first(rows):
        return jnp.where(far_half == 0, rows, jnp.roll(rows, near_count, axis=0))

    def both_halves(block):
        if paired:
            return block, lax.ppermute(block, "narrow", sent_from("narrow", 1, 2, 1))
        whole = gather_blocks(block, "narrow", narrow_levels)
        return tuple(jnp.split(whole, 2, axis=0))

    share_rows = row_dev // narrows
    own_share = lax.dynamic_slice_in_dim(table_rows, narrow_index * share_rows, share_rows, 0)
    far_rows = both_halves(lax.ppermute(own_share, "table", across))
    downs = both_halves(factor_down)
    ups = both_halves(factor_up)

    per_window = bag_rows.shape[1]
    asked = near_first(bag_rows)
    asked = jnp.concatenate([asked[:near_count], asked[near_count:]], axis=1)
    asked = lax.all_to_all(
        asked, "table", split_axis=0, concat_axis=0, tiled=True, axis_index_groups=halves
    )
    near_ids, far_ids = asked[:, :per_window], asked[:, per_window:]

    def pooled_for(part, plain_ids, flag, rows):
        if per_window == SLOTS * HOT:
            sums = pool_lookups(asked, part * per_window, flag, *rows)
        else:
            sums = pool_lookups(plain_ids.reshape(-1, SLOTS * HOT), 0, flag, *rows)
        return lax.all_to_all(
            sums.reshape(near_count, pools_per, emb_width),
            "table",
            split_axis=0,
            concat_axis=0,
            tiled=True,
            axis_index_groups=halves,
        ).reshape(slot_count // 2, emb_width)

    own_rows = tuple(jnp.split(table_rows, 2, axis=0))
    near = pooled_for(0, near_ids, swap * 0, own_rows)
    far = pooled_for(1, far_ids, swap, far_rows)
    other_ids = lax.ppermute(far_ids, "table", across)
    all_ids = near_first(jnp.concatenate([near_ids, other_ids], axis=0))
    counts = lookup_counts(all_ids.reshape(-1, SLOTS * HOT), row_dev)
    near, far, counts = lax.optimization_barrier((near, far, counts))
    logits, bag_grads, kept, sent = dense_step(
        swap, near_first(slot_target), near, far, downs, ups, cross_bias, out_weight, target
    )
    if paired:
        came = lax.ppermute(sent, "narrow", sent_from("narrow", 1, 2, 1))
        narrow_sum = (kept.astype(jnp.float32) + came.astype(jnp.float32)).astype(jnp.bfloat16)
    else:
        narrow_sum = scatter_sum(jnp.concatenate([kept, sent], axis=0), "narrow", narrow_levels)
    slot_grads = return_grads(slot_target, bag_grads)
    returned = lax.all_to_all(
        slot_grads.reshape(tables, pools_per, emb_width),
        "table",
        split_axis=0,
        concat_axis=0,
        tiled=True,
    ).reshape(slot_count, emb_width)
    table_sum = scatter_sum(narrow_sum, "table", table_levels)
    sent_grad = matmul(counts, returned).astype(jnp.bfloat16)
    table_sum, sent_grad = lax.optimization_barrier((table_sum, sent_grad))
    grand_total = gather_blocks(table_sum, "table", table_levels).astype(jnp.float32)
    batch_all = samples * tables * narrows
    grand_total = grand_total * (1.0 / math.sqrt(batch_all))
    rank_size = factor_down.shape[1]
    down_grad = grand_total[:, :rank_size]
    up_grad = grand_total[:, rank_size:]
    if paired:
        mine = sent_grad
        other = lax.ppermute(sent_grad, "narrow", sent_from("narrow", 1, 2, 1))
    else:
        share = scatter_sum(sent_grad, "narrow", narrow_levels)
        mine = gather_blocks(share, "narrow", narrow_levels)
        other = jnp.zeros_like(mine)
    new_rows, new_accum = update_rows(
        narrow_index.reshape(1), table_rows, mine, other, accum, narrows
    )
    return (logits, down_grad, up_grad, new_rows, new_accum)


def solution(mesh):
    in_specs = (
        P("table", None),
        P("table"),
        P("narrow", None),
        P("narrow", None),
        P(),
        P(),
        P(("table", "narrow")),
        P(("table", "narrow"), None),
        P(("table", "narrow"), None),
    )
    out_specs = (
        P(("table", "narrow")),
        P("narrow", None),
        P("narrow", None),
        P("table", None),
        P(("table", "narrow")),
    )
    return jax.shard_map(local, mesh=mesh, in_specs=in_specs, out_specs=out_specs, check_vma=False)
```

```python
import functools
import math

import jax
import jax.numpy as jnp
from jax import lax
from jax.experimental import pallas as pl
from jax.experimental.pallas import tpu as pltpu
from jax.sharding import PartitionSpec as P

FEAT = 8
HOT = 4


LEARN_RATE = 0.2
LOSS_SCALE = 32.0
ADA_EPS = 1e-06


SLOTS = 128
MIB = 1024 * 1024


def matmul(left, right):
    return jnp.dot(left, right, preferred_element_type=jnp.float32)


def transposed_dot(left, right):
    return lax.dot_general(
        left, right, (((0,), (0,)), ((), ())), preferred_element_type=jnp.float32
    )


def rows_dot(left, right):
    return lax.dot_general(
        left, right, (((1,), (1,)), ((), ())), preferred_element_type=jnp.float32
    )


def kernel_call(kernel, out_shape, cost, scratch=(), flags=0, operands=0, room=8):
    flops, moved = cost
    smem = pl.BlockSpec(memory_space=pltpu.SMEM)
    vmem = pl.BlockSpec(memory_space=pltpu.VMEM)
    return pl.pallas_call(
        kernel,
        in_specs=[smem] * flags + [vmem] * operands,
        out_specs=jax.tree.map(lambda _: vmem, out_shape),
        out_shape=out_shape,
        scratch_shapes=scratch,
        compiler_params=pltpu.CompilerParams(vmem_limit_bytes=room * MIB),
        cost_estimate=pl.CostEstimate(flops=flops, bytes_accessed=moved, transcendentals=0),
    )


def split_ids(ids):
    shifted = ids + 1
    high = lax.shift_right_logical(shifted, 5).astype(jnp.float32).astype(jnp.bfloat16)
    low = (shifted & 31).astype(jnp.float32).astype(jnp.bfloat16)
    return high, low


def lookup_choice():
    shape = (HOT * SLOTS, HOT * SLOTS)
    row = lax.broadcasted_iota(jnp.int32, shape, 0)
    column = lax.broadcasted_iota(jnp.int32, shape, 1)
    wanted = (row & (SLOTS - 1)) * HOT + lax.shift_right_logical(row, 7)
    return jnp.where(wanted == column, 1.0, 0.0).astype(jnp.bfloat16)


def joined(digits):
    high, low = digits
    return (high * 32.0 + low - 1.0).astype(jnp.int32)


def ones_where(mask):
    return jnp.where(mask, jnp.asarray(1, jnp.bfloat16), jnp.asarray(0, jnp.bfloat16))


def pool_kernel(offset, swap_ref, ids_ref, first_ref, second_ref, out_ref, counts_ref):
    blocks = ids_ref.shape[0]
    half = first_ref.shape[0]
    high, low = split_ids(ids_ref[:, offset : offset + HOT * SLOTS])
    choice = lookup_choice()
    columns = joined((rows_dot(choice, high), rows_dot(choice, low))).astype(jnp.int16)
    position = lax.broadcasted_iota(jnp.int32, (SLOTS, 2 * half), 1)
    shifted = position + swap_ref[0] * half
    position = jnp.where(shifted >= 2 * half, shifted - 2 * half, shifted).astype(jnp.int16)
    for block in range(blocks):
        counts = None
        for lookup in range(HOT):
            column = columns[lookup * SLOTS : (lookup + 1) * SLOTS, block : block + 1]
            found = ones_where(column == position)
            counts = found if counts is None else counts + found
        counts_ref[block * SLOTS : (block + 1) * SLOTS, :] = counts
    sums = matmul(counts_ref[:, :half], first_ref[...])
    sums = sums + matmul(counts_ref[:, half:], second_ref[...])
    out_ref[...] = sums.astype(jnp.bfloat16)


def pool_lookups(ids, offset, swap, first, second):
    blocks = ids.shape[0]
    half, width = first.shape
    slots = blocks * SLOTS
    return kernel_call(
        functools.partial(pool_kernel, offset),
        jax.ShapeDtypeStruct((slots, width), jnp.bfloat16),
        (4 * slots * half * width, 4 * half * width + 2 * slots * width),
        [pltpu.VMEM((slots, 2 * half), jnp.bfloat16)],
        flags=1,
        operands=3,
    )(swap, ids, first, second)


def counts_kernel(ids_ref, out_ref):
    blocks = ids_ref.shape[0]
    row_dev = out_ref.shape[0]
    tile = 64
    high, low = split_ids(ids_ref[...])
    choice = lookup_choice()
    lines = joined((rows_dot(high, choice), rows_dot(low, choice)))
    position = lax.broadcasted_iota(jnp.int32, (tile, SLOTS), 0).astype(jnp.int16)
    for block in range(blocks):
        spread = []
        for lookup in range(HOT):
            line = lines[block : block + 1, lookup * SLOTS : (lookup + 1) * SLOTS]
            spread.append(jnp.broadcast_to(line, (tile, SLOTS)).astype(jnp.int16))
        for start in range(0, row_dev, tile):
            counts = None
            for lookup in range(HOT):
                found = ones_where(spread[lookup] - jnp.asarray(start, jnp.int16) == position)
                counts = found if counts is None else counts + found
            out_ref[start : start + tile, block * SLOTS : (block + 1) * SLOTS] = counts


def lookup_counts(ids, row_dev):
    slot_count = ids.size // HOT
    return kernel_call(
        counts_kernel,
        jax.ShapeDtypeStruct((row_dev, slot_count), jnp.bfloat16),
        (8 * row_dev * slot_count, 2 * row_dev * slot_count),
        operands=1,
    )(ids)


def diagonal(size):
    row = lax.broadcasted_iota(jnp.int32, (size, size), 0)
    return row == lax.broadcasted_iota(jnp.int32, (size, size), 1)


def as_column(line):
    return jnp.sum(jnp.where(diagonal(line.shape[1]), line, 0.0), axis=1, keepdims=True)


def as_line(column):
    return jnp.sum(jnp.where(diagonal(column.shape[0]), column, 0.0), axis=0, keepdims=True)


def place_kernel(goals_ref, out_ref):
    samples = out_ref.shape[0] // FEAT
    chunk = 512
    first_bag = lax.broadcasted_iota(jnp.int32, (samples, chunk), 0) * FEAT
    for start in range(0, goals_ref.shape[1], chunk):
        line = goals_ref[:, start : start + chunk]
        nth = (jnp.broadcast_to(line, (samples, chunk)) - first_bag).astype(jnp.int16)
        for f in range(FEAT):
            out_ref[f * samples : (f + 1) * samples, start : start + chunk] = ones_where(
                nth == jnp.asarray(f, jnp.int16)
            )


def place_slots(goals, samples):
    slot_count = goals.size
    size = samples * FEAT * slot_count
    return kernel_call(
        place_kernel,
        jax.ShapeDtypeStruct((samples * FEAT, slot_count), jnp.bfloat16),
        (2 * size, 2 * size),
        operands=1,
    )(goals.reshape(1, slot_count))


def pick_kernel(goals_ref, out_ref):
    blocks = goals_ref.shape[0]
    bags = out_ref.shape[1]
    samples = bags // FEAT
    high, low = split_ids(goals_ref[...])
    unit = ones_where(diagonal(SLOTS))
    columns = joined((rows_dot(unit, high), rows_dot(unit, low))).astype(jnp.int16)
    place = lax.broadcasted_iota(jnp.int32, (SLOTS, bags), 1)
    order = ((place % samples) * FEAT + place // samples).astype(jnp.int16)
    for block in range(blocks):
        out_ref[block * SLOTS : (block + 1) * SLOTS, :] = ones_where(
            columns[:, block : block + 1] == order
        )


def pick_bags(goals, samples):
    slot_count = goals.size
    size = samples * FEAT * slot_count
    return kernel_call(
        pick_kernel,
        jax.ShapeDtypeStruct((slot_count, samples * FEAT), jnp.bfloat16),
        (2 * size, 2 * size),
        operands=1,
    )(goals.reshape(slot_count // SLOTS, SLOTS))


def product_kernel(left_ref, right_ref, out_ref):
    out_ref[...] = matmul(left_ref[...], right_ref[...]).astype(jnp.bfloat16)


def product(left, right):
    shape = (left.shape[0], right.shape[1])
    return kernel_call(
        product_kernel,
        jax.ShapeDtypeStruct(shape, jnp.bfloat16),
        (2 * left.size * right.shape[1], 2 * left.size + 2 * right.size),
        operands=2,
    )(left, right)


def dense_kernel(
    swap_ref,
    place_ref,
    near_ref,
    far_ref,
    down_a_ref,
    down_b_ref,
    up_a_ref,
    up_b_ref,
    bias_ref,
    weight_ref,
    target_ref,
    logits_ref,
    grads_ref,
    kept_ref,
    sent_ref,
    wide_ref,
    cross_ref,
    down_ref,
    up_ref,
):
    samples = target_ref.shape[1]
    width, rank = down_ref.shape
    emb = width // FEAT
    slots = near_ref.shape[0]
    half = width // 2
    swapped = swap_ref[0] == 1
    down_ref[:half, :] = jnp.where(swapped, down_b_ref[...], down_a_ref[...])
    down_ref[half:, :] = jnp.where(swapped, down_a_ref[...], down_b_ref[...])
    up_ref[:half, :] = jnp.where(swapped, up_b_ref[...], up_a_ref[...])
    up_ref[half:, :] = jnp.where(swapped, up_a_ref[...], up_b_ref[...])
    features = [slice(f * emb, (f + 1) * emb) for f in range(FEAT)]
    pooled = matmul(place_ref[:, :slots], near_ref[...])
    pooled = (pooled + matmul(place_ref[:, slots:], far_ref[...])).astype(jnp.bfloat16)
    for f, part in enumerate(features):
        wide_ref[:, part] = pooled[f * samples : (f + 1) * samples, :]
    hidden = matmul(wide_ref[...], down_ref[...]).astype(jnp.bfloat16)
    summed = jnp.zeros((samples, emb), jnp.float32)
    for part in features:
        shifted = rows_dot(hidden, up_ref[part, :]) + bias_ref[:, part]
        cross_ref[:, part] = shifted
        feats = wide_ref[:, part].astype(jnp.float32)
        summed = summed + (feats * shifted + feats) * weight_ref[:, part].astype(jnp.float32)
    logits = jnp.sum(summed, axis=1, keepdims=True)
    logits_ref[...] = as_line(logits)
    dlogit = LOSS_SCALE * (jax.nn.sigmoid(logits) - as_column(target_ref[...]))
    dcross = []
    for part in features:
        dmixed = dlogit * weight_ref[:, part].astype(jnp.float32)
        dcross.append((dmixed * wide_ref[:, part].astype(jnp.float32)).astype(jnp.bfloat16))
    dhidden = matmul(jnp.concatenate(dcross, axis=1), up_ref[...]).astype(jnp.bfloat16)
    for f, part in enumerate(features):
        dmixed = dlogit * weight_ref[:, part].astype(jnp.float32)
        back_term = rows_dot(dhidden, down_ref[part, :])
        grads = dmixed * (cross_ref[:, part] + 1.0) + back_term
        grads_ref[f * samples : (f + 1) * samples, :] = grads.astype(jnp.bfloat16)
    unit = ones_where(diagonal(emb))
    for f, part in enumerate(features):
        feats_t = rows_dot(unit, wide_ref[:, part]).astype(jnp.bfloat16)
        down_term = matmul(feats_t, dhidden).astype(jnp.bfloat16)
        cross_t = rows_dot(unit, dcross[f]).astype(jnp.bfloat16)
        up_term = matmul(cross_t, hidden).astype(jnp.bfloat16)
        spot = slice((f * emb) % half, (f * emb) % half + emb)
        keep = swapped if f * emb >= half else jnp.logical_not(swapped)

        @pl.when(keep)
        def _():
            kept_ref[spot, :rank] = down_term
            kept_ref[spot, rank:] = up_term

        @pl.when(jnp.logical_not(keep))
        def _():
            sent_ref[spot, :rank] = down_term
            sent_ref[spot, rank:] = up_term


def dense_step(swap, place, near, far, downs, ups, bias, weight, target):
    samples = target.shape[0]
    slots, emb = near.shape
    width, rank = 2 * downs[0].shape[0], downs[0].shape[1]
    flops = 4 * slots * samples * width + 12 * samples * width * rank
    logits, grads, kept, sent = kernel_call(
        dense_kernel,
        (
            jax.ShapeDtypeStruct((1, samples), jnp.float32),
            jax.ShapeDtypeStruct((samples * FEAT, emb), jnp.bfloat16),
            jax.ShapeDtypeStruct((width // 2, 2 * rank), jnp.bfloat16),
            jax.ShapeDtypeStruct((width // 2, 2 * rank), jnp.bfloat16),
        ),
        (flops, 4 * near.size + 8 * width * rank),
        [
            pltpu.VMEM((samples, width), jnp.bfloat16),
            pltpu.VMEM((samples, width), jnp.float32),
            pltpu.VMEM((width, rank), jnp.bfloat16),
            pltpu.VMEM((width, rank), jnp.bfloat16),
        ],
        flags=1,
        operands=10,
        room=16,
    )(
        swap,
        place,
        near,
        far,
        *downs,
        *ups,
        bias.reshape(1, width),
        weight.reshape(1, width),
        target.reshape(1, samples),
    )
    return logits.reshape(samples), grads, kept, sent


def update_kernel(share_ref, rows_ref, mine_ref, other_ref, accum_ref, rows_out_ref, accum_out_ref):
    chunks = accum_ref.shape[0]
    per_share = accum_out_ref.shape[0]
    for chunk in range(chunks):
        part = slice(chunk * SLOTS, (chunk + 1) * SLOTS)
        row_grad = mine_ref[part, :].astype(jnp.float32) + other_ref[part, :].astype(jnp.float32)
        squares = jnp.mean(row_grad * row_grad, axis=1, keepdims=True)
        accum = as_column(accum_ref[chunk : chunk + 1, :]) + squares
        step = LEARN_RATE * row_grad * lax.rsqrt(accum + ADA_EPS)
        rows_out_ref[part, :] = (rows_ref[part, :].astype(jnp.float32) - step).astype(jnp.bfloat16)

        @pl.when(share_ref[0] == chunk // per_share)
        def _():
            accum_out_ref[chunk % per_share : chunk % per_share + 1, :] = as_line(accum)


def update_rows(share, rows, mine, other, accum, narrows):
    row_dev, emb = rows.shape
    chunks = row_dev // SLOTS
    new_rows, new_accum = kernel_call(
        update_kernel,
        (
            jax.ShapeDtypeStruct((row_dev, emb), jnp.bfloat16),
            jax.ShapeDtypeStruct((chunks // narrows, SLOTS), jnp.float32),
        ),
        (8 * rows.size, 8 * rows.size),
        flags=1,
        operands=4,
    )(share, rows, mine, other, accum.reshape(chunks, SLOTS))
    return new_rows, new_accum.reshape(row_dev // narrows)


def group_levels(size):
    levels = []
    stride = 1
    while size % 4 == 0:
        levels.append((stride, 4))
        stride, size = stride * 4, size // 4
    if size > 1:
        levels.append((stride, size))
    return levels


def partner_index(index, stride, group, step):
    place = (index // stride) % group
    if group & (group - 1) == 0:
        other = place ^ step
    else:
        other = (place + step) % group
    return index + (other - place) * stride


def sent_from(axis, stride, group, step):
    size = lax.axis_size(axis)
    return [(partner_index(i, stride, group, step), i) for i in range(size)]


def scatter_sum(blocks, axis, levels):
    index = lax.axis_index(axis)
    for stride, group in levels:
        rows = blocks.shape[0] // group
        place = (index // stride) % group
        total = lax.dynamic_slice_in_dim(blocks, place * rows, rows, 0).astype(jnp.float32)
        for step in range(1, group):
            pairs = sent_from(axis, stride, group, step)
            if group & (group - 1) == 0:
                goal = place ^ step
            else:
                goal = (place + group - step) % group
            outgoing = lax.dynamic_slice_in_dim(blocks, goal * rows, rows, 0)
            total = total + lax.ppermute(outgoing, axis, pairs).astype(jnp.float32)
        blocks = total.astype(jnp.bfloat16)
    return blocks


def gathered_pieces(block, axis, level):
    stride, group = level
    index = lax.axis_index(axis)
    pieces = [((index // stride) % group, block)]
    for step in range(1, group):
        origin = partner_index(index, stride, group, step)
        came = lax.ppermute(block, axis, sent_from(axis, stride, group, step))
        pieces.append(((origin // stride) % group, came))
    return pieces


def gather_blocks(block, axis, levels):
    for level in reversed(levels):
        rows = block.shape[0]
        pieces = gathered_pieces(block, axis, level)
        block = jnp.zeros((len(pieces) * rows,) + block.shape[1:], block.dtype)
        for place, piece in pieces:
            block = lax.dynamic_update_slice_in_dim(block, piece, place * rows, 0)
    return block


def local(
    table_rows, accum, factor_down, factor_up, cross_bias, out_weight, target, bag_rows, slot_target
):
    tables = lax.axis_size("table")
    narrows = lax.axis_size("narrow")
    row_dev, emb_width = table_rows.shape
    pools_per = slot_target.shape[1]
    samples = target.shape[0]
    bag_count = samples * FEAT
    slot_count = tables * pools_per
    narrow_levels = group_levels(narrows)
    table_levels = group_levels(tables)
    table_index = lax.axis_index("table")
    narrow_index = lax.axis_index("narrow")
    near_count = tables // 2
    far_half = table_index // near_count
    halves = [list(range(near_count)), list(range(near_count, tables))]
    across = [(i, (i + near_count) % tables) for i in range(tables)]
    paired = narrows == 2
    swap = (narrow_index if paired else narrow_index * 0).reshape(1)

    def near_and_far(rows):
        return tuple(
            lax.dynamic_slice_in_dim(rows, half * near_count, near_count, 0)
            for half in (far_half, 1 - far_half)
        )

    def in_order(near, far):
        return jnp.where(
            far_half == 0, jnp.concatenate([near, far]), jnp.concatenate([far, near])
        )

    def both_halves(block):
        if paired:
            return block, lax.ppermute(block, "narrow", sent_from("narrow", 1, 2, 1))
        whole = gather_blocks(block, "narrow", narrow_levels)
        return tuple(jnp.split(whole, 2, axis=0))

    share_rows = row_dev // narrows
    own_share = lax.dynamic_slice_in_dim(table_rows, narrow_index * share_rows, share_rows, 0)
    far_share = lax.ppermute(own_share, "table", across)
    downs = both_halves(factor_down)
    ups = both_halves(factor_up)

    per_window = bag_rows.shape[1]
    asked = jnp.concatenate(near_and_far(bag_rows), axis=1)
    asked = lax.all_to_all(
        asked, "table", split_axis=0, concat_axis=0, tiled=True, axis_index_groups=halves
    )
    asked, far_share = lax.optimization_barrier((asked, far_share))
    far_rows = both_halves(far_share)
    near_ids, far_ids = asked[:, :per_window], asked[:, per_window:]

    def pooled_for(part, plain_ids, flag, rows):
        if per_window == SLOTS * HOT:
            sums = pool_lookups(asked, part * per_window, flag, *rows)
        else:
            sums = pool_lookups(plain_ids.reshape(-1, SLOTS * HOT), 0, flag, *rows)
        return lax.all_to_all(
            sums.reshape(near_count, pools_per, emb_width),
            "table",
            split_axis=0,
            concat_axis=0,
            tiled=True,
            axis_index_groups=halves,
        ).reshape(slot_count // 2, emb_width)

    own_rows = tuple(jnp.split(table_rows, 2, axis=0))
    near = pooled_for(0, near_ids, swap * 0, own_rows)
    far = pooled_for(1, far_ids, swap, far_rows)
    other_ids = lax.ppermute(far_ids, "table", across)
    all_ids = in_order(near_ids, other_ids)
    counts = lookup_counts(all_ids.reshape(-1, SLOTS * HOT), row_dev)
    place = place_slots(jnp.concatenate(near_and_far(slot_target)), samples)
    pick = pick_bags(slot_target, samples)
    near, far, counts, place, pick = lax.optimization_barrier((near, far, counts, place, pick))
    logits, bag_grads, kept, sent = dense_step(
        swap, place, near, far, downs, ups, cross_bias, out_weight, target
    )
    if paired:
        came = lax.ppermute(sent, "narrow", sent_from("narrow", 1, 2, 1))
        narrow_sum = (kept.astype(jnp.float32) + came.astype(jnp.float32)).astype(jnp.bfloat16)
    else:
        narrow_sum = scatter_sum(jnp.concatenate([kept, sent], axis=0), "narrow", narrow_levels)
    slot_grads = product(pick, bag_grads)
    slot_grads, narrow_sum = lax.optimization_barrier((slot_grads, narrow_sum))
    returned = lax.all_to_all(
        slot_grads.reshape(tables, pools_per, emb_width),
        "table",
        split_axis=0,
        concat_axis=0,
        tiled=True,
    ).reshape(slot_count, emb_width)
    table_sum = scatter_sum(narrow_sum, "table", table_levels)
    sent_grad = product(counts, returned)
    level_sum = gather_blocks(table_sum, "table", table_levels[1:])
    level_sum, sent_grad = lax.optimization_barrier((level_sum, sent_grad))
    if paired:
        mine = sent_grad
        other = lax.ppermute(sent_grad, "narrow", sent_from("narrow", 1, 2, 1))
    else:
        share = scatter_sum(sent_grad, "narrow", narrow_levels)
        mine = gather_blocks(share, "narrow", narrow_levels)
        other = jnp.zeros_like(mine)
    new_rows, new_accum = update_rows(
        narrow_index.reshape(1), table_rows, mine, other, accum, narrows
    )
    rank = factor_down.shape[1]
    scale = 1.0 / math.sqrt(samples * tables * narrows)
    down_grad = jnp.zeros(factor_down.shape, jnp.float32)
    up_grad = jnp.zeros(factor_up.shape, jnp.float32)
    pieces = gathered_pieces(level_sum, "table", table_levels[0])
    spot, last = pieces[-1]
    last, new_rows, new_accum = lax.optimization_barrier((last, new_rows, new_accum))
    for spot, piece in pieces[:-1] + [(spot, last)]:
        spot = spot * piece.shape[0]
        scaled = piece.astype(jnp.float32) * scale
        down_grad = lax.dynamic_update_slice_in_dim(down_grad, scaled[:, :rank], spot, 0)
        up_grad = lax.dynamic_update_slice_in_dim(up_grad, scaled[:, rank:], spot, 0)
    return (logits, down_grad, up_grad, new_rows, new_accum)


def solution(mesh):
    in_specs = (
        P("table", None),
        P("table"),
        P("narrow", None),
        P("narrow", None),
        P(),
        P(),
        P(("table", "narrow")),
        P(("table", "narrow"), None),
        P(("table", "narrow"), None),
    )
    out_specs = (
        P(("table", "narrow")),
        P("narrow", None),
        P("narrow", None),
        P("table", None),
        P(("table", "narrow")),
    )
    return jax.shard_map(local, mesh=mesh, in_specs=in_specs, out_specs=out_specs, check_vma=False)
```

```python
import functools
import math

import jax
import jax.numpy as jnp
from jax import lax
from jax.experimental import pallas as pl
from jax.experimental.pallas import tpu as pltpu
from jax.sharding import PartitionSpec as P

FEAT = 8
HOT = 4


LEARN_RATE = 0.2
LOSS_SCALE = 32.0
ADA_EPS = 1e-06


SLOTS = 128
MIB = 1024 * 1024
MOST = 56


def matmul(left, right):
    return jnp.dot(left, right, preferred_element_type=jnp.float32)


def transposed_dot(left, right):
    return lax.dot_general(
        left, right, (((0,), (0,)), ((), ())), preferred_element_type=jnp.float32
    )


def rows_dot(left, right):
    return lax.dot_general(
        left, right, (((1,), (1,)), ((), ())), preferred_element_type=jnp.float32
    )


def kernel_call(
    kernel, out_shape, cost, scratch=(), flags=0, operands=0, left=0, left_out=(), aliases=None, room=8
):
    flops, moved = cost
    smem = pl.BlockSpec(memory_space=pltpu.SMEM)
    vmem = pl.BlockSpec(memory_space=pltpu.VMEM)
    hbm = pl.BlockSpec(memory_space=pltpu.HBM)
    if isinstance(out_shape, tuple):
        out_specs = tuple(hbm if i in left_out else vmem for i in range(len(out_shape)))
    else:
        out_specs = hbm if left_out else vmem
    return pl.pallas_call(
        kernel,
        in_specs=[smem] * flags + [vmem] * operands + [hbm] * left,
        out_specs=out_specs,
        input_output_aliases=aliases or {},
        out_shape=out_shape,
        scratch_shapes=scratch,
        compiler_params=pltpu.CompilerParams(vmem_limit_bytes=room * MIB),
        cost_estimate=pl.CostEstimate(flops=flops, bytes_accessed=moved, transcendentals=0),
    )


def split_ids(ids):
    shifted = ids + 1
    high = lax.shift_right_logical(shifted, 5).astype(jnp.float32).astype(jnp.bfloat16)
    low = (shifted & 31).astype(jnp.float32).astype(jnp.bfloat16)
    return high, low


def lookup_choice():
    shape = (HOT * SLOTS, HOT * SLOTS)
    row = lax.broadcasted_iota(jnp.int32, shape, 0)
    column = lax.broadcasted_iota(jnp.int32, shape, 1)
    wanted = (row & (SLOTS - 1)) * HOT + lax.shift_right_logical(row, 7)
    return jnp.where(wanted == column, 1.0, 0.0).astype(jnp.bfloat16)


def joined(digits):
    high, low = digits
    return (high * 32.0 + low - 1.0).astype(jnp.int32)


def ones_where(mask):
    return jnp.where(mask, jnp.asarray(1, jnp.bfloat16), jnp.asarray(0, jnp.bfloat16))


def pool_kernel(
    swap_ref, ids_ref, first_ref, second_ref, rows_ref, out_ref, counts_ref, near_ref, far_ref, sem
):
    half = first_ref.shape[0]
    fetch = pltpu.make_async_copy(rows_ref, near_ref, sem)
    fetch.start()
    for i, given_ref in enumerate((first_ref, second_ref)):
        into_half = 1 - swap_ref[0] if i else swap_ref[0]
        far_ref[pl.ds(pl.multiple_of(into_half * half, half), half), :] = given_ref[...]
    blocks = ids_ref.shape[0]
    sources, _, pools, _ = out_ref.shape
    per_block = HOT * SLOTS
    choice = lookup_choice()
    for part in range(2):
        high, low = split_ids(ids_ref[:, part * per_block : (part + 1) * per_block])
        columns = joined((rows_dot(choice, high), rows_dot(choice, low))).astype(jnp.int16)
        position = lax.broadcasted_iota(jnp.int32, (SLOTS, 2 * half), 1).astype(jnp.int16)
        for block in range(blocks):
            counts = None
            for lookup in range(HOT):
                column = columns[lookup * SLOTS : (lookup + 1) * SLOTS, block : block + 1]
                found = ones_where(column == position)
                counts = found if counts is None else counts + found
            counts_ref[block * SLOTS : (block + 1) * SLOTS, :] = counts
        if part == 0:
            fetch.wait()
        sums = matmul(counts_ref[...], (far_ref if part else near_ref)[...])
        sums = sums.astype(jnp.bfloat16)
        for source in range(sources):
            out_ref[source, part] = sums[source * pools : (source + 1) * pools]


def pool_lookups(ids, swap, near_rows, far_rows, pools):
    slots = ids.shape[0] * SLOTS
    row_dev, width = near_rows.shape
    return kernel_call(
        pool_kernel,
        jax.ShapeDtypeStruct((slots // pools, 2, pools, width), jnp.bfloat16),
        (4 * slots * row_dev * width, 4 * row_dev * width + 4 * slots * width),
        [
            pltpu.VMEM((slots, row_dev), jnp.bfloat16),
            pltpu.VMEM((row_dev, width), jnp.bfloat16),
            pltpu.VMEM((row_dev, width), jnp.bfloat16),
            pltpu.SemaphoreType.DMA,
        ],
        flags=1,
        operands=3,
        left=1,
        room=MOST,
    )(swap, ids, *far_rows, near_rows)


def row_grad_kernel(ids_ref, given_ref, out_ref, counts_ref, grads_ref, sem):
    fetch = pltpu.make_async_copy(given_ref, grads_ref, sem)
    fetch.start()
    blocks = ids_ref.shape[0]
    row_dev = out_ref.shape[0]
    tile = 64
    high, low = split_ids(ids_ref[...])
    choice = lookup_choice()
    lines = joined((rows_dot(high, choice), rows_dot(low, choice)))
    position = lax.broadcasted_iota(jnp.int32, (tile, SLOTS), 0).astype(jnp.int16)
    for block in range(blocks):
        spread = []
        for lookup in range(HOT):
            line = lines[block : block + 1, lookup * SLOTS : (lookup + 1) * SLOTS]
            spread.append(jnp.broadcast_to(line, (tile, SLOTS)).astype(jnp.int16))
        for start in range(0, row_dev, tile):
            counts = None
            for lookup in range(HOT):
                found = ones_where(spread[lookup] - jnp.asarray(start, jnp.int16) == position)
                counts = found if counts is None else counts + found
            counts_ref[start : start + tile, block * SLOTS : (block + 1) * SLOTS] = counts
    fetch.wait()
    out_ref[...] = matmul(counts_ref[...], grads_ref[...]).astype(jnp.bfloat16)


def row_grads(ids, slot_grads, row_dev):
    slot_count, emb = slot_grads.shape
    return kernel_call(
        row_grad_kernel,
        jax.ShapeDtypeStruct((row_dev, emb), jnp.bfloat16),
        (2 * row_dev * slot_count * emb, 2 * slot_grads.size + 2 * row_dev * emb),
        [
            pltpu.VMEM((row_dev, slot_count), jnp.bfloat16),
            pltpu.VMEM((slot_count, emb), jnp.bfloat16),
            pltpu.SemaphoreType.DMA,
        ],
        operands=1,
        left=1,
        room=16,
    )(ids, slot_grads)


def diagonal(size):
    row = lax.broadcasted_iota(jnp.int32, (size, size), 0)
    return row == lax.broadcasted_iota(jnp.int32, (size, size), 1)


def as_column(line):
    return jnp.sum(jnp.where(diagonal(line.shape[1]), line, 0.0), axis=1, keepdims=True)


def as_line(column):
    return jnp.sum(jnp.where(diagonal(column.shape[0]), column, 0.0), axis=0, keepdims=True)


def return_kernel(goals_ref, grads_ref, out_ref, pick_ref):
    blocks = goals_ref.shape[0]
    bags = grads_ref.shape[0]
    samples = bags // FEAT
    high, low = split_ids(goals_ref[...])
    unit = ones_where(diagonal(SLOTS))
    columns = joined((rows_dot(unit, high), rows_dot(unit, low))).astype(jnp.int16)
    place = lax.broadcasted_iota(jnp.int32, (SLOTS, bags), 1)
    order = ((place % samples) * FEAT + place // samples).astype(jnp.int16)
    for block in range(blocks):
        pick_ref[block * SLOTS : (block + 1) * SLOTS, :] = ones_where(
            columns[:, block : block + 1] == order
        )
    out_ref[...] = matmul(pick_ref[...], grads_ref[...]).astype(jnp.bfloat16)


def return_grads(goals, grads):
    bags, emb = grads.shape
    slot_count = goals.size
    return kernel_call(
        return_kernel,
        jax.ShapeDtypeStruct((slot_count, emb), jnp.bfloat16),
        (2 * slot_count * bags * emb, 2 * grads.size + 2 * slot_count * emb),
        [pltpu.VMEM((slot_count, bags), jnp.bfloat16)],
        operands=2,
        room=12,
    )(goals.reshape(slot_count // SLOTS, SLOTS), grads)


def dense_kernel(
    swap_ref,
    goals_ref,
    bias_ref,
    weight_ref,
    target_ref,
    arrived_ref,
    down_a_ref,
    down_b_ref,
    up_a_ref,
    up_b_ref,
    logits_ref,
    grads_ref,
    kept_ref,
    sent_ref,
    place_ref,
    wide_ref,
    dcross_ref,
    shifted_ref,
    down_ref,
    up_ref,
    sems,
):
    samples = target_ref.shape[1]
    width, rank = down_ref.shape
    emb = width // FEAT
    half = width // 2
    fetches = []
    for source_ref, goal_ref, second in (
        (down_a_ref, down_ref, False),
        (down_b_ref, down_ref, True),
        (up_a_ref, up_ref, False),
        (up_b_ref, up_ref, True),
    ):
        into_half = 1 - swap_ref[0] if second else swap_ref[0]
        spot = pl.ds(pl.multiple_of(into_half * half, half), half)
        fetches.append(
            pltpu.make_async_copy(source_ref, goal_ref.at[spot, :], sems.at[len(fetches)])
        )
        fetches[-1].start()
    chunk = 512
    first_bag = lax.broadcasted_iota(jnp.int32, (samples, chunk), 0) * FEAT
    for start in range(0, goals_ref.shape[1], chunk):
        line = goals_ref[:, start : start + chunk]
        nth = (jnp.broadcast_to(line, (samples, chunk)) - first_bag).astype(jnp.int16)
        for f in range(FEAT):
            place_ref[f * samples : (f + 1) * samples, start : start + chunk] = ones_where(
                nth == jnp.asarray(f, jnp.int16)
            )
    features = [slice(f * emb, (f + 1) * emb) for f in range(FEAT)]
    for f, part in enumerate(features):
        spot = slice(f * samples, (f + 1) * samples)
        wide_ref[:, part] = matmul(place_ref[spot, :], arrived_ref[...]).astype(jnp.bfloat16)
    for fetch in fetches:
        fetch.wait()
    hidden = matmul(wide_ref[...], down_ref[...]).astype(jnp.bfloat16)
    summed = jnp.zeros((samples, emb), jnp.float32)
    for part in features:
        shifted = rows_dot(hidden, up_ref[part, :]) + bias_ref[:, part]
        shifted_ref[:, part] = shifted
        feats = wide_ref[:, part].astype(jnp.float32)
        summed = summed + (feats * shifted + feats) * weight_ref[:, part].astype(jnp.float32)
    logits = jnp.sum(summed, axis=1, keepdims=True)
    logits_ref[...] = as_line(logits)
    dlogit = LOSS_SCALE * (jax.nn.sigmoid(logits) - as_column(target_ref[...]))
    for part in features:
        dmixed = dlogit * weight_ref[:, part].astype(jnp.float32)
        feats = wide_ref[:, part].astype(jnp.float32)
        dcross_ref[:, part] = (dmixed * feats).astype(jnp.bfloat16)
    dhidden = matmul(dcross_ref[...], up_ref[...]).astype(jnp.bfloat16)
    for f, part in enumerate(features):
        dmixed = dlogit * weight_ref[:, part].astype(jnp.float32)
        back_term = rows_dot(dhidden, down_ref[part, :])
        grads = dmixed * (shifted_ref[:, part] + 1.0) + back_term
        grads_ref[f * samples : (f + 1) * samples, :] = grads.astype(jnp.bfloat16)
    for step in range(FEAT):
        into_half = swap_ref[0] if step * emb < half else 1 - swap_ref[0]
        spot = (step * emb) % half
        part = pl.ds(pl.multiple_of(into_half * half + spot, emb), emb)
        out_ref = kept_ref if step * emb < half else sent_ref
        down_term = transposed_dot(wide_ref[:, part], dhidden)
        up_term = transposed_dot(dcross_ref[:, part], hidden)
        out_ref[spot : spot + emb, :rank] = down_term.astype(jnp.bfloat16)
        out_ref[spot : spot + emb, rank:] = up_term.astype(jnp.bfloat16)


def dense_step(swap, goals, arrived, downs, ups, bias, weight, target):
    samples = target.shape[0]
    slots, emb = arrived.shape
    width, rank = 2 * downs[0].shape[0], downs[0].shape[1]
    flops = 2 * slots * samples * width + 12 * samples * width * rank
    logits, grads, kept, sent = kernel_call(
        dense_kernel,
        (
            jax.ShapeDtypeStruct((1, samples), jnp.float32),
            jax.ShapeDtypeStruct((samples * FEAT, emb), jnp.bfloat16),
            jax.ShapeDtypeStruct((width // 2, 2 * rank), jnp.bfloat16),
            jax.ShapeDtypeStruct((width // 2, 2 * rank), jnp.bfloat16),
        ),
        (flops, 2 * arrived.size + 8 * width * rank),
        [
            pltpu.VMEM((samples * FEAT, slots), jnp.bfloat16),
            pltpu.VMEM((samples, width), jnp.bfloat16),
            pltpu.VMEM((samples, width), jnp.bfloat16),
            pltpu.VMEM((samples, width), jnp.float32),
            pltpu.VMEM((width, rank), jnp.bfloat16),
            pltpu.VMEM((width, rank), jnp.bfloat16),
            pltpu.SemaphoreType.DMA((4,)),
        ],
        flags=1,
        operands=5,
        left=4,
        room=MOST,
    )(
        swap,
        goals.reshape(1, slots),
        bias.reshape(1, width),
        weight.reshape(1, width),
        target.reshape(1, samples),
        arrived,
        *downs,
        *ups,
    )
    return logits.reshape(samples), grads, kept, sent


def spread_kernel(count, scale, aliased, spots_ref, *refs):
    piece_refs = refs[:count]
    down_out_ref, up_out_ref, down_ref, up_ref, sems = refs[count + aliased :]
    rows = piece_refs[0].shape[0]
    rank = down_ref.shape[1]
    stores = []
    for i, piece_ref in enumerate(piece_refs):
        here = slice(i * rows, (i + 1) * rows)
        spot = pl.ds(pl.multiple_of(spots_ref[i] * rows, rows), rows)
        for half, (from_ref, to_ref) in enumerate(((down_ref, down_out_ref), (up_ref, up_out_ref))):
            part = slice(half * rank, (half + 1) * rank)
            from_ref[here, :] = piece_ref[:, part].astype(jnp.float32) * scale
            stores.append(
                pltpu.make_async_copy(from_ref.at[here, :], to_ref.at[spot, :], sems.at[len(stores)])
            )
            stores[-1].start()
    for store in stores:
        store.wait()


def spread_pieces(pieces, scale, rows, given=()):
    count = len(pieces)
    spots = jnp.stack([spot for spot, _ in pieces]).astype(jnp.int32)
    arrays = [piece for _, piece in pieces]
    step, both = arrays[0].shape
    rank = both // 2
    shape = jax.ShapeDtypeStruct((rows, rank), jnp.float32)
    block = pltpu.VMEM((count * step, rank), jnp.float32)
    return kernel_call(
        functools.partial(spread_kernel, count, scale, len(given)),
        (shape, shape),
        (count * step * both, 6 * count * step * both),
        [block, block, pltpu.SemaphoreType.DMA((2 * count,))],
        flags=1,
        operands=count,
        left=len(given),
        left_out=(0, 1),
        aliases={1 + count + i: i for i in range(len(given))},
    )(spots, *arrays, *given)


def update_kernel(share_ref, rows_ref, mine_ref, other_ref, accum_ref, rows_out_ref, accum_out_ref):
    chunks = accum_ref.shape[0]
    per_share = accum_out_ref.shape[0]
    for chunk in range(chunks):
        part = slice(chunk * SLOTS, (chunk + 1) * SLOTS)
        row_grad = mine_ref[part, :].astype(jnp.float32) + other_ref[part, :].astype(jnp.float32)
        squares = jnp.mean(row_grad * row_grad, axis=1, keepdims=True)
        accum = as_column(accum_ref[chunk : chunk + 1, :]) + squares
        step = LEARN_RATE * row_grad * lax.rsqrt(accum + ADA_EPS)
        rows_out_ref[part, :] = (rows_ref[part, :].astype(jnp.float32) - step).astype(jnp.bfloat16)

        @pl.when(share_ref[0] == chunk // per_share)
        def _():
            accum_out_ref[chunk % per_share : chunk % per_share + 1, :] = as_line(accum)


def update_rows(share, rows, mine, other, accum, narrows):
    row_dev, emb = rows.shape
    chunks = row_dev // SLOTS
    new_rows, new_accum = kernel_call(
        update_kernel,
        (
            jax.ShapeDtypeStruct((row_dev, emb), jnp.bfloat16),
            jax.ShapeDtypeStruct((chunks // narrows, SLOTS), jnp.float32),
        ),
        (8 * rows.size, 8 * rows.size),
        flags=1,
        operands=4,
    )(share, rows, mine, other, accum.reshape(chunks, SLOTS))
    return new_rows, new_accum.reshape(row_dev // narrows)


def group_levels(size):
    levels = []
    stride = 1
    while size % 4 == 0:
        levels.append((stride, 4))
        stride, size = stride * 4, size // 4
    if size > 1:
        levels.append((stride, size))
    return levels


def partner_index(index, stride, group, step):
    place = (index // stride) % group
    if group & (group - 1) == 0:
        other = place ^ step
    else:
        other = (place + step) % group
    return index + (other - place) * stride


def sent_from(axis, stride, group, step):
    size = lax.axis_size(axis)
    return [(partner_index(i, stride, group, step), i) for i in range(size)]


def scattered_pieces(blocks, axis, level):
    stride, group = level
    rows = blocks.shape[0] // group
    place = (lax.axis_index(axis) // stride) % group
    pieces = [lax.dynamic_slice_in_dim(blocks, place * rows, rows, 0)]
    for step in range(1, group):
        pairs = sent_from(axis, stride, group, step)
        if group & (group - 1) == 0:
            goal = place ^ step
        else:
            goal = (place + group - step) % group
        outgoing = lax.dynamic_slice_in_dim(blocks, goal * rows, rows, 0)
        pieces.append(lax.ppermute(outgoing, axis, pairs))
    return pieces


def summed(pieces):
    total = pieces[0].astype(jnp.float32)
    for piece in pieces[1:]:
        total = total + piece.astype(jnp.float32)
    return total.astype(jnp.bfloat16)


def scatter_sum(blocks, axis, levels):
    for level in levels:
        blocks = summed(scattered_pieces(blocks, axis, level))
    return blocks


def gathered_pieces(block, axis, level):
    stride, group = level
    index = lax.axis_index(axis)
    pieces = [((index // stride) % group, block)]
    for step in range(1, group):
        origin = partner_index(index, stride, group, step)
        came = lax.ppermute(block, axis, sent_from(axis, stride, group, step))
        pieces.append(((origin // stride) % group, came))
    return pieces


def gather_blocks(block, axis, levels):
    for level in reversed(levels):
        rows = block.shape[0]
        pieces = gathered_pieces(block, axis, level)
        block = jnp.zeros((len(pieces) * rows,) + block.shape[1:], block.dtype)
        for place, piece in pieces:
            block = lax.dynamic_update_slice_in_dim(block, piece, place * rows, 0)
    return block


def local(
    table_rows, accum, factor_down, factor_up, cross_bias, out_weight, target, bag_rows, slot_target
):
    tables = lax.axis_size("table")
    narrows = lax.axis_size("narrow")
    row_dev, emb_width = table_rows.shape
    pools_per = slot_target.shape[1]
    samples = target.shape[0]
    bag_count = samples * FEAT
    slot_count = tables * pools_per
    narrow_levels = group_levels(narrows)
    table_levels = group_levels(tables)
    table_index = lax.axis_index("table")
    narrow_index = lax.axis_index("narrow")
    near_count = tables // 2
    far_half = table_index // near_count
    halves = [list(range(near_count)), list(range(near_count, tables))]
    across = [(i, (i + near_count) % tables) for i in range(tables)]
    paired = narrows == 2
    swap = (narrow_index if paired else narrow_index * 0).reshape(1)

    def near_and_far(rows):
        return tuple(
            lax.dynamic_slice_in_dim(rows, half * near_count, near_count, 0)
            for half in (far_half, 1 - far_half)
        )

    def in_order(near, far):
        return jnp.where(
            far_half == 0, jnp.concatenate([near, far]), jnp.concatenate([far, near])
        )

    def both_halves(block):
        if paired:
            return block, lax.ppermute(block, "narrow", sent_from("narrow", 1, 2, 1))
        whole = gather_blocks(block, "narrow", narrow_levels)
        return tuple(jnp.split(whole, 2, axis=0))

    share_rows = row_dev // narrows
    own_share = lax.dynamic_slice_in_dim(table_rows, narrow_index * share_rows, share_rows, 0)
    far_share = lax.ppermute(own_share, "table", across)
    downs = both_halves(factor_down)
    ups = both_halves(factor_up)

    per_window = bag_rows.shape[1]
    asked = jnp.concatenate(near_and_far(bag_rows), axis=1)
    asked = lax.all_to_all(
        asked, "table", split_axis=0, concat_axis=0, tiled=True, axis_index_groups=halves
    )
    asked, far_share = lax.optimization_barrier((asked, far_share))
    far_rows = both_halves(far_share)
    near_ids, far_ids = asked[:, :per_window], asked[:, per_window:]

    if per_window != SLOTS * HOT:
        by_block = (ids.reshape(-1, SLOTS * HOT) for ids in (near_ids, far_ids))
        asked = jnp.concatenate(tuple(by_block), axis=1)
    sums = pool_lookups(asked, swap, table_rows, far_rows, pools_per)
    arrived = lax.all_to_all(
        sums, "table", split_axis=0, concat_axis=0, tiled=True, axis_index_groups=halves
    )
    other_ids = lax.ppermute(far_ids, "table", across)
    arrived, other_ids = lax.optimization_barrier((arrived, other_ids))
    logits, bag_grads, kept, sent = dense_step(
        swap,
        jnp.stack(near_and_far(slot_target), axis=1),
        arrived.reshape(slot_count, emb_width),
        downs,
        ups,
        cross_bias,
        out_weight,
        target,
    )
    if paired:
        came = lax.ppermute(sent, "narrow", sent_from("narrow", 1, 2, 1))
        narrow_sum = (kept.astype(jnp.float32) + came.astype(jnp.float32)).astype(jnp.bfloat16)
    else:
        narrow_sum = scatter_sum(jnp.concatenate([kept, sent], axis=0), "narrow", narrow_levels)
    bag_grads, narrow_sum = lax.optimization_barrier((bag_grads, narrow_sum))
    slot_grads = return_grads(slot_target, bag_grads)
    pieces = scattered_pieces(narrow_sum, "table", table_levels[0])
    slot_grads, *pieces = lax.optimization_barrier((slot_grads, *pieces))
    returned = lax.all_to_all(
        slot_grads.reshape(tables, pools_per, emb_width),
        "table",
        split_axis=0,
        concat_axis=0,
        tiled=True,
    ).reshape(slot_count, emb_width)
    table_sum = scatter_sum(summed(pieces), "table", table_levels[1:])
    level_sum = gather_blocks(table_sum, "table", table_levels[1:])
    pieces = gathered_pieces(level_sum, "table", table_levels[0])
    all_ids = in_order(near_ids, other_ids).reshape(-1, SLOTS * HOT)
    sent_grad = row_grads(all_ids, returned, row_dev)
    spot, first = pieces[1]
    first, sent_grad = lax.optimization_barrier((first, sent_grad))
    pieces[1] = (spot, first)
    if paired:
        mine = sent_grad
        other = lax.ppermute(sent_grad, "narrow", sent_from("narrow", 1, 2, 1))
    else:
        share = scatter_sum(sent_grad, "narrow", narrow_levels)
        mine = gather_blocks(share, "narrow", narrow_levels)
        other = jnp.zeros_like(mine)
    new_rows, new_accum = update_rows(
        narrow_index.reshape(1), table_rows, mine, other, accum, narrows
    )
    scale = 1.0 / math.sqrt(samples * tables * narrows)
    spot, last = pieces[-1]
    grads = spread_pieces(pieces[:-1], scale, factor_down.shape[0])
    last, new_rows, new_accum, *grads = lax.optimization_barrier(
        (last, new_rows, new_accum, *grads)
    )
    down_grad, up_grad = spread_pieces([(spot, last)], scale, factor_down.shape[0], grads)
    return (logits, down_grad, up_grad, new_rows, new_accum)


def solution(mesh):
    in_specs = (
        P("table", None),
        P("table"),
        P("narrow", None),
        P("narrow", None),
        P(),
        P(),
        P(("table", "narrow")),
        P(("table", "narrow"), None),
        P(("table", "narrow"), None),
    )
    out_specs = (
        P(("table", "narrow")),
        P("narrow", None),
        P("narrow", None),
        P("table", None),
        P(("table", "narrow")),
    )
    return jax.shard_map(local, mesh=mesh, in_specs=in_specs, out_specs=out_specs, check_vma=False)
```

```python
import functools
import math

import jax
import jax.numpy as jnp
from jax import lax
from jax.experimental import pallas as pl
from jax.experimental.pallas import tpu as pltpu
from jax.sharding import PartitionSpec as P

FEAT = 8
HOT = 4


LEARN_RATE = 0.2
LOSS_SCALE = 32.0
ADA_EPS = 1e-06


SLOTS = 128
MIB = 1024 * 1024


def matmul(left, right):
    return jnp.dot(left, right, preferred_element_type=jnp.float32)


def transposed_dot(left, right):
    return lax.dot_general(
        left, right, (((0,), (0,)), ((), ())), preferred_element_type=jnp.float32
    )


def rows_dot(left, right):
    return lax.dot_general(
        left, right, (((1,), (1,)), ((), ())), preferred_element_type=jnp.float32
    )


def kernel_call(
    kernel, out_shape, cost, scratch=(), flags=0, operands=0, left=0, left_out=(), aliases=None, room=8
):
    flops, moved = cost
    smem = pl.BlockSpec(memory_space=pltpu.SMEM)
    vmem = pl.BlockSpec(memory_space=pltpu.VMEM)
    hbm = pl.BlockSpec(memory_space=pltpu.HBM)
    if isinstance(out_shape, tuple):
        out_specs = tuple(hbm if i in left_out else vmem for i in range(len(out_shape)))
    else:
        out_specs = hbm if left_out else vmem
    return pl.pallas_call(
        kernel,
        in_specs=[smem] * flags + [vmem] * operands + [hbm] * left,
        out_specs=out_specs,
        input_output_aliases=aliases or {},
        out_shape=out_shape,
        scratch_shapes=scratch,
        compiler_params=pltpu.CompilerParams(vmem_limit_bytes=room * MIB),
        cost_estimate=pl.CostEstimate(flops=flops, bytes_accessed=moved, transcendentals=0),
    )


def split_ids(ids):
    shifted = ids + 1
    high = lax.shift_right_logical(shifted, 5).astype(jnp.float32).astype(jnp.bfloat16)
    low = (shifted & 31).astype(jnp.float32).astype(jnp.bfloat16)
    return high, low


def lookup_choice():
    shape = (HOT * SLOTS, HOT * SLOTS)
    row = lax.broadcasted_iota(jnp.int32, shape, 0)
    column = lax.broadcasted_iota(jnp.int32, shape, 1)
    wanted = (row & (SLOTS - 1)) * HOT + lax.shift_right_logical(row, 7)
    return jnp.where(wanted == column, 1.0, 0.0).astype(jnp.bfloat16)


def joined(digits):
    high, low = digits
    return (high * 32.0 + low - 1.0).astype(jnp.int32)


def ones_where(mask):
    return jnp.where(mask, jnp.asarray(1, jnp.bfloat16), jnp.asarray(0, jnp.bfloat16))


def pool_kernel(part, ids_ref, rows_ref, *refs):
    out_ref, counts_ref, sums_ref, sem = refs[-4:]
    slots = counts_ref.shape[0]
    sources, _, pools, _ = out_ref.shape
    per_block = HOT * SLOTS
    if len(ids_ref.shape) == 3:
        ids = ids_ref[:, 0, part * per_block : (part + 1) * per_block]
    else:
        ids = ids_ref[:, part * per_block : (part + 1) * per_block]
    choice = lookup_choice()
    high, low = split_ids(ids)
    columns = joined((rows_dot(choice, high), rows_dot(choice, low))).astype(jnp.int16)
    position = lax.broadcasted_iota(jnp.int32, (SLOTS, rows_ref.shape[0]), 1).astype(jnp.int16)
    for block in range(slots // SLOTS):
        counts = None
        for lookup in range(HOT):
            column = columns[lookup * SLOTS : (lookup + 1) * SLOTS, block : block + 1]
            found = ones_where(column == position)
            counts = found if counts is None else counts + found
        counts_ref[block * SLOTS : (block + 1) * SLOTS, :] = counts
    sums = matmul(counts_ref[...], rows_ref[...]).astype(jnp.bfloat16)
    for source in range(sources):
        sums_ref[source] = sums[source * pools : (source + 1) * pools]
    store = pltpu.make_async_copy(sums_ref, out_ref.at[:, part], sem)
    store.start()
    store.wait()


def pool_lookups(part, ids, rows, pools, given=()):
    slots = ids.shape[0] * SLOTS
    row_dev, width = rows.shape
    return kernel_call(
        functools.partial(pool_kernel, part),
        jax.ShapeDtypeStruct((slots // pools, 2, pools, width), jnp.bfloat16),
        (2 * slots * row_dev * width, 2 * row_dev * width + 2 * slots * width),
        [
            pltpu.VMEM((slots, row_dev), jnp.bfloat16),
            pltpu.VMEM((slots // pools, pools, width), jnp.bfloat16),
            pltpu.SemaphoreType.DMA,
        ],
        operands=2,
        left=len(given),
        left_out=(0,),
        aliases={2: 0} if given else None,
        room=12,
    )(ids, rows, *given)


def row_grad_kernel(ids_ref, given_ref, out_ref, counts_ref, grads_ref, sem):
    fetch = pltpu.make_async_copy(given_ref, grads_ref, sem)
    fetch.start()
    blocks = ids_ref.shape[0]
    row_dev = out_ref.shape[0]
    tile = 64
    high, low = split_ids(ids_ref[...])
    choice = lookup_choice()
    lines = joined((rows_dot(high, choice), rows_dot(low, choice)))
    position = lax.broadcasted_iota(jnp.int32, (tile, SLOTS), 0).astype(jnp.int16)
    for block in range(blocks):
        spread = []
        for lookup in range(HOT):
            line = lines[block : block + 1, lookup * SLOTS : (lookup + 1) * SLOTS]
            spread.append(jnp.broadcast_to(line, (tile, SLOTS)).astype(jnp.int16))
        for start in range(0, row_dev, tile):
            counts = None
            for lookup in range(HOT):
                found = ones_where(spread[lookup] - jnp.asarray(start, jnp.int16) == position)
                counts = found if counts is None else counts + found
            counts_ref[start : start + tile, block * SLOTS : (block + 1) * SLOTS] = counts
    fetch.wait()
    out_ref[...] = matmul(counts_ref[...], grads_ref[...]).astype(jnp.bfloat16)


def row_grads(ids, slot_grads, row_dev):
    slot_count, emb = slot_grads.shape
    return kernel_call(
        row_grad_kernel,
        jax.ShapeDtypeStruct((row_dev, emb), jnp.bfloat16),
        (2 * row_dev * slot_count * emb, 2 * slot_grads.size + 2 * row_dev * emb),
        [
            pltpu.VMEM((row_dev, slot_count), jnp.bfloat16),
            pltpu.VMEM((slot_count, emb), jnp.bfloat16),
            pltpu.SemaphoreType.DMA,
        ],
        operands=1,
        left=1,
        room=16,
    )(ids, slot_grads)


def diagonal(size):
    row = lax.broadcasted_iota(jnp.int32, (size, size), 0)
    return row == lax.broadcasted_iota(jnp.int32, (size, size), 1)


def as_column(line):
    return jnp.sum(jnp.where(diagonal(line.shape[1]), line, 0.0), axis=1, keepdims=True)


def as_line(column):
    return jnp.sum(jnp.where(diagonal(column.shape[0]), column, 0.0), axis=0, keepdims=True)


def return_kernel(goals_ref, grads_ref, out_ref, pick_ref):
    blocks = goals_ref.shape[0]
    bags = grads_ref.shape[0]
    samples = bags // FEAT
    high, low = split_ids(goals_ref[...])
    unit = ones_where(diagonal(SLOTS))
    columns = joined((rows_dot(unit, high), rows_dot(unit, low))).astype(jnp.int16)
    place = lax.broadcasted_iota(jnp.int32, (SLOTS, bags), 1)
    order = ((place % samples) * FEAT + place // samples).astype(jnp.int16)
    for block in range(blocks):
        pick_ref[block * SLOTS : (block + 1) * SLOTS, :] = ones_where(
            columns[:, block : block + 1] == order
        )
    out_ref[...] = matmul(pick_ref[...], grads_ref[...]).astype(jnp.bfloat16)


def return_grads(goals, grads):
    bags, emb = grads.shape
    slot_count = goals.size
    return kernel_call(
        return_kernel,
        jax.ShapeDtypeStruct((slot_count, emb), jnp.bfloat16),
        (2 * slot_count * bags * emb, 2 * grads.size + 2 * slot_count * emb),
        [pltpu.VMEM((slot_count, bags), jnp.bfloat16)],
        operands=2,
        room=12,
    )(goals.reshape(slot_count // SLOTS, SLOTS), grads)


def dense_kernel(
    swap_ref,
    goals_ref,
    bias_ref,
    weight_ref,
    target_ref,
    arrived_ref,
    down_ref,
    up_ref,
    logits_ref,
    grads_ref,
    kept_ref,
    sent_ref,
    place_ref,
    wide_ref,
    dcross_ref,
    shifted_ref,
):
    samples = target_ref.shape[1]
    width, rank = down_ref.shape
    emb = width // FEAT
    half = width // 2
    chunk = 512
    first_bag = lax.broadcasted_iota(jnp.int32, (samples, chunk), 0) * FEAT
    for start in range(0, goals_ref.shape[1], chunk):
        line = goals_ref[:, start : start + chunk]
        nth = (jnp.broadcast_to(line, (samples, chunk)) - first_bag).astype(jnp.int16)
        for f in range(FEAT):
            place_ref[f * samples : (f + 1) * samples, start : start + chunk] = ones_where(
                nth == jnp.asarray(f, jnp.int16)
            )
    features = [slice(f * emb, (f + 1) * emb) for f in range(FEAT)]
    for f, part in enumerate(features):
        spot = slice(f * samples, (f + 1) * samples)
        wide_ref[:, part] = matmul(place_ref[spot, :], arrived_ref[...]).astype(jnp.bfloat16)
    hidden = matmul(wide_ref[...], down_ref[...]).astype(jnp.bfloat16)
    summed = jnp.zeros((samples, emb), jnp.float32)
    for part in features:
        shifted = rows_dot(hidden, up_ref[part, :]) + bias_ref[:, part]
        shifted_ref[:, part] = shifted
        feats = wide_ref[:, part].astype(jnp.float32)
        summed = summed + (feats * shifted + feats) * weight_ref[:, part].astype(jnp.float32)
    logits = jnp.sum(summed, axis=1, keepdims=True)
    logits_ref[...] = as_line(logits)
    dlogit = LOSS_SCALE * (jax.nn.sigmoid(logits) - as_column(target_ref[...]))
    for part in features:
        dmixed = dlogit * weight_ref[:, part].astype(jnp.float32)
        feats = wide_ref[:, part].astype(jnp.float32)
        dcross_ref[:, part] = (dmixed * feats).astype(jnp.bfloat16)
    dhidden = matmul(dcross_ref[...], up_ref[...]).astype(jnp.bfloat16)
    for f, part in enumerate(features):
        dmixed = dlogit * weight_ref[:, part].astype(jnp.float32)
        back_term = rows_dot(dhidden, down_ref[part, :])
        grads = dmixed * (shifted_ref[:, part] + 1.0) + back_term
        grads_ref[f * samples : (f + 1) * samples, :] = grads.astype(jnp.bfloat16)
    for step in range(FEAT):
        into_half = swap_ref[0] if step * emb < half else 1 - swap_ref[0]
        spot = (step * emb) % half
        part = pl.ds(pl.multiple_of(into_half * half + spot, emb), emb)
        out_ref = kept_ref if step * emb < half else sent_ref
        down_term = transposed_dot(wide_ref[:, part], dhidden)
        up_term = transposed_dot(dcross_ref[:, part], hidden)
        out_ref[spot : spot + emb, :rank] = down_term.astype(jnp.bfloat16)
        out_ref[spot : spot + emb, rank:] = up_term.astype(jnp.bfloat16)


def dense_step(swap, goals, arrived, down_full, up_full, bias, weight, target):
    samples = target.shape[0]
    slots, emb = arrived.shape
    width, rank = down_full.shape
    flops = 2 * slots * samples * width + 12 * samples * width * rank
    logits, grads, kept, sent = kernel_call(
        dense_kernel,
        (
            jax.ShapeDtypeStruct((1, samples), jnp.float32),
            jax.ShapeDtypeStruct((samples * FEAT, emb), jnp.bfloat16),
            jax.ShapeDtypeStruct((width // 2, 2 * rank), jnp.bfloat16),
            jax.ShapeDtypeStruct((width // 2, 2 * rank), jnp.bfloat16),
        ),
        (flops, 2 * arrived.size + 8 * width * rank),
        [
            pltpu.VMEM((samples * FEAT, slots), jnp.bfloat16),
            pltpu.VMEM((samples, width), jnp.bfloat16),
            pltpu.VMEM((samples, width), jnp.bfloat16),
            pltpu.VMEM((samples, width), jnp.float32),
        ],
        flags=1,
        operands=7,
        room=20,
    )(
        swap,
        goals.reshape(1, slots),
        bias.reshape(1, width),
        weight.reshape(1, width),
        target.reshape(1, samples),
        arrived,
        down_full,
        up_full,
    )
    return logits.reshape(samples), grads, kept, sent


def spread_kernel(count, scale, aliased, spots_ref, *refs):
    piece_refs = refs[:count]
    down_out_ref, up_out_ref, down_ref, up_ref, sems = refs[count + aliased :]
    rows = piece_refs[0].shape[0]
    rank = down_ref.shape[1]
    stores = []
    for i, piece_ref in enumerate(piece_refs):
        here = slice(i * rows, (i + 1) * rows)
        spot = pl.ds(pl.multiple_of(spots_ref[i] * rows, rows), rows)
        for half, (from_ref, to_ref) in enumerate(((down_ref, down_out_ref), (up_ref, up_out_ref))):
            part = slice(half * rank, (half + 1) * rank)
            from_ref[here, :] = piece_ref[:, part].astype(jnp.float32) * scale
            stores.append(
                pltpu.make_async_copy(from_ref.at[here, :], to_ref.at[spot, :], sems.at[len(stores)])
            )
            stores[-1].start()
    for store in stores:
        store.wait()


def spread_pieces(pieces, scale, rows, given=()):
    count = len(pieces)
    spots = jnp.stack([spot for spot, _ in pieces]).astype(jnp.int32)
    arrays = [piece for _, piece in pieces]
    step, both = arrays[0].shape
    rank = both // 2
    shape = jax.ShapeDtypeStruct((rows, rank), jnp.float32)
    block = pltpu.VMEM((count * step, rank), jnp.float32)
    return kernel_call(
        functools.partial(spread_kernel, count, scale, len(given)),
        (shape, shape),
        (count * step * both, 6 * count * step * both),
        [block, block, pltpu.SemaphoreType.DMA((2 * count,))],
        flags=1,
        operands=count,
        left=len(given),
        left_out=(0, 1),
        aliases={1 + count + i: i for i in range(len(given))},
    )(spots, *arrays, *given)


def update_kernel(share_ref, rows_ref, mine_ref, other_ref, accum_ref, rows_out_ref, accum_out_ref):
    chunks = accum_ref.shape[0]
    per_share = accum_out_ref.shape[0]
    for chunk in range(chunks):
        part = slice(chunk * SLOTS, (chunk + 1) * SLOTS)
        row_grad = mine_ref[part, :].astype(jnp.float32) + other_ref[part, :].astype(jnp.float32)
        squares = jnp.mean(row_grad * row_grad, axis=1, keepdims=True)
        accum = as_column(accum_ref[chunk : chunk + 1, :]) + squares
        step = LEARN_RATE * row_grad * lax.rsqrt(accum + ADA_EPS)
        rows_out_ref[part, :] = (rows_ref[part, :].astype(jnp.float32) - step).astype(jnp.bfloat16)

        @pl.when(share_ref[0] == chunk // per_share)
        def _():
            accum_out_ref[chunk % per_share : chunk % per_share + 1, :] = as_line(accum)


def update_rows(share, rows, mine, other, accum, narrows):
    row_dev, emb = rows.shape
    chunks = row_dev // SLOTS
    new_rows, new_accum = kernel_call(
        update_kernel,
        (
            jax.ShapeDtypeStruct((row_dev, emb), jnp.bfloat16),
            jax.ShapeDtypeStruct((chunks // narrows, SLOTS), jnp.float32),
        ),
        (8 * rows.size, 8 * rows.size),
        flags=1,
        operands=4,
    )(share, rows, mine, other, accum.reshape(chunks, SLOTS))
    return new_rows, new_accum.reshape(row_dev // narrows)


def group_levels(size):
    levels = []
    stride = 1
    while size % 4 == 0:
        levels.append((stride, 4))
        stride, size = stride * 4, size // 4
    if size > 1:
        levels.append((stride, size))
    return levels


def partner_index(index, stride, group, step):
    place = (index // stride) % group
    if group & (group - 1) == 0:
        other = place ^ step
    else:
        other = (place + step) % group
    return index + (other - place) * stride


def sent_from(axis, stride, group, step):
    size = lax.axis_size(axis)
    return [(partner_index(i, stride, group, step), i) for i in range(size)]


def scattered_pieces(blocks, axis, level):
    stride, group = level
    rows = blocks.shape[0] // group
    place = (lax.axis_index(axis) // stride) % group
    pieces = [lax.dynamic_slice_in_dim(blocks, place * rows, rows, 0)]
    for step in range(1, group):
        pairs = sent_from(axis, stride, group, step)
        if group & (group - 1) == 0:
            goal = place ^ step
        else:
            goal = (place + group - step) % group
        outgoing = lax.dynamic_slice_in_dim(blocks, goal * rows, rows, 0)
        pieces.append(lax.ppermute(outgoing, axis, pairs))
    return pieces


def summed(pieces):
    total = pieces[0].astype(jnp.float32)
    for piece in pieces[1:]:
        total = total + piece.astype(jnp.float32)
    return total.astype(jnp.bfloat16)


def scatter_sum(blocks, axis, levels):
    for level in levels:
        blocks = summed(scattered_pieces(blocks, axis, level))
    return blocks


def gathered_pieces(block, axis, level):
    stride, group = level
    index = lax.axis_index(axis)
    pieces = [((index // stride) % group, block)]
    for step in range(1, group):
        origin = partner_index(index, stride, group, step)
        came = lax.ppermute(block, axis, sent_from(axis, stride, group, step))
        pieces.append(((origin // stride) % group, came))
    return pieces


def gather_blocks(block, axis, levels):
    for level in reversed(levels):
        rows = block.shape[0]
        pieces = gathered_pieces(block, axis, level)
        block = jnp.zeros((len(pieces) * rows,) + block.shape[1:], block.dtype)
        for place, piece in pieces:
            block = lax.dynamic_update_slice_in_dim(block, piece, place * rows, 0)
    return block


def local(
    table_rows, accum, factor_down, factor_up, cross_bias, out_weight, target, bag_rows, slot_target
):
    tables = lax.axis_size("table")
    narrows = lax.axis_size("narrow")
    row_dev, emb_width = table_rows.shape
    pools_per = slot_target.shape[1]
    samples = target.shape[0]
    bag_count = samples * FEAT
    slot_count = tables * pools_per
    narrow_levels = group_levels(narrows)
    table_levels = group_levels(tables)
    table_index = lax.axis_index("table")
    narrow_index = lax.axis_index("narrow")
    near_count = tables // 2
    far_half = table_index // near_count
    halves = [list(range(near_count)), list(range(near_count, tables))]
    across = [(i, (i + near_count) % tables) for i in range(tables)]
    paired = narrows == 2
    swap = (narrow_index if paired else narrow_index * 0).reshape(1)

    def near_and_far(rows):
        return tuple(
            lax.dynamic_slice_in_dim(rows, half * near_count, near_count, 0)
            for half in (far_half, 1 - far_half)
        )

    def in_order(near, far):
        return jnp.where(
            far_half == 0, jnp.concatenate([near, far]), jnp.concatenate([far, near])
        )

    def narrow_whole(block):
        if not paired:
            return gather_blocks(block, "narrow", narrow_levels)
        came = lax.ppermute(block, "narrow", sent_from("narrow", 1, 2, 1))
        first = jnp.where(narrow_index == 0, block, came)
        second = jnp.where(narrow_index == 0, came, block)
        return jnp.concatenate([first, second], axis=0)

    share_rows = row_dev // narrows
    own_share = lax.dynamic_slice_in_dim(table_rows, narrow_index * share_rows, share_rows, 0)
    far_share = lax.ppermute(own_share, "table", across)
    down_full = narrow_whole(factor_down)
    up_full = narrow_whole(factor_up)

    per_window = bag_rows.shape[1]
    asked = jnp.concatenate(near_and_far(bag_rows), axis=1)[:, None, :]
    asked = lax.all_to_all(
        asked, "table", split_axis=0, concat_axis=0, tiled=True, axis_index_groups=halves
    )
    near_ids, far_ids = asked[:, 0, :per_window], asked[:, 0, per_window:]
    if per_window != SLOTS * HOT:
        by_block = (ids.reshape(-1, SLOTS * HOT) for ids in (near_ids, far_ids))
        asked = jnp.concatenate(tuple(by_block), axis=1)
    sums = pool_lookups(0, asked, table_rows, pools_per)
    sums, far_share = lax.optimization_barrier((sums, far_share))
    sums = pool_lookups(1, asked, narrow_whole(far_share), pools_per, (sums,))
    arrived = lax.all_to_all(
        sums, "table", split_axis=0, concat_axis=0, tiled=True, axis_index_groups=halves
    )
    other_ids = lax.ppermute(far_ids, "table", across)
    goals = jnp.stack(near_and_far(slot_target), axis=1)
    arrived, other_ids, down_full, up_full, goals = lax.optimization_barrier(
        (arrived, other_ids, down_full, up_full, goals)
    )
    logits, bag_grads, kept, sent = dense_step(
        swap,
        goals,
        arrived.reshape(slot_count, emb_width),
        down_full,
        up_full,
        cross_bias,
        out_weight,
        target,
    )
    if paired:
        came = lax.ppermute(sent, "narrow", sent_from("narrow", 1, 2, 1))
        narrow_sum = (kept.astype(jnp.float32) + came.astype(jnp.float32)).astype(jnp.bfloat16)
    else:
        narrow_sum = scatter_sum(jnp.concatenate([kept, sent], axis=0), "narrow", narrow_levels)
    slot_grads = return_grads(slot_target, bag_grads)
    slot_grads, narrow_sum = lax.optimization_barrier((slot_grads, narrow_sum))
    returned = lax.all_to_all(
        slot_grads.reshape(tables, pools_per, emb_width),
        "table",
        split_axis=0,
        concat_axis=0,
        tiled=True,
    ).reshape(slot_count, emb_width)
    level_sum = scatter_sum(narrow_sum, "table", table_levels[:1])
    table_sum = scatter_sum(level_sum, "table", table_levels[1:-1])
    all_ids = in_order(near_ids, other_ids).reshape(-1, SLOTS * HOT)
    sent_grad = row_grads(all_ids, returned, row_dev)
    pieces = scattered_pieces(table_sum, "table", table_levels[-1])
    sent_grad, *pieces = lax.optimization_barrier((sent_grad, *pieces))
    if paired:
        mine = sent_grad
        other = lax.ppermute(sent_grad, "narrow", sent_from("narrow", 1, 2, 1))
    else:
        share = scatter_sum(sent_grad, "narrow", narrow_levels)
        mine = gather_blocks(share, "narrow", narrow_levels)
        other = jnp.zeros_like(mine)
    level_sum = gather_blocks(summed(pieces), "table", table_levels[1:])
    level_sum, other = lax.optimization_barrier((level_sum, other))
    pieces = gathered_pieces(level_sum, "table", table_levels[0])
    new_rows, new_accum = update_rows(
        narrow_index.reshape(1), table_rows, mine, other, accum, narrows
    )
    scale = 1.0 / math.sqrt(samples * tables * narrows)
    spot, last = pieces[-1]
    grads = spread_pieces(pieces[:-1], scale, factor_down.shape[0])
    last, new_rows, new_accum, *grads = lax.optimization_barrier(
        (last, new_rows, new_accum, *grads)
    )
    down_grad, up_grad = spread_pieces([(spot, last)], scale, factor_down.shape[0], grads)
    return (logits, down_grad, up_grad, new_rows, new_accum)


def solution(mesh):
    in_specs = (
        P("table", None),
        P("table"),
        P("narrow", None),
        P("narrow", None),
        P(),
        P(),
        P(("table", "narrow")),
        P(("table", "narrow"), None),
        P(("table", "narrow"), None),
    )
    out_specs = (
        P(("table", "narrow")),
        P("narrow", None),
        P("narrow", None),
        P("table", None),
        P(("table", "narrow")),
    )
    return jax.shard_map(local, mesh=mesh, in_specs=in_specs, out_specs=out_specs, check_vma=False)
```

```python
import functools
import math

import jax
import jax.numpy as jnp
from jax import lax
from jax.experimental import pallas as pl
from jax.experimental.pallas import tpu as pltpu
from jax.sharding import PartitionSpec as P

FEAT = 8
HOT = 4


LEARN_RATE = 0.2
LOSS_SCALE = 32.0
ADA_EPS = 1e-06


SLOTS = 128
MIB = 1024 * 1024


def matmul(left, right):
    return jnp.dot(left, right, preferred_element_type=jnp.float32)


def transposed_dot(left, right):
    return lax.dot_general(
        left, right, (((0,), (0,)), ((), ())), preferred_element_type=jnp.float32
    )


def rows_dot(left, right):
    return lax.dot_general(
        left, right, (((1,), (1,)), ((), ())), preferred_element_type=jnp.float32
    )


def kernel_call(
    kernel, out_shape, cost, scratch=(), flags=0, operands=0, left=0, left_out=(), aliases=None, room=8
):
    flops, moved = cost
    smem = pl.BlockSpec(memory_space=pltpu.SMEM)
    vmem = pl.BlockSpec(memory_space=pltpu.VMEM)
    hbm = pl.BlockSpec(memory_space=pltpu.HBM)
    if isinstance(out_shape, tuple):
        out_specs = tuple(hbm if i in left_out else vmem for i in range(len(out_shape)))
    else:
        out_specs = hbm if left_out else vmem
    return pl.pallas_call(
        kernel,
        in_specs=[smem] * flags + [vmem] * operands + [hbm] * left,
        out_specs=out_specs,
        input_output_aliases=aliases or {},
        out_shape=out_shape,
        scratch_shapes=scratch,
        compiler_params=pltpu.CompilerParams(vmem_limit_bytes=room * MIB),
        cost_estimate=pl.CostEstimate(flops=flops, bytes_accessed=moved, transcendentals=0),
    )


def split_ids(ids):
    shifted = ids + 1
    high = lax.shift_right_logical(shifted, 5).astype(jnp.float32).astype(jnp.bfloat16)
    low = (shifted & 31).astype(jnp.float32).astype(jnp.bfloat16)
    return high, low


def lookup_choice():
    shape = (HOT * SLOTS, HOT * SLOTS)
    row = lax.broadcasted_iota(jnp.int32, shape, 0)
    column = lax.broadcasted_iota(jnp.int32, shape, 1)
    wanted = (row & (SLOTS - 1)) * HOT + lax.shift_right_logical(row, 7)
    return jnp.where(wanted == column, 1.0, 0.0).astype(jnp.bfloat16)


def joined(digits):
    high, low = digits
    return (high * 32.0 + low - 1.0).astype(jnp.int32)


def ones_where(mask):
    return jnp.where(mask, jnp.asarray(1, jnp.bfloat16), jnp.asarray(0, jnp.bfloat16))


def pool_kernel(part, far, ids_ref, rows_ref, *refs):
    if far:
        out_ref, counts_ref = refs
    else:
        out_ref, counts_ref, held_ref, sem = refs
        fetch = pltpu.make_async_copy(rows_ref, held_ref, sem)
        fetch.start()
    slots = counts_ref.shape[0]
    per_block = HOT * SLOTS
    if len(ids_ref.shape) == 3:
        ids = ids_ref[:, 0, part * per_block : (part + 1) * per_block]
    else:
        ids = ids_ref[:, part * per_block : (part + 1) * per_block]
    choice = lookup_choice()
    high, low = split_ids(ids)
    columns = joined((rows_dot(choice, high), rows_dot(choice, low))).astype(jnp.int16)
    position = lax.broadcasted_iota(jnp.int32, (SLOTS, rows_ref.shape[0]), 1).astype(jnp.int16)
    for block in range(slots // SLOTS):
        counts = None
        for lookup in range(HOT):
            column = columns[lookup * SLOTS : (lookup + 1) * SLOTS, block : block + 1]
            found = ones_where(column == position)
            counts = found if counts is None else counts + found
        counts_ref[block * SLOTS : (block + 1) * SLOTS, :] = counts
    if far:
        rows = rows_ref[...]
    else:
        fetch.wait()
        rows = held_ref[...]
    out_ref[...] = matmul(counts_ref[...], rows).astype(jnp.bfloat16)


def pool_lookups(part, ids, rows):
    far = part == 1
    slots = ids.shape[0] * SLOTS
    row_dev, width = rows.shape
    scratch = [pltpu.VMEM((slots, row_dev), jnp.bfloat16)]
    if not far:
        scratch += [pltpu.VMEM((row_dev, width), jnp.bfloat16), pltpu.SemaphoreType.DMA]
    return kernel_call(
        functools.partial(pool_kernel, part, far),
        jax.ShapeDtypeStruct((slots, width), jnp.bfloat16),
        (2 * slots * row_dev * width, 2 * row_dev * width + 2 * slots * width),
        scratch,
        operands=2 if far else 1,
        left=0 if far else 1,
        room=12 if far else 56,
    )(ids, rows)


def row_grad_kernel(ids_ref, given_ref, out_ref, counts_ref, grads_ref, sem):
    fetch = pltpu.make_async_copy(given_ref, grads_ref, sem)
    fetch.start()
    blocks = ids_ref.shape[0]
    row_dev = out_ref.shape[0]
    tile = 64
    high, low = split_ids(ids_ref[...])
    choice = lookup_choice()
    lines = joined((rows_dot(high, choice), rows_dot(low, choice)))
    position = lax.broadcasted_iota(jnp.int32, (tile, SLOTS), 0).astype(jnp.int16)
    for block in range(blocks):
        spread = []
        for lookup in range(HOT):
            line = lines[block : block + 1, lookup * SLOTS : (lookup + 1) * SLOTS]
            spread.append(jnp.broadcast_to(line, (tile, SLOTS)).astype(jnp.int16))
        for start in range(0, row_dev, tile):
            counts = None
            for lookup in range(HOT):
                found = ones_where(spread[lookup] - jnp.asarray(start, jnp.int16) == position)
                counts = found if counts is None else counts + found
            counts_ref[start : start + tile, block * SLOTS : (block + 1) * SLOTS] = counts
    fetch.wait()
    out_ref[...] = matmul(counts_ref[...], grads_ref[...]).astype(jnp.bfloat16)


def row_grads(ids, slot_grads, row_dev):
    slot_count, emb = slot_grads.shape
    return kernel_call(
        row_grad_kernel,
        jax.ShapeDtypeStruct((row_dev, emb), jnp.bfloat16),
        (2 * row_dev * slot_count * emb, 2 * slot_grads.size + 2 * row_dev * emb),
        [
            pltpu.VMEM((row_dev, slot_count), jnp.bfloat16),
            pltpu.VMEM((slot_count, emb), jnp.bfloat16),
            pltpu.SemaphoreType.DMA,
        ],
        operands=1,
        left=1,
        room=16,
    )(ids, slot_grads)


def diagonal(size):
    row = lax.broadcasted_iota(jnp.int32, (size, size), 0)
    return row == lax.broadcasted_iota(jnp.int32, (size, size), 1)


def as_column(line):
    return jnp.sum(jnp.where(diagonal(line.shape[1]), line, 0.0), axis=1, keepdims=True)


def as_line(column):
    return jnp.sum(jnp.where(diagonal(column.shape[0]), column, 0.0), axis=0, keepdims=True)


def return_kernel(goals_ref, grads_ref, out_ref, pick_ref):
    blocks = goals_ref.shape[0]
    bags = grads_ref.shape[0]
    samples = bags // FEAT
    high, low = split_ids(goals_ref[...])
    unit = ones_where(diagonal(SLOTS))
    columns = joined((rows_dot(unit, high), rows_dot(unit, low))).astype(jnp.int16)
    place = lax.broadcasted_iota(jnp.int32, (SLOTS, bags), 1)
    order = ((place % samples) * FEAT + place // samples).astype(jnp.int16)
    for block in range(blocks):
        pick_ref[block * SLOTS : (block + 1) * SLOTS, :] = ones_where(
            columns[:, block : block + 1] == order
        )
    out_ref[...] = matmul(pick_ref[...], grads_ref[...]).astype(jnp.bfloat16)


def return_grads(goals, grads):
    bags, emb = grads.shape
    slot_count = goals.size
    return kernel_call(
        return_kernel,
        jax.ShapeDtypeStruct((slot_count, emb), jnp.bfloat16),
        (2 * slot_count * bags * emb, 2 * grads.size + 2 * slot_count * emb),
        [pltpu.VMEM((slot_count, bags), jnp.bfloat16)],
        operands=2,
        room=12,
    )(goals.reshape(slot_count // SLOTS, SLOTS), grads)


def dense_kernel(
    swap_ref,
    goals_ref,
    bias_ref,
    weight_ref,
    target_ref,
    near_ref,
    far_ref,
    down_ref,
    up_ref,
    logits_ref,
    grads_ref,
    kept_ref,
    sent_ref,
    place_ref,
    wide_ref,
    dcross_ref,
    shifted_ref,
):
    samples = target_ref.shape[1]
    width, rank = down_ref.shape
    emb = width // FEAT
    half = width // 2
    chunk = 512
    first_bag = lax.broadcasted_iota(jnp.int32, (samples, chunk), 0) * FEAT
    for start in range(0, goals_ref.shape[1], chunk):
        line = goals_ref[:, start : start + chunk]
        nth = (jnp.broadcast_to(line, (samples, chunk)) - first_bag).astype(jnp.int16)
        for f in range(FEAT):
            place_ref[f * samples : (f + 1) * samples, start : start + chunk] = ones_where(
                nth == jnp.asarray(f, jnp.int16)
            )
    features = [slice(f * emb, (f + 1) * emb) for f in range(FEAT)]
    slots = near_ref.shape[0]
    for f, part in enumerate(features):
        spot = slice(f * samples, (f + 1) * samples)
        pooled = matmul(place_ref[spot, :slots], near_ref[...])
        pooled = pooled + matmul(place_ref[spot, slots:], far_ref[...])
        wide_ref[:, part] = pooled.astype(jnp.bfloat16)
    hidden = matmul(wide_ref[...], down_ref[...]).astype(jnp.bfloat16)
    summed = jnp.zeros((samples, emb), jnp.float32)
    for part in features:
        shifted = rows_dot(hidden, up_ref[part, :]) + bias_ref[:, part]
        shifted_ref[:, part] = shifted
        feats = wide_ref[:, part].astype(jnp.float32)
        summed = summed + (feats * shifted + feats) * weight_ref[:, part].astype(jnp.float32)
    logits = jnp.sum(summed, axis=1, keepdims=True)
    logits_ref[...] = as_line(logits)
    dlogit = LOSS_SCALE * (jax.nn.sigmoid(logits) - as_column(target_ref[...]))
    for part in features:
        dmixed = dlogit * weight_ref[:, part].astype(jnp.float32)
        feats = wide_ref[:, part].astype(jnp.float32)
        dcross_ref[:, part] = (dmixed * feats).astype(jnp.bfloat16)
    dhidden = matmul(dcross_ref[...], up_ref[...]).astype(jnp.bfloat16)
    for f, part in enumerate(features):
        dmixed = dlogit * weight_ref[:, part].astype(jnp.float32)
        back_term = rows_dot(dhidden, down_ref[part, :])
        grads = dmixed * (shifted_ref[:, part] + 1.0) + back_term
        grads_ref[f * samples : (f + 1) * samples, :] = grads.astype(jnp.bfloat16)
    for step in range(FEAT):
        into_half = swap_ref[0] if step * emb < half else 1 - swap_ref[0]
        spot = (step * emb) % half
        part = pl.ds(pl.multiple_of(into_half * half + spot, emb), emb)
        out_ref = kept_ref if step * emb < half else sent_ref
        down_term = transposed_dot(wide_ref[:, part], dhidden)
        up_term = transposed_dot(dcross_ref[:, part], hidden)
        out_ref[spot : spot + emb, :rank] = down_term.astype(jnp.bfloat16)
        out_ref[spot : spot + emb, rank:] = up_term.astype(jnp.bfloat16)


def dense_step(swap, goals, near, far, down_full, up_full, bias, weight, target):
    samples = target.shape[0]
    slots, emb = 2 * near.shape[0], near.shape[1]
    width, rank = down_full.shape
    flops = 2 * slots * samples * width + 12 * samples * width * rank
    logits, grads, kept, sent = kernel_call(
        dense_kernel,
        (
            jax.ShapeDtypeStruct((1, samples), jnp.float32),
            jax.ShapeDtypeStruct((samples * FEAT, emb), jnp.bfloat16),
            jax.ShapeDtypeStruct((width // 2, 2 * rank), jnp.bfloat16),
            jax.ShapeDtypeStruct((width // 2, 2 * rank), jnp.bfloat16),
        ),
        (flops, 4 * near.size + 8 * width * rank),
        [
            pltpu.VMEM((samples * FEAT, slots), jnp.bfloat16),
            pltpu.VMEM((samples, width), jnp.bfloat16),
            pltpu.VMEM((samples, width), jnp.bfloat16),
            pltpu.VMEM((samples, width), jnp.float32),
        ],
        flags=1,
        operands=8,
        room=20,
    )(
        swap,
        goals.reshape(1, slots),
        bias.reshape(1, width),
        weight.reshape(1, width),
        target.reshape(1, samples),
        near,
        far,
        down_full,
        up_full,
    )
    return logits.reshape(samples), grads, kept, sent


def spread_kernel(count, scale, aliased, spots_ref, *refs):
    piece_refs = refs[:count]
    down_out_ref, up_out_ref, down_ref, up_ref, sems = refs[count + aliased :]
    rows = piece_refs[0].shape[0]
    rank = down_ref.shape[1]
    stores = []
    for i, piece_ref in enumerate(piece_refs):
        here = slice(i * rows, (i + 1) * rows)
        spot = pl.ds(pl.multiple_of(spots_ref[i] * rows, rows), rows)
        for half, (from_ref, to_ref) in enumerate(((down_ref, down_out_ref), (up_ref, up_out_ref))):
            part = slice(half * rank, (half + 1) * rank)
            from_ref[here, :] = piece_ref[:, part].astype(jnp.float32) * scale
            stores.append(
                pltpu.make_async_copy(from_ref.at[here, :], to_ref.at[spot, :], sems.at[len(stores)])
            )
            stores[-1].start()
    for store in stores:
        store.wait()


def spread_pieces(pieces, scale, rows, given=()):
    count = len(pieces)
    spots = jnp.stack([spot for spot, _ in pieces]).astype(jnp.int32)
    arrays = [piece for _, piece in pieces]
    step, both = arrays[0].shape
    rank = both // 2
    shape = jax.ShapeDtypeStruct((rows, rank), jnp.float32)
    block = pltpu.VMEM((count * step, rank), jnp.float32)
    return kernel_call(
        functools.partial(spread_kernel, count, scale, len(given)),
        (shape, shape),
        (count * step * both, 6 * count * step * both),
        [block, block, pltpu.SemaphoreType.DMA((2 * count,))],
        flags=1,
        operands=count,
        left=len(given),
        left_out=(0, 1),
        aliases={1 + count + i: i for i in range(len(given))},
    )(spots, *arrays, *given)


def update_kernel(share_ref, rows_ref, mine_ref, other_ref, accum_ref, rows_out_ref, accum_out_ref):
    chunks = accum_ref.shape[0]
    per_share = accum_out_ref.shape[0]
    for chunk in range(chunks):
        part = slice(chunk * SLOTS, (chunk + 1) * SLOTS)
        row_grad = mine_ref[part, :].astype(jnp.float32) + other_ref[part, :].astype(jnp.float32)
        squares = jnp.mean(row_grad * row_grad, axis=1, keepdims=True)
        accum = as_column(accum_ref[chunk : chunk + 1, :]) + squares
        step = LEARN_RATE * row_grad * lax.rsqrt(accum + ADA_EPS)
        rows_out_ref[part, :] = (rows_ref[part, :].astype(jnp.float32) - step).astype(jnp.bfloat16)

        @pl.when(share_ref[0] == chunk // per_share)
        def _():
            accum_out_ref[chunk % per_share : chunk % per_share + 1, :] = as_line(accum)


def update_rows(share, rows, mine, other, accum, narrows):
    row_dev, emb = rows.shape
    chunks = row_dev // SLOTS
    new_rows, new_accum = kernel_call(
        update_kernel,
        (
            jax.ShapeDtypeStruct((row_dev, emb), jnp.bfloat16),
            jax.ShapeDtypeStruct((chunks // narrows, SLOTS), jnp.float32),
        ),
        (8 * rows.size, 8 * rows.size),
        flags=1,
        operands=4,
    )(share, rows, mine, other, accum.reshape(chunks, SLOTS))
    return new_rows, new_accum.reshape(row_dev // narrows)


def group_levels(size):
    levels = []
    stride = 1
    while size % 4 == 0:
        levels.append((stride, 4))
        stride, size = stride * 4, size // 4
    if size > 1:
        levels.append((stride, size))
    return levels


def partner_index(index, stride, group, step):
    place = (index // stride) % group
    if group & (group - 1) == 0:
        other = place ^ step
    else:
        other = (place + step) % group
    return index + (other - place) * stride


def sent_from(axis, stride, group, step):
    size = lax.axis_size(axis)
    return [(partner_index(i, stride, group, step), i) for i in range(size)]


def scattered_pieces(blocks, axis, level):
    stride, group = level
    rows = blocks.shape[0] // group
    place = (lax.axis_index(axis) // stride) % group
    pieces = [lax.dynamic_slice_in_dim(blocks, place * rows, rows, 0)]
    for step in range(1, group):
        pairs = sent_from(axis, stride, group, step)
        if group & (group - 1) == 0:
            goal = place ^ step
        else:
            goal = (place + group - step) % group
        outgoing = lax.dynamic_slice_in_dim(blocks, goal * rows, rows, 0)
        pieces.append(lax.ppermute(outgoing, axis, pairs))
    return pieces


def summed(pieces):
    total = pieces[0].astype(jnp.float32)
    for piece in pieces[1:]:
        total = total + piece.astype(jnp.float32)
    return total.astype(jnp.bfloat16)


def scatter_sum(blocks, axis, levels):
    for level in levels:
        blocks = summed(scattered_pieces(blocks, axis, level))
    return blocks


def gathered_pieces(block, axis, level):
    stride, group = level
    index = lax.axis_index(axis)
    pieces = [((index // stride) % group, block)]
    for step in range(1, group):
        origin = partner_index(index, stride, group, step)
        came = lax.ppermute(block, axis, sent_from(axis, stride, group, step))
        pieces.append(((origin // stride) % group, came))
    return pieces


def gather_blocks(block, axis, levels):
    for level in reversed(levels):
        rows = block.shape[0]
        pieces = gathered_pieces(block, axis, level)
        block = jnp.zeros((len(pieces) * rows,) + block.shape[1:], block.dtype)
        for place, piece in pieces:
            block = lax.dynamic_update_slice_in_dim(block, piece, place * rows, 0)
    return block


def local(
    table_rows, accum, factor_down, factor_up, cross_bias, out_weight, target, bag_rows, slot_target
):
    tables = lax.axis_size("table")
    narrows = lax.axis_size("narrow")
    row_dev, emb_width = table_rows.shape
    pools_per = slot_target.shape[1]
    samples = target.shape[0]
    bag_count = samples * FEAT
    slot_count = tables * pools_per
    narrow_levels = group_levels(narrows)
    table_levels = group_levels(tables)
    table_index = lax.axis_index("table")
    narrow_index = lax.axis_index("narrow")
    near_count = tables // 2
    far_half = table_index // near_count
    halves = [list(range(near_count)), list(range(near_count, tables))]
    across = [(i, (i + near_count) % tables) for i in range(tables)]
    paired = narrows == 2
    swap = (narrow_index if paired else narrow_index * 0).reshape(1)

    def near_and_far(rows):
        return tuple(
            lax.dynamic_slice_in_dim(rows, half * near_count, near_count, 0)
            for half in (far_half, 1 - far_half)
        )

    def in_order(near, far):
        return jnp.where(
            far_half == 0, jnp.concatenate([near, far]), jnp.concatenate([far, near])
        )

    def narrow_whole(block):
        if not paired:
            return gather_blocks(block, "narrow", narrow_levels)
        came = lax.ppermute(block, "narrow", sent_from("narrow", 1, 2, 1))
        first = jnp.where(narrow_index == 0, block, came)
        second = jnp.where(narrow_index == 0, came, block)
        return jnp.concatenate([first, second], axis=0)

    share_rows = row_dev // narrows
    own_share = lax.dynamic_slice_in_dim(table_rows, narrow_index * share_rows, share_rows, 0)
    far_share = lax.ppermute(own_share, "table", across)
    down_full = narrow_whole(factor_down)
    up_full = narrow_whole(factor_up)

    per_window = bag_rows.shape[1]
    asked = jnp.concatenate(near_and_far(bag_rows), axis=1)[:, None, :]
    asked = lax.all_to_all(
        asked, "table", split_axis=0, concat_axis=0, tiled=True, axis_index_groups=halves
    )
    near_ids, far_ids = asked[:, 0, :per_window], asked[:, 0, per_window:]
    if per_window != SLOTS * HOT:
        by_block = (ids.reshape(-1, SLOTS * HOT) for ids in (near_ids, far_ids))
        asked = jnp.concatenate(tuple(by_block), axis=1)

    def answered(sums):
        return lax.all_to_all(
            sums.reshape(near_count, pools_per, emb_width),
            "table",
            split_axis=0,
            concat_axis=0,
            tiled=True,
            axis_index_groups=halves,
        ).reshape(slot_count // 2, emb_width)

    sums = pool_lookups(0, asked, table_rows)
    sums, far_share = lax.optimization_barrier((sums, far_share))
    near = answered(sums)
    far = answered(pool_lookups(1, asked, narrow_whole(far_share)))
    other_ids = lax.ppermute(far_ids, "table", across)
    goals = jnp.concatenate(near_and_far(slot_target))
    near, far, other_ids, down_full, up_full, goals = lax.optimization_barrier(
        (near, far, other_ids, down_full, up_full, goals)
    )
    logits, bag_grads, kept, sent = dense_step(
        swap,
        goals,
        near,
        far,
        down_full,
        up_full,
        cross_bias,
        out_weight,
        target,
    )
    if paired:
        came = lax.ppermute(sent, "narrow", sent_from("narrow", 1, 2, 1))
        narrow_sum = (kept.astype(jnp.float32) + came.astype(jnp.float32)).astype(jnp.bfloat16)
    else:
        narrow_sum = scatter_sum(jnp.concatenate([kept, sent], axis=0), "narrow", narrow_levels)
    slot_grads = return_grads(slot_target, bag_grads)
    slot_grads, narrow_sum = lax.optimization_barrier((slot_grads, narrow_sum))
    returned = lax.all_to_all(
        slot_grads.reshape(tables, pools_per, emb_width),
        "table",
        split_axis=0,
        concat_axis=0,
        tiled=True,
    ).reshape(slot_count, emb_width)
    level_sum = scatter_sum(narrow_sum, "table", table_levels[:1])
    table_sum = scatter_sum(level_sum, "table", table_levels[1:-1])
    all_ids = in_order(near_ids, other_ids).reshape(-1, SLOTS * HOT)
    sent_grad = row_grads(all_ids, returned, row_dev)
    pieces = scattered_pieces(table_sum, "table", table_levels[-1])
    sent_grad, *pieces = lax.optimization_barrier((sent_grad, *pieces))
    if paired:
        mine = sent_grad
        other = lax.ppermute(sent_grad, "narrow", sent_from("narrow", 1, 2, 1))
    else:
        share = scatter_sum(sent_grad, "narrow", narrow_levels)
        mine = gather_blocks(share, "narrow", narrow_levels)
        other = jnp.zeros_like(mine)
    level_sum = gather_blocks(summed(pieces), "table", table_levels[1:])
    pieces = gathered_pieces(level_sum, "table", table_levels[0])
    new_rows, new_accum = update_rows(
        narrow_index.reshape(1), table_rows, mine, other, accum, narrows
    )
    scale = 1.0 / math.sqrt(samples * tables * narrows)
    spot, last = pieces[-1]
    grads = spread_pieces(pieces[:-1], scale, factor_down.shape[0])
    last, new_rows, new_accum, *grads = lax.optimization_barrier(
        (last, new_rows, new_accum, *grads)
    )
    down_grad, up_grad = spread_pieces([(spot, last)], scale, factor_down.shape[0], grads)
    return (logits, down_grad, up_grad, new_rows, new_accum)


def solution(mesh):
    in_specs = (
        P("table", None),
        P("table"),
        P("narrow", None),
        P("narrow", None),
        P(),
        P(),
        P(("table", "narrow")),
        P(("table", "narrow"), None),
        P(("table", "narrow"), None),
    )
    out_specs = (
        P(("table", "narrow")),
        P("narrow", None),
        P("narrow", None),
        P("table", None),
        P(("table", "narrow")),
    )
    return jax.shard_map(local, mesh=mesh, in_specs=in_specs, out_specs=out_specs, check_vma=False)
```

```python
import functools
import math

import jax
import jax.numpy as jnp
from jax import lax
from jax.experimental import pallas as pl
from jax.experimental.pallas import tpu as pltpu
from jax.sharding import PartitionSpec as P

FEAT = 8
HOT = 4


LEARN_RATE = 0.2
LOSS_SCALE = 32.0
ADA_EPS = 1e-06


SLOTS = 128
MIB = 1024 * 1024


def matmul(left, right):
    return jnp.dot(left, right, preferred_element_type=jnp.float32)


def transposed_dot(left, right):
    return lax.dot_general(
        left, right, (((0,), (0,)), ((), ())), preferred_element_type=jnp.float32
    )


def rows_dot(left, right):
    return lax.dot_general(
        left, right, (((1,), (1,)), ((), ())), preferred_element_type=jnp.float32
    )


def kernel_call(
    kernel, out_shape, cost, scratch=(), flags=0, operands=0, left=0, left_out=(), aliases=None, room=8
):
    flops, moved = cost
    smem = pl.BlockSpec(memory_space=pltpu.SMEM)
    vmem = pl.BlockSpec(memory_space=pltpu.VMEM)
    hbm = pl.BlockSpec(memory_space=pltpu.HBM)
    if isinstance(out_shape, tuple):
        out_specs = tuple(hbm if i in left_out else vmem for i in range(len(out_shape)))
    else:
        out_specs = hbm if left_out else vmem
    return pl.pallas_call(
        kernel,
        in_specs=[smem] * flags + [vmem] * operands + [hbm] * left,
        out_specs=out_specs,
        input_output_aliases=aliases or {},
        out_shape=out_shape,
        scratch_shapes=scratch,
        compiler_params=pltpu.CompilerParams(vmem_limit_bytes=room * MIB),
        cost_estimate=pl.CostEstimate(flops=flops, bytes_accessed=moved, transcendentals=0),
    )


def split_ids(ids):
    shifted = ids + 1
    high = lax.shift_right_logical(shifted, 5).astype(jnp.float32).astype(jnp.bfloat16)
    low = (shifted & 31).astype(jnp.float32).astype(jnp.bfloat16)
    return high, low


def lookup_choice():
    shape = (HOT * SLOTS, HOT * SLOTS)
    row = lax.broadcasted_iota(jnp.int32, shape, 0)
    column = lax.broadcasted_iota(jnp.int32, shape, 1)
    wanted = (row & (SLOTS - 1)) * HOT + lax.shift_right_logical(row, 7)
    return jnp.where(wanted == column, 1.0, 0.0).astype(jnp.bfloat16)


def joined(digits):
    high, low = digits
    return (high * 32.0 + low - 1.0).astype(jnp.int32)


def ones_where(mask):
    return jnp.where(mask, jnp.asarray(1, jnp.bfloat16), jnp.asarray(0, jnp.bfloat16))


def pool_kernel(part, ids_ref, rows_ref, *refs):
    out_ref, counts_ref, sums_ref, sem = refs[-4:]
    slots = counts_ref.shape[0]
    sources, _, pools, _ = out_ref.shape
    per_block = HOT * SLOTS
    if len(ids_ref.shape) == 3:
        ids = ids_ref[:, 0, part * per_block : (part + 1) * per_block]
    else:
        ids = ids_ref[:, part * per_block : (part + 1) * per_block]
    choice = lookup_choice()
    high, low = split_ids(ids)
    columns = joined((rows_dot(choice, high), rows_dot(choice, low))).astype(jnp.int16)
    position = lax.broadcasted_iota(jnp.int32, (SLOTS, rows_ref.shape[0]), 1).astype(jnp.int16)
    for block in range(slots // SLOTS):
        counts = None
        for lookup in range(HOT):
            column = columns[lookup * SLOTS : (lookup + 1) * SLOTS, block : block + 1]
            found = ones_where(column == position)
            counts = found if counts is None else counts + found
        counts_ref[block * SLOTS : (block + 1) * SLOTS, :] = counts
    sums = matmul(counts_ref[...], rows_ref[...]).astype(jnp.bfloat16)
    for source in range(sources):
        sums_ref[source] = sums[source * pools : (source + 1) * pools]
    store = pltpu.make_async_copy(sums_ref, out_ref.at[:, part], sem)
    store.start()
    store.wait()


def pool_lookups(part, ids, rows, pools, given=()):
    slots = ids.shape[0] * SLOTS
    row_dev, width = rows.shape
    return kernel_call(
        functools.partial(pool_kernel, part),
        jax.ShapeDtypeStruct((slots // pools, 2, pools, width), jnp.bfloat16),
        (2 * slots * row_dev * width, 2 * row_dev * width + 2 * slots * width),
        [
            pltpu.VMEM((slots, row_dev), jnp.bfloat16),
            pltpu.VMEM((slots // pools, pools, width), jnp.bfloat16),
            pltpu.SemaphoreType.DMA,
        ],
        operands=2,
        left=len(given),
        left_out=(0,),
        aliases={2: 0} if given else None,
        room=12,
    )(ids, rows, *given)


def row_grad_kernel(swap_ref, ids_ref, grads_ref, kept_ref, sent_ref, counts_ref, sums_ref):
    sources, _, pools, emb = grads_ref.shape
    row_dev, slots = counts_ref.shape
    half = row_dev // 2
    per_block = HOT * SLOTS
    tile = 64
    choice = lookup_choice()
    position = lax.broadcasted_iota(jnp.int32, (tile, SLOTS), 0).astype(jnp.int16)
    for part in range(2):
        lanes = slice(part * per_block, (part + 1) * per_block)
        ids = ids_ref[:, 0, lanes] if len(ids_ref.shape) == 3 else ids_ref[:, lanes]
        high, low = split_ids(ids)
        lines = joined((rows_dot(high, choice), rows_dot(low, choice)))
        for block in range(slots // SLOTS):
            spread = []
            for lookup in range(HOT):
                line = lines[block : block + 1, lookup * SLOTS : (lookup + 1) * SLOTS]
                spread.append(jnp.broadcast_to(line, (tile, SLOTS)).astype(jnp.int16))
            for start in range(0, row_dev, tile):
                counts = None
                for lookup in range(HOT):
                    found = ones_where(spread[lookup] - jnp.asarray(start, jnp.int16) == position)
                    counts = found if counts is None else counts + found
                counts_ref[start : start + tile, block * SLOTS : (block + 1) * SLOTS] = counts
        grads = grads_ref[:, part].reshape(sources * pools, emb)
        where = slice(part * emb, (part + 1) * emb)
        sums_ref[:, where] = matmul(counts_ref[...], grads).astype(jnp.bfloat16)
    for out_ref, into_half in ((kept_ref, swap_ref[0]), (sent_ref, 1 - swap_ref[0])):
        out_ref[...] = sums_ref[pl.ds(pl.multiple_of(into_half * half, half), half), :]


def row_grads(swap, ids, slot_grads, row_dev):
    sources, _, pools, emb = slot_grads.shape
    slots = sources * pools
    half = jax.ShapeDtypeStruct((row_dev // 2, 2 * emb), jnp.bfloat16)
    return kernel_call(
        row_grad_kernel,
        (half, half),
        (4 * row_dev * slots * emb, 2 * slot_grads.size + 4 * row_dev * emb),
        [
            pltpu.VMEM((row_dev, slots), jnp.bfloat16),
            pltpu.VMEM((row_dev, 2 * emb), jnp.bfloat16),
        ],
        flags=1,
        operands=2,
        room=12,
    )(swap, ids, slot_grads)


def diagonal(size):
    row = lax.broadcasted_iota(jnp.int32, (size, size), 0)
    return row == lax.broadcasted_iota(jnp.int32, (size, size), 1)


def as_column(line):
    return jnp.sum(jnp.where(diagonal(line.shape[1]), line, 0.0), axis=1, keepdims=True)


def as_line(column):
    return jnp.sum(jnp.where(diagonal(column.shape[0]), column, 0.0), axis=0, keepdims=True)


def return_kernel(goals_ref, grads_ref, out_ref, pick_ref):
    blocks = goals_ref.shape[0]
    bags = grads_ref.shape[0]
    samples = bags // FEAT
    high, low = split_ids(goals_ref[...])
    unit = ones_where(diagonal(SLOTS))
    columns = joined((rows_dot(unit, high), rows_dot(unit, low))).astype(jnp.int16)
    place = lax.broadcasted_iota(jnp.int32, (SLOTS, bags), 1)
    order = ((place % samples) * FEAT + place // samples).astype(jnp.int16)
    for block in range(blocks):
        pick_ref[block * SLOTS : (block + 1) * SLOTS, :] = ones_where(
            columns[:, block : block + 1] == order
        )
    out_ref[...] = matmul(pick_ref[...], grads_ref[...]).astype(jnp.bfloat16)


def return_grads(goals, grads):
    bags, emb = grads.shape
    slot_count = goals.size
    return kernel_call(
        return_kernel,
        jax.ShapeDtypeStruct((slot_count, emb), jnp.bfloat16),
        (2 * slot_count * bags * emb, 2 * grads.size + 2 * slot_count * emb),
        [pltpu.VMEM((slot_count, bags), jnp.bfloat16)],
        operands=2,
        room=12,
    )(goals.reshape(slot_count // SLOTS, SLOTS), grads)


def dense_kernel(
    swap_ref,
    goals_ref,
    bias_ref,
    weight_ref,
    target_ref,
    arrived_ref,
    down_ref,
    up_ref,
    logits_ref,
    grads_ref,
    kept_ref,
    sent_ref,
    place_ref,
    wide_ref,
    dcross_ref,
    shifted_ref,
):
    samples = target_ref.shape[1]
    width, rank = down_ref.shape
    emb = width // FEAT
    half = width // 2
    chunk = 512
    first_bag = lax.broadcasted_iota(jnp.int32, (samples, chunk), 0) * FEAT
    for start in range(0, goals_ref.shape[1], chunk):
        line = goals_ref[:, start : start + chunk]
        nth = (jnp.broadcast_to(line, (samples, chunk)) - first_bag).astype(jnp.int16)
        for f in range(FEAT):
            place_ref[f * samples : (f + 1) * samples, start : start + chunk] = ones_where(
                nth == jnp.asarray(f, jnp.int16)
            )
    features = [slice(f * emb, (f + 1) * emb) for f in range(FEAT)]
    for f, part in enumerate(features):
        spot = slice(f * samples, (f + 1) * samples)
        wide_ref[:, part] = matmul(place_ref[spot, :], arrived_ref[...]).astype(jnp.bfloat16)
    hidden = matmul(wide_ref[...], down_ref[...]).astype(jnp.bfloat16)
    summed = jnp.zeros((samples, emb), jnp.float32)
    for part in features:
        shifted = rows_dot(hidden, up_ref[part, :]) + bias_ref[:, part]
        shifted_ref[:, part] = shifted
        feats = wide_ref[:, part].astype(jnp.float32)
        summed = summed + (feats * shifted + feats) * weight_ref[:, part].astype(jnp.float32)
    logits = jnp.sum(summed, axis=1, keepdims=True)
    logits_ref[...] = as_line(logits)
    dlogit = LOSS_SCALE * (jax.nn.sigmoid(logits) - as_column(target_ref[...]))
    for part in features:
        dmixed = dlogit * weight_ref[:, part].astype(jnp.float32)
        feats = wide_ref[:, part].astype(jnp.float32)
        dcross_ref[:, part] = (dmixed * feats).astype(jnp.bfloat16)
    dhidden = matmul(dcross_ref[...], up_ref[...]).astype(jnp.bfloat16)
    for f, part in enumerate(features):
        dmixed = dlogit * weight_ref[:, part].astype(jnp.float32)
        back_term = rows_dot(dhidden, down_ref[part, :])
        grads = dmixed * (shifted_ref[:, part] + 1.0) + back_term
        grads_ref[f * samples : (f + 1) * samples, :] = grads.astype(jnp.bfloat16)
    for step in range(FEAT):
        into_half = swap_ref[0] if step * emb < half else 1 - swap_ref[0]
        spot = (step * emb) % half
        part = pl.ds(pl.multiple_of(into_half * half + spot, emb), emb)
        out_ref = kept_ref if step * emb < half else sent_ref
        down_term = transposed_dot(wide_ref[:, part], dhidden)
        up_term = transposed_dot(dcross_ref[:, part], hidden)
        out_ref[spot : spot + emb, :rank] = down_term.astype(jnp.bfloat16)
        out_ref[spot : spot + emb, rank:] = up_term.astype(jnp.bfloat16)


def dense_step(swap, goals, arrived, down_full, up_full, bias, weight, target):
    samples = target.shape[0]
    slots, emb = arrived.shape
    width, rank = down_full.shape
    flops = 2 * slots * samples * width + 12 * samples * width * rank
    logits, grads, kept, sent = kernel_call(
        dense_kernel,
        (
            jax.ShapeDtypeStruct((1, samples), jnp.float32),
            jax.ShapeDtypeStruct((samples * FEAT, emb), jnp.bfloat16),
            jax.ShapeDtypeStruct((width // 2, 2 * rank), jnp.bfloat16),
            jax.ShapeDtypeStruct((width // 2, 2 * rank), jnp.bfloat16),
        ),
        (flops, 2 * arrived.size + 8 * width * rank),
        [
            pltpu.VMEM((samples * FEAT, slots), jnp.bfloat16),
            pltpu.VMEM((samples, width), jnp.bfloat16),
            pltpu.VMEM((samples, width), jnp.bfloat16),
            pltpu.VMEM((samples, width), jnp.float32),
        ],
        flags=1,
        operands=7,
        room=20,
    )(
        swap,
        goals.reshape(1, slots),
        bias.reshape(1, width),
        weight.reshape(1, width),
        target.reshape(1, samples),
        arrived,
        down_full,
        up_full,
    )
    return logits.reshape(samples), grads, kept, sent


def spread_kernel(count, scale, aliased, spots_ref, *refs):
    piece_refs = refs[:count]
    down_out_ref, up_out_ref, down_ref, up_ref, sems = refs[count + aliased :]
    rows = piece_refs[0].shape[0]
    rank = down_ref.shape[1]
    stores = []
    for i, piece_ref in enumerate(piece_refs):
        here = slice(i * rows, (i + 1) * rows)
        spot = pl.ds(pl.multiple_of(spots_ref[i] * rows, rows), rows)
        for half, (from_ref, to_ref) in enumerate(((down_ref, down_out_ref), (up_ref, up_out_ref))):
            part = slice(half * rank, (half + 1) * rank)
            from_ref[here, :] = piece_ref[:, part].astype(jnp.float32) * scale
            stores.append(
                pltpu.make_async_copy(from_ref.at[here, :], to_ref.at[spot, :], sems.at[len(stores)])
            )
            stores[-1].start()
    for store in stores:
        store.wait()


def spread_pieces(pieces, scale, rows, given=()):
    count = len(pieces)
    spots = jnp.stack([spot for spot, _ in pieces]).astype(jnp.int32)
    arrays = [piece for _, piece in pieces]
    step, both = arrays[0].shape
    rank = both // 2
    shape = jax.ShapeDtypeStruct((rows, rank), jnp.float32)
    block = pltpu.VMEM((count * step, rank), jnp.float32)
    return kernel_call(
        functools.partial(spread_kernel, count, scale, len(given)),
        (shape, shape),
        (count * step * both, 6 * count * step * both),
        [block, block, pltpu.SemaphoreType.DMA((2 * count,))],
        flags=1,
        operands=count,
        left=len(given),
        left_out=(0, 1),
        aliases={1 + count + i: i for i in range(len(given))},
    )(spots, *arrays, *given)


def update_kernel(rows_ref, far_ref, accum_ref, *refs):
    near_refs = refs[:-2]
    rows_out_ref, accum_out_ref = refs[-2:]
    emb = rows_ref.shape[1]
    for chunk in range(accum_ref.shape[0]):
        part = slice(chunk * SLOTS, (chunk + 1) * SLOTS)
        row_grad = far_ref[part, :].astype(jnp.float32)
        for near_ref in near_refs:
            row_grad = row_grad + near_ref[part, :emb].astype(jnp.float32)
        squares = jnp.mean(row_grad * row_grad, axis=1, keepdims=True)
        accum = as_column(accum_ref[chunk : chunk + 1, :]) + squares
        step = LEARN_RATE * row_grad * lax.rsqrt(accum + ADA_EPS)
        rows_out_ref[part, :] = (rows_ref[part, :].astype(jnp.float32) - step).astype(jnp.bfloat16)
        accum_out_ref[chunk : chunk + 1, :] = as_line(accum)


def update_rows(rows, far, accum, nears):
    share, emb = rows.shape
    chunks = share // SLOTS
    new_rows, new_accum = kernel_call(
        update_kernel,
        (
            jax.ShapeDtypeStruct((share, emb), jnp.bfloat16),
            jax.ShapeDtypeStruct((chunks, SLOTS), jnp.float32),
        ),
        (8 * rows.size, 8 * rows.size),
        operands=3 + len(nears),
    )(rows, far, accum.reshape(chunks, SLOTS), *nears)
    return new_rows, new_accum.reshape(share)


def join_kernel(swap_ref, mine_ref, other_ref, out_ref, sems):
    half = mine_ref.shape[0]
    copies = []
    for i, (from_ref, at) in enumerate(((mine_ref, swap_ref[0]), (other_ref, 1 - swap_ref[0]))):
        spot = pl.ds(pl.multiple_of(at * half, half), half)
        copies.append(pltpu.make_async_copy(from_ref, out_ref.at[spot, :], sems.at[i]))
        copies[-1].start()
    for copy in copies:
        copy.wait()


def join_halves(swap, mine, other):
    return kernel_call(
        join_kernel,
        jax.ShapeDtypeStruct((2 * mine.shape[0], mine.shape[1]), mine.dtype),
        (0, 8 * mine.size),
        [pltpu.SemaphoreType.DMA((2,))],
        flags=1,
        operands=2,
        left_out=(0,),
    )(swap, mine, other)


def group_levels(size):
    levels = []
    stride = 1
    while size % 4 == 0:
        levels.append((stride, 4))
        stride, size = stride * 4, size // 4
    if size > 1:
        levels.append((stride, size))
    return levels


def partner_index(index, stride, group, step):
    place = (index // stride) % group
    if group & (group - 1) == 0:
        other = place ^ step
    else:
        other = (place + step) % group
    return index + (other - place) * stride


def sent_from(axis, stride, group, step):
    size = lax.axis_size(axis)
    return [(partner_index(i, stride, group, step), i) for i in range(size)]


def scattered_pieces(blocks, axis, level):
    stride, group = level
    rows = blocks.shape[0] // group
    place = (lax.axis_index(axis) // stride) % group
    pieces = [lax.dynamic_slice_in_dim(blocks, place * rows, rows, 0)]
    for step in range(1, group):
        pairs = sent_from(axis, stride, group, step)
        if group & (group - 1) == 0:
            goal = place ^ step
        else:
            goal = (place + group - step) % group
        outgoing = lax.dynamic_slice_in_dim(blocks, goal * rows, rows, 0)
        pieces.append(lax.ppermute(outgoing, axis, pairs))
    return pieces


def summed(pieces):
    total = pieces[0].astype(jnp.float32)
    for piece in pieces[1:]:
        total = total + piece.astype(jnp.float32)
    return total.astype(jnp.bfloat16)


def scatter_sum(blocks, axis, levels):
    for level in levels:
        blocks = summed(scattered_pieces(blocks, axis, level))
    return blocks


def gathered_pieces(block, axis, level):
    stride, group = level
    index = lax.axis_index(axis)
    pieces = [((index // stride) % group, block)]
    for step in range(1, group):
        origin = partner_index(index, stride, group, step)
        came = lax.ppermute(block, axis, sent_from(axis, stride, group, step))
        pieces.append(((origin // stride) % group, came))
    return pieces


def gather_blocks(block, axis, levels):
    for level in reversed(levels):
        rows = block.shape[0]
        pieces = gathered_pieces(block, axis, level)
        block = jnp.zeros((len(pieces) * rows,) + block.shape[1:], block.dtype)
        for place, piece in pieces:
            block = lax.dynamic_update_slice_in_dim(block, piece, place * rows, 0)
    return block


def local(
    table_rows, accum, factor_down, factor_up, cross_bias, out_weight, target, bag_rows, slot_target
):
    tables = lax.axis_size("table")
    narrows = lax.axis_size("narrow")
    row_dev, emb_width = table_rows.shape
    pools_per = slot_target.shape[1]
    samples = target.shape[0]
    bag_count = samples * FEAT
    slot_count = tables * pools_per
    narrow_levels = group_levels(narrows)
    table_levels = group_levels(tables)
    table_index = lax.axis_index("table")
    narrow_index = lax.axis_index("narrow")
    near_count = tables // 2
    far_half = table_index // near_count
    halves = [list(range(near_count)), list(range(near_count, tables))]
    across = [(i, (i + near_count) % tables) for i in range(tables)]
    paired = narrows == 2
    swap = (narrow_index if paired else narrow_index * 0).reshape(1)

    def near_and_far(rows):
        return tuple(
            lax.dynamic_slice_in_dim(rows, half * near_count, near_count, 0)
            for half in (far_half, 1 - far_half)
        )

    def in_order(near, far):
        return jnp.where(
            far_half == 0, jnp.concatenate([near, far]), jnp.concatenate([far, near])
        )

    def narrow_whole(block):
        if not paired:
            return gather_blocks(block, "narrow", narrow_levels)
        came = lax.ppermute(block, "narrow", sent_from("narrow", 1, 2, 1))
        first = jnp.where(narrow_index == 0, block, came)
        second = jnp.where(narrow_index == 0, came, block)
        return jnp.concatenate([first, second], axis=0)

    share_rows = row_dev // narrows
    own_share = lax.dynamic_slice_in_dim(table_rows, narrow_index * share_rows, share_rows, 0)
    far_share = lax.ppermute(own_share, "table", across)
    down_full = narrow_whole(factor_down)
    up_full = narrow_whole(factor_up)

    per_window = bag_rows.shape[1]
    asked = jnp.concatenate(near_and_far(bag_rows), axis=1)[:, None, :]
    asked = lax.all_to_all(
        asked, "table", split_axis=0, concat_axis=0, tiled=True, axis_index_groups=halves
    )
    near_ids, far_ids = asked[:, 0, :per_window], asked[:, 0, per_window:]
    if per_window != SLOTS * HOT:
        by_block = (ids.reshape(-1, SLOTS * HOT) for ids in (near_ids, far_ids))
        asked = jnp.concatenate(tuple(by_block), axis=1)
    sums = pool_lookups(0, asked, table_rows, pools_per)
    sums, far_share = lax.optimization_barrier((sums, far_share))
    sums = pool_lookups(1, asked, narrow_whole(far_share), pools_per, (sums,))
    arrived = lax.all_to_all(
        sums, "table", split_axis=0, concat_axis=0, tiled=True, axis_index_groups=halves
    )
    goals = jnp.stack(near_and_far(slot_target), axis=1)
    arrived, down_full, up_full, goals = lax.optimization_barrier(
        (arrived, down_full, up_full, goals)
    )
    logits, bag_grads, kept, sent = dense_step(
        swap,
        goals,
        arrived.reshape(slot_count, emb_width),
        down_full,
        up_full,
        cross_bias,
        out_weight,
        target,
    )
    if paired:
        came = lax.ppermute(sent, "narrow", sent_from("narrow", 1, 2, 1))
        narrow_sum = (kept.astype(jnp.float32) + came.astype(jnp.float32)).astype(jnp.bfloat16)
    else:
        narrow_sum = scatter_sum(jnp.concatenate([kept, sent], axis=0), "narrow", narrow_levels)
    slot_grads = return_grads(goals, bag_grads)
    slot_grads, narrow_sum = lax.optimization_barrier((slot_grads, narrow_sum))
    returned = lax.all_to_all(
        slot_grads.reshape(near_count, 2, pools_per, emb_width),
        "table",
        split_axis=0,
        concat_axis=0,
        tiled=True,
        axis_index_groups=halves,
    )
    level_sum = scatter_sum(narrow_sum, "table", table_levels[:1])
    table_sum = scatter_sum(level_sum, "table", table_levels[1:-1])
    mine, passed = row_grads(swap, asked, returned, row_dev)
    pieces = scattered_pieces(table_sum, "table", table_levels[-1])
    mine, passed, *pieces = lax.optimization_barrier((mine, passed, *pieces))
    if paired:
        nears = [mine, lax.ppermute(passed, "narrow", sent_from("narrow", 1, 2, 1))]
    else:
        nears = [scatter_sum(jnp.concatenate([mine, passed], axis=0), "narrow", narrow_levels)]
    far_term = summed([term[:, emb_width:] for term in nears])
    level_sum = gather_blocks(summed(pieces), "table", table_levels[1:])
    pieces = gathered_pieces(level_sum, "table", table_levels[0])
    far_term = lax.ppermute(far_term, "table", across)
    own_accum = lax.dynamic_slice_in_dim(accum, narrow_index * share_rows, share_rows, 0)
    new_share, new_accum = update_rows(own_share, far_term, own_accum, nears)
    if paired:
        other_share = lax.ppermute(new_share, "narrow", sent_from("narrow", 1, 2, 1))
        new_rows = join_halves(swap, new_share, other_share)
    else:
        new_rows = gather_blocks(new_share, "narrow", narrow_levels)
    scale = 1.0 / math.sqrt(samples * tables * narrows)
    spot, last = pieces[-1]
    grads = spread_pieces(pieces[:-1], scale, factor_down.shape[0])
    last, *grads = lax.optimization_barrier((last, *grads))
    down_grad, up_grad = spread_pieces([(spot, last)], scale, factor_down.shape[0], grads)
    return (logits, down_grad, up_grad, new_rows, new_accum)


def solution(mesh):
    in_specs = (
        P("table", None),
        P("table"),
        P("narrow", None),
        P("narrow", None),
        P(),
        P(),
        P(("table", "narrow")),
        P(("table", "narrow"), None),
        P(("table", "narrow"), None),
    )
    out_specs = (
        P(("table", "narrow")),
        P("narrow", None),
        P("narrow", None),
        P("table", None),
        P(("table", "narrow")),
    )
    return jax.shard_map(local, mesh=mesh, in_specs=in_specs, out_specs=out_specs, check_vma=False)
```

```python
import functools
import math

import jax
import jax.numpy as jnp
from jax import lax
from jax.experimental import pallas as pl
from jax.experimental.pallas import tpu as pltpu
from jax.sharding import PartitionSpec as P

FEAT = 8
HOT = 4


LEARN_RATE = 0.2
LOSS_SCALE = 32.0
ADA_EPS = 1e-06


SLOTS = 128
MIB = 1024 * 1024


def matmul(left, right):
    return jnp.dot(left, right, preferred_element_type=jnp.float32)


def transposed_dot(left, right):
    return lax.dot_general(
        left, right, (((0,), (0,)), ((), ())), preferred_element_type=jnp.float32
    )


def rows_dot(left, right):
    return lax.dot_general(
        left, right, (((1,), (1,)), ((), ())), preferred_element_type=jnp.float32
    )


def kernel_call(
    kernel, out_shape, cost, scratch=(), flags=0, operands=0, left=0, left_out=(), aliases=None, room=8
):
    flops, moved = cost
    smem = pl.BlockSpec(memory_space=pltpu.SMEM)
    vmem = pl.BlockSpec(memory_space=pltpu.VMEM)
    hbm = pl.BlockSpec(memory_space=pltpu.HBM)
    if isinstance(out_shape, tuple):
        out_specs = tuple(hbm if i in left_out else vmem for i in range(len(out_shape)))
    else:
        out_specs = hbm if left_out else vmem
    return pl.pallas_call(
        kernel,
        in_specs=[smem] * flags + [vmem] * operands + [hbm] * left,
        out_specs=out_specs,
        input_output_aliases=aliases or {},
        out_shape=out_shape,
        scratch_shapes=scratch,
        compiler_params=pltpu.CompilerParams(vmem_limit_bytes=room * MIB),
        cost_estimate=pl.CostEstimate(flops=flops, bytes_accessed=moved, transcendentals=0),
    )


def split_ids(ids):
    shifted = ids + 1
    high = lax.shift_right_logical(shifted, 5).astype(jnp.float32).astype(jnp.bfloat16)
    low = (shifted & 31).astype(jnp.float32).astype(jnp.bfloat16)
    return high, low


def lookup_choice():
    shape = (HOT * SLOTS, HOT * SLOTS)
    row = lax.broadcasted_iota(jnp.int32, shape, 0)
    column = lax.broadcasted_iota(jnp.int32, shape, 1)
    wanted = (row & (SLOTS - 1)) * HOT + lax.shift_right_logical(row, 7)
    return jnp.where(wanted == column, 1.0, 0.0).astype(jnp.bfloat16)


def joined(digits):
    high, low = digits
    return (high * 32.0 + low - 1.0).astype(jnp.int32)


def ones_where(mask):
    return jnp.where(mask, jnp.asarray(1, jnp.bfloat16), jnp.asarray(0, jnp.bfloat16))


def pool_kernel(part, ids_ref, rows_ref, *refs):
    out_ref, counts_ref, sums_ref, sem = refs[-4:]
    slots = counts_ref.shape[0]
    sources, _, pools, _ = out_ref.shape
    per_block = HOT * SLOTS
    if len(ids_ref.shape) == 3:
        ids = ids_ref[:, 0, part * per_block : (part + 1) * per_block]
    else:
        ids = ids_ref[:, part * per_block : (part + 1) * per_block]
    choice = lookup_choice()
    high, low = split_ids(ids)
    columns = joined((rows_dot(choice, high), rows_dot(choice, low))).astype(jnp.int16)
    position = lax.broadcasted_iota(jnp.int32, (SLOTS, rows_ref.shape[0]), 1).astype(jnp.int16)
    for block in range(slots // SLOTS):
        counts = None
        for lookup in range(HOT):
            column = columns[lookup * SLOTS : (lookup + 1) * SLOTS, block : block + 1]
            found = ones_where(column == position)
            counts = found if counts is None else counts + found
        counts_ref[block * SLOTS : (block + 1) * SLOTS, :] = counts
    sums = matmul(counts_ref[...], rows_ref[...]).astype(jnp.bfloat16)
    for source in range(sources):
        sums_ref[source] = sums[source * pools : (source + 1) * pools]
    store = pltpu.make_async_copy(sums_ref, out_ref.at[:, part], sem)
    store.start()
    store.wait()


def pool_lookups(part, ids, rows, pools, given=()):
    slots = ids.shape[0] * SLOTS
    row_dev, width = rows.shape
    return kernel_call(
        functools.partial(pool_kernel, part),
        jax.ShapeDtypeStruct((slots // pools, 2, pools, width), jnp.bfloat16),
        (2 * slots * row_dev * width, 2 * row_dev * width + 2 * slots * width),
        [
            pltpu.VMEM((slots, row_dev), jnp.bfloat16),
            pltpu.VMEM((slots // pools, pools, width), jnp.bfloat16),
            pltpu.SemaphoreType.DMA,
        ],
        operands=2,
        left=len(given),
        left_out=(0,),
        aliases={2: 0} if given else None,
        room=12,
    )(ids, rows, *given)


def row_grad_kernel(swap_ref, ids_ref, grads_ref, kept_ref, sent_ref, counts_ref, sums_ref):
    sources, _, emb = grads_ref.shape
    row_dev, slots = counts_ref.shape
    pools = slots // sources
    half = row_dev // 2
    per_block = HOT * SLOTS
    tile = 64
    choice = lookup_choice()
    position = lax.broadcasted_iota(jnp.int32, (tile, SLOTS), 0).astype(jnp.int16)
    for part in range(2):
        lanes = slice(part * per_block, (part + 1) * per_block)
        ids = ids_ref[:, 0, lanes] if len(ids_ref.shape) == 3 else ids_ref[:, lanes]
        high, low = split_ids(ids)
        lines = joined((rows_dot(high, choice), rows_dot(low, choice)))
        for block in range(slots // SLOTS):
            spread = []
            for lookup in range(HOT):
                line = lines[block : block + 1, lookup * SLOTS : (lookup + 1) * SLOTS]
                spread.append(jnp.broadcast_to(line, (tile, SLOTS)).astype(jnp.int16))
            for start in range(0, row_dev, tile):
                counts = None
                for lookup in range(HOT):
                    found = ones_where(spread[lookup] - jnp.asarray(start, jnp.int16) == position)
                    counts = found if counts is None else counts + found
                counts_ref[start : start + tile, block * SLOTS : (block + 1) * SLOTS] = counts
        grads = grads_ref[:, part * pools : (part + 1) * pools].reshape(slots, emb)
        where = slice(part * emb, (part + 1) * emb)
        sums_ref[:, where] = matmul(counts_ref[...], grads).astype(jnp.bfloat16)
    for out_ref, into_half in ((kept_ref, swap_ref[0]), (sent_ref, 1 - swap_ref[0])):
        out_ref[...] = sums_ref[pl.ds(pl.multiple_of(into_half * half, half), half), :]


def row_grads(swap, ids, slot_grads, pools, row_dev):
    sources, _, emb = slot_grads.shape
    slots = sources * pools
    half = jax.ShapeDtypeStruct((row_dev // 2, 2 * emb), jnp.bfloat16)
    return kernel_call(
        row_grad_kernel,
        (half, half),
        (4 * row_dev * slots * emb, 2 * slot_grads.size + 4 * row_dev * emb),
        [
            pltpu.VMEM((row_dev, slots), jnp.bfloat16),
            pltpu.VMEM((row_dev, 2 * emb), jnp.bfloat16),
        ],
        flags=1,
        operands=2,
        room=12,
    )(swap, ids, slot_grads)


def diagonal(size):
    row = lax.broadcasted_iota(jnp.int32, (size, size), 0)
    return row == lax.broadcasted_iota(jnp.int32, (size, size), 1)


def as_column(line):
    return jnp.sum(jnp.where(diagonal(line.shape[1]), line, 0.0), axis=1, keepdims=True)


def as_line(column):
    return jnp.sum(jnp.where(diagonal(column.shape[0]), column, 0.0), axis=0, keepdims=True)


def return_kernel(goals_ref, grads_ref, out_ref, pick_ref):
    blocks = goals_ref.shape[0]
    bags = grads_ref.shape[0]
    samples = bags // FEAT
    high, low = split_ids(goals_ref[...])
    unit = ones_where(diagonal(SLOTS))
    columns = joined((rows_dot(unit, high), rows_dot(unit, low))).astype(jnp.int16)
    place = lax.broadcasted_iota(jnp.int32, (SLOTS, bags), 1)
    order = ((place % samples) * FEAT + place // samples).astype(jnp.int16)
    for block in range(blocks):
        pick_ref[block * SLOTS : (block + 1) * SLOTS, :] = ones_where(
            columns[:, block : block + 1] == order
        )
    out_ref[...] = matmul(pick_ref[...], grads_ref[...]).astype(jnp.bfloat16)


def return_grads(goals, grads):
    bags, emb = grads.shape
    slot_count = goals.size
    return kernel_call(
        return_kernel,
        jax.ShapeDtypeStruct((slot_count, emb), jnp.bfloat16),
        (2 * slot_count * bags * emb, 2 * grads.size + 2 * slot_count * emb),
        [pltpu.VMEM((slot_count, bags), jnp.bfloat16)],
        operands=2,
        room=12,
    )(goals.reshape(slot_count // SLOTS, SLOTS), grads)


def dense_kernel(
    swap_ref,
    goals_ref,
    bias_ref,
    weight_ref,
    target_ref,
    arrived_ref,
    down_ref,
    up_ref,
    logits_ref,
    grads_ref,
    kept_ref,
    sent_ref,
    place_ref,
    wide_ref,
    dcross_ref,
    shifted_ref,
):
    samples = target_ref.shape[1]
    width, rank = down_ref.shape
    emb = width // FEAT
    half = width // 2
    chunk = 512
    first_bag = lax.broadcasted_iota(jnp.int32, (samples, chunk), 0) * FEAT
    for start in range(0, goals_ref.shape[1], chunk):
        line = goals_ref[:, start : start + chunk]
        nth = (jnp.broadcast_to(line, (samples, chunk)) - first_bag).astype(jnp.int16)
        for f in range(FEAT):
            place_ref[f * samples : (f + 1) * samples, start : start + chunk] = ones_where(
                nth == jnp.asarray(f, jnp.int16)
            )
    features = [slice(f * emb, (f + 1) * emb) for f in range(FEAT)]
    for f, part in enumerate(features):
        spot = slice(f * samples, (f + 1) * samples)
        wide_ref[:, part] = matmul(place_ref[spot, :], arrived_ref[...]).astype(jnp.bfloat16)
    hidden = matmul(wide_ref[...], down_ref[...]).astype(jnp.bfloat16)
    summed = jnp.zeros((samples, emb), jnp.float32)
    for part in features:
        shifted = rows_dot(hidden, up_ref[part, :]) + bias_ref[:, part]
        shifted_ref[:, part] = shifted
        feats = wide_ref[:, part].astype(jnp.float32)
        summed = summed + (feats * shifted + feats) * weight_ref[:, part].astype(jnp.float32)
    logits = jnp.sum(summed, axis=1, keepdims=True)
    logits_ref[...] = as_line(logits)
    dlogit = LOSS_SCALE * (jax.nn.sigmoid(logits) - as_column(target_ref[...]))
    for part in features:
        dmixed = dlogit * weight_ref[:, part].astype(jnp.float32)
        feats = wide_ref[:, part].astype(jnp.float32)
        dcross_ref[:, part] = (dmixed * feats).astype(jnp.bfloat16)
    dhidden = matmul(dcross_ref[...], up_ref[...]).astype(jnp.bfloat16)
    for f, part in enumerate(features):
        dmixed = dlogit * weight_ref[:, part].astype(jnp.float32)
        back_term = rows_dot(dhidden, down_ref[part, :])
        grads = dmixed * (shifted_ref[:, part] + 1.0) + back_term
        grads_ref[f * samples : (f + 1) * samples, :] = grads.astype(jnp.bfloat16)
    for step in range(FEAT):
        into_half = swap_ref[0] if step * emb < half else 1 - swap_ref[0]
        spot = (step * emb) % half
        part = pl.ds(pl.multiple_of(into_half * half + spot, emb), emb)
        out_ref = kept_ref if step * emb < half else sent_ref
        down_term = transposed_dot(wide_ref[:, part], dhidden)
        up_term = transposed_dot(dcross_ref[:, part], hidden)
        out_ref[spot : spot + emb, :rank] = down_term.astype(jnp.bfloat16)
        out_ref[spot : spot + emb, rank:] = up_term.astype(jnp.bfloat16)


def dense_step(swap, goals, arrived, down_full, up_full, bias, weight, target):
    samples = target.shape[0]
    slots, emb = arrived.shape
    width, rank = down_full.shape
    flops = 2 * slots * samples * width + 12 * samples * width * rank
    logits, grads, kept, sent = kernel_call(
        dense_kernel,
        (
            jax.ShapeDtypeStruct((1, samples), jnp.float32),
            jax.ShapeDtypeStruct((samples * FEAT, emb), jnp.bfloat16),
            jax.ShapeDtypeStruct((width // 2, 2 * rank), jnp.bfloat16),
            jax.ShapeDtypeStruct((width // 2, 2 * rank), jnp.bfloat16),
        ),
        (flops, 2 * arrived.size + 8 * width * rank),
        [
            pltpu.VMEM((samples * FEAT, slots), jnp.bfloat16),
            pltpu.VMEM((samples, width), jnp.bfloat16),
            pltpu.VMEM((samples, width), jnp.bfloat16),
            pltpu.VMEM((samples, width), jnp.float32),
        ],
        flags=1,
        operands=7,
        room=20,
    )(
        swap,
        goals.reshape(1, slots),
        bias.reshape(1, width),
        weight.reshape(1, width),
        target.reshape(1, samples),
        arrived,
        down_full,
        up_full,
    )
    return logits.reshape(samples), grads, kept, sent


def spread_kernel(count, scale, aliased, spots_ref, *refs):
    piece_refs = refs[:count]
    down_out_ref, up_out_ref, down_ref, up_ref, sems = refs[count + aliased :]
    rows = piece_refs[0].shape[0]
    rank = down_ref.shape[1]
    stores = []
    for i, piece_ref in enumerate(piece_refs):
        here = slice(i * rows, (i + 1) * rows)
        spot = pl.ds(pl.multiple_of(spots_ref[i] * rows, rows), rows)
        for half, (from_ref, to_ref) in enumerate(((down_ref, down_out_ref), (up_ref, up_out_ref))):
            part = slice(half * rank, (half + 1) * rank)
            from_ref[here, :] = piece_ref[:, part].astype(jnp.float32) * scale
            stores.append(
                pltpu.make_async_copy(from_ref.at[here, :], to_ref.at[spot, :], sems.at[len(stores)])
            )
            stores[-1].start()
    for store in stores:
        store.wait()


def spread_pieces(pieces, scale, rows, given=()):
    count = len(pieces)
    spots = jnp.stack([spot for spot, _ in pieces]).astype(jnp.int32)
    arrays = [piece for _, piece in pieces]
    step, both = arrays[0].shape
    rank = both // 2
    shape = jax.ShapeDtypeStruct((rows, rank), jnp.float32)
    block = pltpu.VMEM((count * step, rank), jnp.float32)
    return kernel_call(
        functools.partial(spread_kernel, count, scale, len(given)),
        (shape, shape),
        (count * step * both, 6 * count * step * both),
        [block, block, pltpu.SemaphoreType.DMA((2 * count,))],
        flags=1,
        operands=count,
        left=len(given),
        left_out=(0, 1),
        aliases={1 + count + i: i for i in range(len(given))},
    )(spots, *arrays, *given)


def update_kernel(rows_ref, far_ref, accum_ref, *refs):
    near_refs = refs[:-2]
    rows_out_ref, accum_out_ref = refs[-2:]
    emb = rows_ref.shape[1]
    for chunk in range(accum_ref.shape[0]):
        part = slice(chunk * SLOTS, (chunk + 1) * SLOTS)
        row_grad = far_ref[part, :].astype(jnp.float32)
        for near_ref in near_refs:
            row_grad = row_grad + near_ref[part, :emb].astype(jnp.float32)
        squares = jnp.mean(row_grad * row_grad, axis=1, keepdims=True)
        accum = as_column(accum_ref[chunk : chunk + 1, :]) + squares
        step = LEARN_RATE * row_grad * lax.rsqrt(accum + ADA_EPS)
        rows_out_ref[part, :] = (rows_ref[part, :].astype(jnp.float32) - step).astype(jnp.bfloat16)
        accum_out_ref[chunk : chunk + 1, :] = as_line(accum)


def update_rows(rows, far, accum, nears):
    share, emb = rows.shape
    chunks = share // SLOTS
    new_rows, new_accum = kernel_call(
        update_kernel,
        (
            jax.ShapeDtypeStruct((share, emb), jnp.bfloat16),
            jax.ShapeDtypeStruct((chunks, SLOTS), jnp.float32),
        ),
        (8 * rows.size, 8 * rows.size),
        operands=3 + len(nears),
    )(rows, far, accum.reshape(chunks, SLOTS), *nears)
    return new_rows, new_accum.reshape(share)


def join_kernel(swap_ref, mine_ref, other_ref, out_ref, sems):
    half = mine_ref.shape[0]
    copies = []
    for i, (from_ref, at) in enumerate(((mine_ref, swap_ref[0]), (other_ref, 1 - swap_ref[0]))):
        spot = pl.ds(pl.multiple_of(at * half, half), half)
        copies.append(pltpu.make_async_copy(from_ref, out_ref.at[spot, :], sems.at[i]))
        copies[-1].start()
    for copy in copies:
        copy.wait()


def join_halves(swap, mine, other):
    return kernel_call(
        join_kernel,
        jax.ShapeDtypeStruct((2 * mine.shape[0], mine.shape[1]), mine.dtype),
        (0, 8 * mine.size),
        [pltpu.SemaphoreType.DMA((2,))],
        flags=1,
        operands=2,
        left_out=(0,),
    )(swap, mine, other)


def group_levels(size):
    levels = []
    stride = 1
    while size % 4 == 0:
        levels.append((stride, 4))
        stride, size = stride * 4, size // 4
    if size > 1:
        levels.append((stride, size))
    return levels


def partner_index(index, stride, group, step):
    place = (index // stride) % group
    if group & (group - 1) == 0:
        other = place ^ step
    else:
        other = (place + step) % group
    return index + (other - place) * stride


def sent_from(axis, stride, group, step):
    size = lax.axis_size(axis)
    return [(partner_index(i, stride, group, step), i) for i in range(size)]


def scattered_pieces(blocks, axis, level):
    stride, group = level
    rows = blocks.shape[0] // group
    place = (lax.axis_index(axis) // stride) % group
    pieces = [lax.dynamic_slice_in_dim(blocks, place * rows, rows, 0)]
    for step in range(1, group):
        pairs = sent_from(axis, stride, group, step)
        if group & (group - 1) == 0:
            goal = place ^ step
        else:
            goal = (place + group - step) % group
        outgoing = lax.dynamic_slice_in_dim(blocks, goal * rows, rows, 0)
        pieces.append(lax.ppermute(outgoing, axis, pairs))
    return pieces


def summed(pieces):
    total = pieces[0].astype(jnp.float32)
    for piece in pieces[1:]:
        total = total + piece.astype(jnp.float32)
    return total.astype(jnp.bfloat16)


def scatter_sum(blocks, axis, levels):
    for level in levels:
        blocks = summed(scattered_pieces(blocks, axis, level))
    return blocks


def gathered_pieces(block, axis, level):
    stride, group = level
    index = lax.axis_index(axis)
    pieces = [((index // stride) % group, block)]
    for step in range(1, group):
        origin = partner_index(index, stride, group, step)
        came = lax.ppermute(block, axis, sent_from(axis, stride, group, step))
        pieces.append(((origin // stride) % group, came))
    return pieces


def gather_blocks(block, axis, levels):
    for level in reversed(levels):
        rows = block.shape[0]
        pieces = gathered_pieces(block, axis, level)
        block = jnp.zeros((len(pieces) * rows,) + block.shape[1:], block.dtype)
        for place, piece in pieces:
            block = lax.dynamic_update_slice_in_dim(block, piece, place * rows, 0)
    return block


def local(
    table_rows, accum, factor_down, factor_up, cross_bias, out_weight, target, bag_rows, slot_target
):
    tables = lax.axis_size("table")
    narrows = lax.axis_size("narrow")
    row_dev, emb_width = table_rows.shape
    pools_per = slot_target.shape[1]
    samples = target.shape[0]
    bag_count = samples * FEAT
    slot_count = tables * pools_per
    narrow_levels = group_levels(narrows)
    table_index = lax.axis_index("table")
    narrow_index = lax.axis_index("narrow")
    near_count = tables // 2
    half_levels = group_levels(near_count)
    far_half = table_index // near_count
    halves = [list(range(near_count)), list(range(near_count, tables))]
    across = [(i, (i + near_count) % tables) for i in range(tables)]
    paired = narrows == 2
    swap = (narrow_index if paired else narrow_index * 0).reshape(1)

    def near_and_far(rows):
        return tuple(
            lax.dynamic_slice_in_dim(rows, half * near_count, near_count, 0)
            for half in (far_half, 1 - far_half)
        )

    def in_order(near, far):
        return jnp.where(
            far_half == 0, jnp.concatenate([near, far]), jnp.concatenate([far, near])
        )

    def narrow_whole(block):
        if not paired:
            return gather_blocks(block, "narrow", narrow_levels)
        came = lax.ppermute(block, "narrow", sent_from("narrow", 1, 2, 1))
        first = jnp.where(narrow_index == 0, block, came)
        second = jnp.where(narrow_index == 0, came, block)
        return jnp.concatenate([first, second], axis=0)

    share_rows = row_dev // narrows
    own_share = lax.dynamic_slice_in_dim(table_rows, narrow_index * share_rows, share_rows, 0)
    far_share = lax.ppermute(own_share, "table", across)
    down_full = narrow_whole(factor_down)
    up_full = narrow_whole(factor_up)

    per_window = bag_rows.shape[1]
    asked = jnp.concatenate(near_and_far(bag_rows), axis=1)[:, None, :]
    asked = lax.all_to_all(
        asked, "table", split_axis=0, concat_axis=0, tiled=True, axis_index_groups=halves
    )
    near_ids, far_ids = asked[:, 0, :per_window], asked[:, 0, per_window:]
    if per_window != SLOTS * HOT:
        by_block = (ids.reshape(-1, SLOTS * HOT) for ids in (near_ids, far_ids))
        asked = jnp.concatenate(tuple(by_block), axis=1)
    sums = pool_lookups(0, asked, table_rows, pools_per)
    sums, far_share = lax.optimization_barrier((sums, far_share))
    sums = pool_lookups(1, asked, narrow_whole(far_share), pools_per, (sums,))
    arrived = lax.all_to_all(
        sums, "table", split_axis=0, concat_axis=0, tiled=True, axis_index_groups=halves
    )
    goals = jnp.stack(near_and_far(slot_target), axis=1)
    arrived, down_full, up_full, goals = lax.optimization_barrier(
        (arrived, down_full, up_full, goals)
    )
    logits, bag_grads, kept, sent = dense_step(
        swap,
        goals,
        arrived.reshape(slot_count, emb_width),
        down_full,
        up_full,
        cross_bias,
        out_weight,
        target,
    )
    if paired:
        came = lax.ppermute(sent, "narrow", sent_from("narrow", 1, 2, 1))
        narrow_sum = (kept.astype(jnp.float32) + came.astype(jnp.float32)).astype(jnp.bfloat16)
    else:
        narrow_sum = scatter_sum(jnp.concatenate([kept, sent], axis=0), "narrow", narrow_levels)
    slot_grads = return_grads(goals, bag_grads)
    groups = [group for _, group in half_levels]
    share_terms = narrow_sum.reshape(*groups, -1, narrow_sum.shape[1])
    order = list(range(len(groups)))[::-1] + [len(groups), len(groups) + 1]
    share_terms = share_terms.transpose(order).reshape(near_count, -1, narrow_sum.shape[1])
    rank = factor_down.shape[1]
    outgoing = [slot_grads.reshape(near_count, 2 * pools_per, emb_width)]
    outgoing += [share_terms[:, :, :rank], share_terms[:, :, rank:]]
    returned = lax.all_to_all(
        jnp.concatenate(outgoing, axis=1),
        "table",
        split_axis=0,
        concat_axis=0,
        tiled=True,
        axis_index_groups=halves,
    )
    terms = jnp.sum(returned[:, 2 * pools_per :].astype(jnp.float32), axis=0)
    half_sum = jnp.concatenate(jnp.split(terms, 2, axis=0), axis=1).astype(jnp.bfloat16)
    other_sum = lax.ppermute(half_sum, "table", across)
    mine, passed = row_grads(swap, asked, returned, pools_per, row_dev)
    other_sum, mine, passed = lax.optimization_barrier((other_sum, mine, passed))
    table_sum = summed([half_sum, other_sum])
    if paired:
        nears = [mine, lax.ppermute(passed, "narrow", sent_from("narrow", 1, 2, 1))]
    else:
        nears = [scatter_sum(jnp.concatenate([mine, passed], axis=0), "narrow", narrow_levels)]
    far_term = summed([term[:, emb_width:] for term in nears])
    level_sum = gather_blocks(table_sum, "table", half_levels[1:])
    pieces = gathered_pieces(level_sum, "table", half_levels[0])
    far_term = lax.ppermute(far_term, "table", across)
    own_accum = lax.dynamic_slice_in_dim(accum, narrow_index * share_rows, share_rows, 0)
    new_share, new_accum = update_rows(own_share, far_term, own_accum, nears)
    if paired:
        other_share = lax.ppermute(new_share, "narrow", sent_from("narrow", 1, 2, 1))
        new_rows = join_halves(swap, new_share, other_share)
    else:
        new_rows = gather_blocks(new_share, "narrow", narrow_levels)
    scale = 1.0 / math.sqrt(samples * tables * narrows)
    spot, last = pieces[-1]
    grads = spread_pieces(pieces[:-1], scale, factor_down.shape[0])
    last, *grads = lax.optimization_barrier((last, *grads))
    down_grad, up_grad = spread_pieces([(spot, last)], scale, factor_down.shape[0], grads)
    return (logits, down_grad, up_grad, new_rows, new_accum)


def solution(mesh):
    in_specs = (
        P("table", None),
        P("table"),
        P("narrow", None),
        P("narrow", None),
        P(),
        P(),
        P(("table", "narrow")),
        P(("table", "narrow"), None),
        P(("table", "narrow"), None),
    )
    out_specs = (
        P(("table", "narrow")),
        P("narrow", None),
        P("narrow", None),
        P("table", None),
        P(("table", "narrow")),
    )
    return jax.shard_map(local, mesh=mesh, in_specs=in_specs, out_specs=out_specs, check_vma=False)
```

```python
import functools
import math

import jax
import jax.numpy as jnp
from jax import lax
from jax.experimental import pallas as pl
from jax.experimental.pallas import tpu as pltpu
from jax.sharding import PartitionSpec as P

FEAT = 8
HOT = 4


LEARN_RATE = 0.2
LOSS_SCALE = 32.0
ADA_EPS = 1e-06


SLOTS = 128
MIB = 1024 * 1024


def matmul(left, right):
    return jnp.dot(left, right, preferred_element_type=jnp.float32)


def transposed_dot(left, right):
    return lax.dot_general(
        left, right, (((0,), (0,)), ((), ())), preferred_element_type=jnp.float32
    )


def rows_dot(left, right):
    return lax.dot_general(
        left, right, (((1,), (1,)), ((), ())), preferred_element_type=jnp.float32
    )


def kernel_call(
    kernel, out_shape, cost, scratch=(), flags=0, operands=0, left=0, left_out=(), aliases=None, room=8
):
    flops, moved = cost
    smem = pl.BlockSpec(memory_space=pltpu.SMEM)
    vmem = pl.BlockSpec(memory_space=pltpu.VMEM)
    hbm = pl.BlockSpec(memory_space=pltpu.HBM)
    if isinstance(out_shape, tuple):
        out_specs = tuple(hbm if i in left_out else vmem for i in range(len(out_shape)))
    else:
        out_specs = hbm if left_out else vmem
    return pl.pallas_call(
        kernel,
        in_specs=[smem] * flags + [vmem] * operands + [hbm] * left,
        out_specs=out_specs,
        input_output_aliases=aliases or {},
        out_shape=out_shape,
        scratch_shapes=scratch,
        compiler_params=pltpu.CompilerParams(vmem_limit_bytes=room * MIB),
        cost_estimate=pl.CostEstimate(flops=flops, bytes_accessed=moved, transcendentals=0),
    )


def split_ids(ids):
    shifted = ids + 1
    high = lax.shift_right_logical(shifted, 5).astype(jnp.float32).astype(jnp.bfloat16)
    low = (shifted & 31).astype(jnp.float32).astype(jnp.bfloat16)
    return high, low


def lookup_choice():
    shape = (HOT * SLOTS, HOT * SLOTS)
    row = lax.broadcasted_iota(jnp.int32, shape, 0)
    column = lax.broadcasted_iota(jnp.int32, shape, 1)
    wanted = (row & (SLOTS - 1)) * HOT + lax.shift_right_logical(row, 7)
    return jnp.where(wanted == column, 1.0, 0.0).astype(jnp.bfloat16)


def joined(digits):
    high, low = digits
    return (high * 32.0 + low - 1.0).astype(jnp.int32)


def ones_where(mask):
    return jnp.where(mask, jnp.asarray(1, jnp.bfloat16), jnp.asarray(0, jnp.bfloat16))


def pool_kernel(part, swap_ref, ids_ref, first_ref, second_ref, *refs):
    out_ref, counts_ref, sums_ref, sem = refs[-4:]
    slots = counts_ref.shape[0]
    sources, _, pools, _ = out_ref.shape
    per_block = HOT * SLOTS
    if len(ids_ref.shape) == 3:
        ids = ids_ref[:, 0, part * per_block : (part + 1) * per_block]
    else:
        ids = ids_ref[:, part * per_block : (part + 1) * per_block]
    choice = lookup_choice()
    high, low = split_ids(ids)
    columns = joined((rows_dot(choice, high), rows_dot(choice, low))).astype(jnp.int16)
    half = first_ref.shape[0]
    position = lax.broadcasted_iota(jnp.int32, (SLOTS, 2 * half), 1) + swap_ref[0] * half
    position = jnp.where(position >= 2 * half, position - 2 * half, position).astype(jnp.int16)
    for block in range(slots // SLOTS):
        counts = None
        for lookup in range(HOT):
            column = columns[lookup * SLOTS : (lookup + 1) * SLOTS, block : block + 1]
            found = ones_where(column == position)
            counts = found if counts is None else counts + found
        counts_ref[block * SLOTS : (block + 1) * SLOTS, :] = counts
    sums = matmul(counts_ref[:, :half], first_ref[...])
    sums = (sums + matmul(counts_ref[:, half:], second_ref[...])).astype(jnp.bfloat16)
    for source in range(sources):
        sums_ref[source] = sums[source * pools : (source + 1) * pools]
    store = pltpu.make_async_copy(sums_ref, out_ref.at[:, part], sem)
    store.start()
    store.wait()


def pool_lookups(part, swap, ids, halves, pools, given=()):
    slots = ids.shape[0] * SLOTS
    row_dev, width = 2 * halves[0].shape[0], halves[0].shape[1]
    return kernel_call(
        functools.partial(pool_kernel, part),
        jax.ShapeDtypeStruct((slots // pools, 2, pools, width), jnp.bfloat16),
        (2 * slots * row_dev * width, 2 * row_dev * width + 2 * slots * width),
        [
            pltpu.VMEM((slots, row_dev), jnp.bfloat16),
            pltpu.VMEM((slots // pools, pools, width), jnp.bfloat16),
            pltpu.SemaphoreType.DMA,
        ],
        flags=1,
        operands=3,
        left=len(given),
        left_out=(0,),
        aliases={4: 0} if given else None,
        room=12,
    )(swap, ids, *halves, *given)


def row_grad_kernel(swap_ref, ids_ref, grads_ref, kept_ref, sent_ref, counts_ref, sums_ref):
    sources, _, emb = grads_ref.shape
    row_dev, slots = counts_ref.shape
    pools = slots // sources
    half = row_dev // 2
    per_block = HOT * SLOTS
    tile = 64
    choice = lookup_choice()
    position = lax.broadcasted_iota(jnp.int32, (tile, SLOTS), 0).astype(jnp.int16)
    for part in range(2):
        lanes = slice(part * per_block, (part + 1) * per_block)
        ids = ids_ref[:, 0, lanes] if len(ids_ref.shape) == 3 else ids_ref[:, lanes]
        high, low = split_ids(ids)
        lines = joined((rows_dot(high, choice), rows_dot(low, choice)))
        for block in range(slots // SLOTS):
            spread = []
            for lookup in range(HOT):
                line = lines[block : block + 1, lookup * SLOTS : (lookup + 1) * SLOTS]
                spread.append(jnp.broadcast_to(line, (tile, SLOTS)).astype(jnp.int16))
            for start in range(0, row_dev, tile):
                counts = None
                for lookup in range(HOT):
                    found = ones_where(spread[lookup] - jnp.asarray(start, jnp.int16) == position)
                    counts = found if counts is None else counts + found
                counts_ref[start : start + tile, block * SLOTS : (block + 1) * SLOTS] = counts
        grads = grads_ref[:, part * pools : (part + 1) * pools].reshape(slots, emb)
        where = slice(part * emb, (part + 1) * emb)
        sums_ref[:, where] = matmul(counts_ref[...], grads).astype(jnp.bfloat16)
    for out_ref, into_half in ((kept_ref, swap_ref[0]), (sent_ref, 1 - swap_ref[0])):
        out_ref[...] = sums_ref[pl.ds(pl.multiple_of(into_half * half, half), half), :]


def row_grads(swap, ids, slot_grads, pools, row_dev):
    sources, _, emb = slot_grads.shape
    slots = sources * pools
    half = jax.ShapeDtypeStruct((row_dev // 2, 2 * emb), jnp.bfloat16)
    return kernel_call(
        row_grad_kernel,
        (half, half),
        (4 * row_dev * slots * emb, 2 * slot_grads.size + 4 * row_dev * emb),
        [
            pltpu.VMEM((row_dev, slots), jnp.bfloat16),
            pltpu.VMEM((row_dev, 2 * emb), jnp.bfloat16),
        ],
        flags=1,
        operands=2,
        room=12,
    )(swap, ids, slot_grads)


def diagonal(size):
    row = lax.broadcasted_iota(jnp.int32, (size, size), 0)
    return row == lax.broadcasted_iota(jnp.int32, (size, size), 1)


def as_column(line):
    return jnp.sum(jnp.where(diagonal(line.shape[1]), line, 0.0), axis=1, keepdims=True)


def as_line(column):
    return jnp.sum(jnp.where(diagonal(column.shape[0]), column, 0.0), axis=0, keepdims=True)


def return_kernel(goals_ref, grads_ref, out_ref, pick_ref):
    blocks = goals_ref.shape[0]
    bags = grads_ref.shape[0]
    samples = bags // FEAT
    high, low = split_ids(goals_ref[...])
    unit = ones_where(diagonal(SLOTS))
    columns = joined((rows_dot(unit, high), rows_dot(unit, low))).astype(jnp.int16)
    place = lax.broadcasted_iota(jnp.int32, (SLOTS, bags), 1)
    order = ((place % samples) * FEAT + place // samples).astype(jnp.int16)
    for block in range(blocks):
        pick_ref[block * SLOTS : (block + 1) * SLOTS, :] = ones_where(
            columns[:, block : block + 1] == order
        )
    out_ref[...] = matmul(pick_ref[...], grads_ref[...]).astype(jnp.bfloat16)


def return_grads(goals, grads):
    bags, emb = grads.shape
    slot_count = goals.size
    return kernel_call(
        return_kernel,
        jax.ShapeDtypeStruct((slot_count, emb), jnp.bfloat16),
        (2 * slot_count * bags * emb, 2 * grads.size + 2 * slot_count * emb),
        [pltpu.VMEM((slot_count, bags), jnp.bfloat16)],
        operands=2,
        room=12,
    )(goals.reshape(slot_count // SLOTS, SLOTS), grads)


def dense_kernel(
    swap_ref,
    goals_ref,
    bias_ref,
    weight_ref,
    target_ref,
    arrived_ref,
    down_ref,
    up_ref,
    logits_ref,
    grads_ref,
    kept_ref,
    sent_ref,
    place_ref,
    wide_ref,
    dcross_ref,
    shifted_ref,
):
    samples = target_ref.shape[1]
    width, rank = down_ref.shape
    emb = width // FEAT
    half = width // 2
    chunk = 512
    first_bag = lax.broadcasted_iota(jnp.int32, (samples, chunk), 0) * FEAT
    for start in range(0, goals_ref.shape[1], chunk):
        line = goals_ref[:, start : start + chunk]
        nth = (jnp.broadcast_to(line, (samples, chunk)) - first_bag).astype(jnp.int16)
        for f in range(FEAT):
            place_ref[f * samples : (f + 1) * samples, start : start + chunk] = ones_where(
                nth == jnp.asarray(f, jnp.int16)
            )
    features = [slice(f * emb, (f + 1) * emb) for f in range(FEAT)]
    for f, part in enumerate(features):
        spot = slice(f * samples, (f + 1) * samples)
        wide_ref[:, part] = matmul(place_ref[spot, :], arrived_ref[...]).astype(jnp.bfloat16)
    hidden = matmul(wide_ref[...], down_ref[...]).astype(jnp.bfloat16)
    summed = jnp.zeros((samples, emb), jnp.float32)
    for part in features:
        shifted = rows_dot(hidden, up_ref[part, :]) + bias_ref[:, part]
        shifted_ref[:, part] = shifted
        feats = wide_ref[:, part].astype(jnp.float32)
        summed = summed + (feats * shifted + feats) * weight_ref[:, part].astype(jnp.float32)
    logits = jnp.sum(summed, axis=1, keepdims=True)
    logits_ref[...] = as_line(logits)
    dlogit = LOSS_SCALE * (jax.nn.sigmoid(logits) - as_column(target_ref[...]))
    for part in features:
        dmixed = dlogit * weight_ref[:, part].astype(jnp.float32)
        feats = wide_ref[:, part].astype(jnp.float32)
        dcross_ref[:, part] = (dmixed * feats).astype(jnp.bfloat16)
    dhidden = matmul(dcross_ref[...], up_ref[...]).astype(jnp.bfloat16)
    for f, part in enumerate(features):
        dmixed = dlogit * weight_ref[:, part].astype(jnp.float32)
        back_term = rows_dot(dhidden, down_ref[part, :])
        grads = dmixed * (shifted_ref[:, part] + 1.0) + back_term
        grads_ref[f * samples : (f + 1) * samples, :] = grads.astype(jnp.bfloat16)
    for step in range(FEAT):
        into_half = swap_ref[0] if step * emb < half else 1 - swap_ref[0]
        spot = (step * emb) % half
        part = pl.ds(pl.multiple_of(into_half * half + spot, emb), emb)
        out_ref = kept_ref if step * emb < half else sent_ref
        down_term = transposed_dot(wide_ref[:, part], dhidden)
        up_term = transposed_dot(dcross_ref[:, part], hidden)
        out_ref[spot : spot + emb, :rank] = down_term.astype(jnp.bfloat16)
        out_ref[spot : spot + emb, rank:] = up_term.astype(jnp.bfloat16)


def dense_step(swap, goals, arrived, down_full, up_full, bias, weight, target):
    samples = target.shape[0]
    slots, emb = arrived.shape
    width, rank = down_full.shape
    flops = 2 * slots * samples * width + 12 * samples * width * rank
    logits, grads, kept, sent = kernel_call(
        dense_kernel,
        (
            jax.ShapeDtypeStruct((1, samples), jnp.float32),
            jax.ShapeDtypeStruct((samples * FEAT, emb), jnp.bfloat16),
            jax.ShapeDtypeStruct((width // 2, 2 * rank), jnp.bfloat16),
            jax.ShapeDtypeStruct((width // 2, 2 * rank), jnp.bfloat16),
        ),
        (flops, 2 * arrived.size + 8 * width * rank),
        [
            pltpu.VMEM((samples * FEAT, slots), jnp.bfloat16),
            pltpu.VMEM((samples, width), jnp.bfloat16),
            pltpu.VMEM((samples, width), jnp.bfloat16),
            pltpu.VMEM((samples, width), jnp.float32),
        ],
        flags=1,
        operands=7,
        room=20,
    )(
        swap,
        goals.reshape(1, slots),
        bias.reshape(1, width),
        weight.reshape(1, width),
        target.reshape(1, samples),
        arrived,
        down_full,
        up_full,
    )
    return logits.reshape(samples), grads, kept, sent


def spread_kernel(count, scale, aliased, spots_ref, *refs):
    piece_refs = refs[:count]
    down_out_ref, up_out_ref, down_ref, up_ref, sems = refs[count + aliased :]
    rows = piece_refs[0].shape[0]
    rank = down_ref.shape[1]
    stores = []
    for i, piece_ref in enumerate(piece_refs):
        here = slice(i * rows, (i + 1) * rows)
        spot = pl.ds(pl.multiple_of(spots_ref[i] * rows, rows), rows)
        for half, (from_ref, to_ref) in enumerate(((down_ref, down_out_ref), (up_ref, up_out_ref))):
            part = slice(half * rank, (half + 1) * rank)
            from_ref[here, :] = piece_ref[:, part].astype(jnp.float32) * scale
            stores.append(
                pltpu.make_async_copy(from_ref.at[here, :], to_ref.at[spot, :], sems.at[len(stores)])
            )
            stores[-1].start()
    for store in stores:
        store.wait()


def spread_pieces(pieces, scale, rows, given=()):
    count = len(pieces)
    spots = jnp.stack([spot for spot, _ in pieces]).astype(jnp.int32)
    arrays = [piece for _, piece in pieces]
    step, both = arrays[0].shape
    rank = both // 2
    shape = jax.ShapeDtypeStruct((rows, rank), jnp.float32)
    block = pltpu.VMEM((count * step, rank), jnp.float32)
    return kernel_call(
        functools.partial(spread_kernel, count, scale, len(given)),
        (shape, shape),
        (count * step * both, 6 * count * step * both),
        [block, block, pltpu.SemaphoreType.DMA((2 * count,))],
        flags=1,
        operands=count,
        left=len(given),
        left_out=(0, 1),
        aliases={1 + count + i: i for i in range(len(given))},
    )(spots, *arrays, *given)


def update_kernel(rows_ref, far_ref, accum_ref, *refs):
    near_refs = refs[:-2]
    rows_out_ref, accum_out_ref = refs[-2:]
    emb = rows_ref.shape[1]
    for chunk in range(accum_ref.shape[0]):
        part = slice(chunk * SLOTS, (chunk + 1) * SLOTS)
        row_grad = far_ref[part, :].astype(jnp.float32)
        for near_ref in near_refs:
            row_grad = row_grad + near_ref[part, :emb].astype(jnp.float32)
        squares = jnp.mean(row_grad * row_grad, axis=1, keepdims=True)
        accum = as_column(accum_ref[chunk : chunk + 1, :]) + squares
        step = LEARN_RATE * row_grad * lax.rsqrt(accum + ADA_EPS)
        rows_out_ref[part, :] = (rows_ref[part, :].astype(jnp.float32) - step).astype(jnp.bfloat16)
        accum_out_ref[chunk : chunk + 1, :] = as_line(accum)


def update_rows(rows, far, accum, nears):
    share, emb = rows.shape
    chunks = share // SLOTS
    new_rows, new_accum = kernel_call(
        update_kernel,
        (
            jax.ShapeDtypeStruct((share, emb), jnp.bfloat16),
            jax.ShapeDtypeStruct((chunks, SLOTS), jnp.float32),
        ),
        (8 * rows.size, 8 * rows.size),
        operands=3 + len(nears),
    )(rows, far, accum.reshape(chunks, SLOTS), *nears)
    return new_rows, new_accum.reshape(share)


def join_kernel(swap_ref, mine_ref, other_ref, out_ref, sems):
    half = mine_ref.shape[0]
    copies = []
    for i, (from_ref, at) in enumerate(((mine_ref, swap_ref[0]), (other_ref, 1 - swap_ref[0]))):
        spot = pl.ds(pl.multiple_of(at * half, half), half)
        copies.append(pltpu.make_async_copy(from_ref, out_ref.at[spot, :], sems.at[i]))
        copies[-1].start()
    for copy in copies:
        copy.wait()


def join_halves(swap, mine, other):
    return kernel_call(
        join_kernel,
        jax.ShapeDtypeStruct((2 * mine.shape[0], mine.shape[1]), mine.dtype),
        (0, 8 * mine.size),
        [pltpu.SemaphoreType.DMA((2,))],
        flags=1,
        operands=2,
        left_out=(0,),
    )(swap, mine, other)


def group_levels(size):
    levels = []
    stride = 1
    while size % 4 == 0:
        levels.append((stride, 4))
        stride, size = stride * 4, size // 4
    if size > 1:
        levels.append((stride, size))
    return levels


def partner_index(index, stride, group, step):
    place = (index // stride) % group
    if group & (group - 1) == 0:
        other = place ^ step
    else:
        other = (place + step) % group
    return index + (other - place) * stride


def sent_from(axis, stride, group, step):
    size = lax.axis_size(axis)
    return [(partner_index(i, stride, group, step), i) for i in range(size)]


def scattered_pieces(blocks, axis, level):
    stride, group = level
    rows = blocks.shape[0] // group
    place = (lax.axis_index(axis) // stride) % group
    pieces = [lax.dynamic_slice_in_dim(blocks, place * rows, rows, 0)]
    for step in range(1, group):
        pairs = sent_from(axis, stride, group, step)
        if group & (group - 1) == 0:
            goal = place ^ step
        else:
            goal = (place + group - step) % group
        outgoing = lax.dynamic_slice_in_dim(blocks, goal * rows, rows, 0)
        pieces.append(lax.ppermute(outgoing, axis, pairs))
    return pieces


def summed(pieces):
    total = pieces[0].astype(jnp.float32)
    for piece in pieces[1:]:
        total = total + piece.astype(jnp.float32)
    return total.astype(jnp.bfloat16)


def scatter_sum(blocks, axis, levels):
    for level in levels:
        blocks = summed(scattered_pieces(blocks, axis, level))
    return blocks


def gathered_pieces(block, axis, level):
    stride, group = level
    index = lax.axis_index(axis)
    pieces = [((index // stride) % group, block)]
    for step in range(1, group):
        origin = partner_index(index, stride, group, step)
        came = lax.ppermute(block, axis, sent_from(axis, stride, group, step))
        pieces.append(((origin // stride) % group, came))
    return pieces


def gather_blocks(block, axis, levels):
    for level in reversed(levels):
        rows = block.shape[0]
        pieces = gathered_pieces(block, axis, level)
        block = jnp.zeros((len(pieces) * rows,) + block.shape[1:], block.dtype)
        for place, piece in pieces:
            block = lax.dynamic_update_slice_in_dim(block, piece, place * rows, 0)
    return block


def local(
    table_rows, accum, factor_down, factor_up, cross_bias, out_weight, target, bag_rows, slot_target
):
    tables = lax.axis_size("table")
    narrows = lax.axis_size("narrow")
    row_dev, emb_width = table_rows.shape
    pools_per = slot_target.shape[1]
    samples = target.shape[0]
    bag_count = samples * FEAT
    slot_count = tables * pools_per
    narrow_levels = group_levels(narrows)
    table_index = lax.axis_index("table")
    narrow_index = lax.axis_index("narrow")
    near_count = tables // 2
    half_levels = group_levels(near_count)
    far_half = table_index // near_count
    halves = [list(range(near_count)), list(range(near_count, tables))]
    across = [(i, (i + near_count) % tables) for i in range(tables)]
    paired = narrows == 2
    swap = (narrow_index if paired else narrow_index * 0).reshape(1)

    def near_and_far(rows):
        return tuple(
            lax.dynamic_slice_in_dim(rows, half * near_count, near_count, 0)
            for half in (far_half, 1 - far_half)
        )

    def in_order(near, far):
        return jnp.where(
            far_half == 0, jnp.concatenate([near, far]), jnp.concatenate([far, near])
        )

    def narrow_whole(block):
        if not paired:
            return gather_blocks(block, "narrow", narrow_levels)
        came = lax.ppermute(block, "narrow", sent_from("narrow", 1, 2, 1))
        first = jnp.where(narrow_index == 0, block, came)
        second = jnp.where(narrow_index == 0, came, block)
        return jnp.concatenate([first, second], axis=0)

    share_rows = row_dev // narrows
    own_halves = tuple(
        lax.dynamic_slice_in_dim(table_rows, half * (row_dev // 2), row_dev // 2, 0)
        for half in (swap[0], 1 - swap[0])
    )
    own_share = lax.dynamic_slice_in_dim(table_rows, narrow_index * share_rows, share_rows, 0)
    far_share = lax.ppermute(own_share, "table", across)
    down_full = narrow_whole(factor_down)
    up_full = narrow_whole(factor_up)

    per_window = bag_rows.shape[1]
    asked = jnp.concatenate(near_and_far(bag_rows), axis=1)[:, None, :]
    asked = lax.all_to_all(
        asked, "table", split_axis=0, concat_axis=0, tiled=True, axis_index_groups=halves
    )
    near_ids, far_ids = asked[:, 0, :per_window], asked[:, 0, per_window:]
    if per_window != SLOTS * HOT:
        by_block = (ids.reshape(-1, SLOTS * HOT) for ids in (near_ids, far_ids))
        asked = jnp.concatenate(tuple(by_block), axis=1)
    sums = pool_lookups(0, swap, asked, own_halves, pools_per)
    sums, far_share = lax.optimization_barrier((sums, far_share))
    if paired:
        came = lax.ppermute(far_share, "narrow", sent_from("narrow", 1, 2, 1))
        far_halves = (far_share, came)
    else:
        far_halves = tuple(jnp.split(narrow_whole(far_share), 2, axis=0))
    sums = pool_lookups(1, swap, asked, far_halves, pools_per, (sums,))
    arrived = lax.all_to_all(
        sums, "table", split_axis=0, concat_axis=0, tiled=True, axis_index_groups=halves
    )
    goals = jnp.stack(near_and_far(slot_target), axis=1)
    arrived, down_full, up_full, goals = lax.optimization_barrier(
        (arrived, down_full, up_full, goals)
    )
    logits, bag_grads, kept, sent = dense_step(
        swap,
        goals,
        arrived.reshape(slot_count, emb_width),
        down_full,
        up_full,
        cross_bias,
        out_weight,
        target,
    )
    if paired:
        came = lax.ppermute(sent, "narrow", sent_from("narrow", 1, 2, 1))
        narrow_sum = (kept.astype(jnp.float32) + came.astype(jnp.float32)).astype(jnp.bfloat16)
    else:
        narrow_sum = scatter_sum(jnp.concatenate([kept, sent], axis=0), "narrow", narrow_levels)
    slot_grads = return_grads(goals, bag_grads)
    groups = [group for _, group in half_levels]
    share_terms = narrow_sum.reshape(*groups, -1, narrow_sum.shape[1])
    order = list(range(len(groups)))[::-1] + [len(groups), len(groups) + 1]
    share_terms = share_terms.transpose(order).reshape(near_count, -1, narrow_sum.shape[1])
    rank = factor_down.shape[1]
    outgoing = [slot_grads.reshape(near_count, 2 * pools_per, emb_width)]
    outgoing += [share_terms[:, :, :rank], share_terms[:, :, rank:]]
    returned = lax.all_to_all(
        jnp.concatenate(outgoing, axis=1),
        "table",
        split_axis=0,
        concat_axis=0,
        tiled=True,
        axis_index_groups=halves,
    )
    terms = jnp.sum(returned[:, 2 * pools_per :].astype(jnp.float32), axis=0)
    half_sum = jnp.concatenate(jnp.split(terms, 2, axis=0), axis=1).astype(jnp.bfloat16)
    other_sum = lax.ppermute(half_sum, "table", across)
    mine, passed = row_grads(swap, asked, returned, pools_per, row_dev)
    other_sum, mine, passed = lax.optimization_barrier((other_sum, mine, passed))
    table_sum = summed([half_sum, other_sum])
    if paired:
        nears = [mine, lax.ppermute(passed, "narrow", sent_from("narrow", 1, 2, 1))]
    else:
        nears = [scatter_sum(jnp.concatenate([mine, passed], axis=0), "narrow", narrow_levels)]
    far_term = summed([term[:, emb_width:] for term in nears])
    inner = gather_blocks(table_sum, "table", half_levels[2:])
    blocks, fan = [(0, inner)], 1
    if len(half_levels) > 1:
        blocks, fan = gathered_pieces(inner, "table", half_levels[1]), half_levels[1][1]
    early, late = [], []
    for i, (place, block) in enumerate(blocks):
        pieces = gathered_pieces(block, "table", half_levels[0])
        pieces = [(spot * fan + place, piece) for spot, piece in pieces]
        early += pieces if i == 0 else pieces[:1]
        late += [] if i == 0 else pieces[1:]
    far_term = lax.ppermute(far_term, "table", across)
    spots, came = zip(*early, *late)
    far_term, *came = lax.optimization_barrier((far_term, *came))
    pieces = list(zip(spots, came))
    own_accum = lax.dynamic_slice_in_dim(accum, narrow_index * share_rows, share_rows, 0)
    new_share, new_accum = update_rows(own_share, far_term, own_accum, nears)
    if paired:
        other_share = lax.ppermute(new_share, "narrow", sent_from("narrow", 1, 2, 1))
        new_rows = join_halves(swap, new_share, other_share)
    else:
        new_rows = gather_blocks(new_share, "narrow", narrow_levels)
    scale = 1.0 / math.sqrt(samples * tables * narrows)
    down_grad, up_grad = spread_pieces(pieces, scale, factor_down.shape[0])
    return (logits, down_grad, up_grad, new_rows, new_accum)


def solution(mesh):
    in_specs = (
        P("table", None),
        P("table"),
        P("narrow", None),
        P("narrow", None),
        P(),
        P(),
        P(("table", "narrow")),
        P(("table", "narrow"), None),
        P(("table", "narrow"), None),
    )
    out_specs = (
        P(("table", "narrow")),
        P("narrow", None),
        P("narrow", None),
        P("table", None),
        P(("table", "narrow")),
    )
    return jax.shard_map(local, mesh=mesh, in_specs=in_specs, out_specs=out_specs, check_vma=False)
```

```python
import functools
import math

import jax
import jax.numpy as jnp
from jax import lax
from jax.experimental import pallas as pl
from jax.experimental.pallas import tpu as pltpu
from jax.sharding import PartitionSpec as P

FEAT = 8
HOT = 4


LEARN_RATE = 0.2
LOSS_SCALE = 32.0
ADA_EPS = 1e-06


SLOTS = 128
MIB = 1024 * 1024


def matmul(left, right):
    return jnp.dot(left, right, preferred_element_type=jnp.float32)


def transposed_dot(left, right):
    return lax.dot_general(
        left, right, (((0,), (0,)), ((), ())), preferred_element_type=jnp.float32
    )


def rows_dot(left, right):
    return lax.dot_general(
        left, right, (((1,), (1,)), ((), ())), preferred_element_type=jnp.float32
    )


def kernel_call(
    kernel, out_shape, cost, scratch=(), flags=0, operands=0, left=0, left_out=(), aliases=None, room=8
):
    flops, moved = cost
    smem = pl.BlockSpec(memory_space=pltpu.SMEM)
    vmem = pl.BlockSpec(memory_space=pltpu.VMEM)
    hbm = pl.BlockSpec(memory_space=pltpu.HBM)
    if isinstance(out_shape, tuple):
        out_specs = tuple(hbm if i in left_out else vmem for i in range(len(out_shape)))
    else:
        out_specs = hbm if left_out else vmem
    return pl.pallas_call(
        kernel,
        in_specs=[smem] * flags + [vmem] * operands + [hbm] * left,
        out_specs=out_specs,
        input_output_aliases=aliases or {},
        out_shape=out_shape,
        scratch_shapes=scratch,
        compiler_params=pltpu.CompilerParams(vmem_limit_bytes=room * MIB),
        cost_estimate=pl.CostEstimate(flops=flops, bytes_accessed=moved, transcendentals=0),
    )


def split_ids(ids):
    shifted = ids + 1
    high = lax.shift_right_logical(shifted, 5).astype(jnp.float32).astype(jnp.bfloat16)
    low = (shifted & 31).astype(jnp.float32).astype(jnp.bfloat16)
    return high, low


def lookup_choice():
    shape = (HOT * SLOTS, HOT * SLOTS)
    row = lax.broadcasted_iota(jnp.int32, shape, 0)
    column = lax.broadcasted_iota(jnp.int32, shape, 1)
    wanted = (row & (SLOTS - 1)) * HOT + lax.shift_right_logical(row, 7)
    return jnp.where(wanted == column, 1.0, 0.0).astype(jnp.bfloat16)


def joined(digits):
    high, low = digits
    return (high * 32.0 + low - 1.0).astype(jnp.int32)


def ones_where(mask):
    return jnp.where(mask, jnp.asarray(1, jnp.bfloat16), jnp.asarray(0, jnp.bfloat16))


def pool_kernel(part, swap_ref, ids_ref, first_ref, second_ref, *refs):
    out_ref, counts_ref, sums_ref, sem = refs[-4:]
    slots = counts_ref.shape[0]
    sources, _, pools, _ = out_ref.shape
    per_block = HOT * SLOTS
    if len(ids_ref.shape) == 3:
        ids = ids_ref[:, 0, part * per_block : (part + 1) * per_block]
    else:
        ids = ids_ref[:, part * per_block : (part + 1) * per_block]
    choice = lookup_choice()
    high, low = split_ids(ids)
    columns = joined((rows_dot(choice, high), rows_dot(choice, low))).astype(jnp.int16)
    half = first_ref.shape[0]
    position = lax.broadcasted_iota(jnp.int32, (SLOTS, 2 * half), 1) + swap_ref[0] * half
    position = jnp.where(position >= 2 * half, position - 2 * half, position).astype(jnp.int16)
    for block in range(slots // SLOTS):
        counts = None
        for lookup in range(HOT):
            column = columns[lookup * SLOTS : (lookup + 1) * SLOTS, block : block + 1]
            found = ones_where(column == position)
            counts = found if counts is None else counts + found
        counts_ref[block * SLOTS : (block + 1) * SLOTS, :] = counts
    sums = matmul(counts_ref[:, :half], first_ref[...])
    sums = (sums + matmul(counts_ref[:, half:], second_ref[...])).astype(jnp.bfloat16)
    for source in range(sources):
        sums_ref[source] = sums[source * pools : (source + 1) * pools]
    store = pltpu.make_async_copy(sums_ref, out_ref.at[:, part], sem)
    store.start()
    store.wait()


def pool_lookups(part, swap, ids, halves, pools, given=()):
    slots = ids.shape[0] * SLOTS
    row_dev, width = 2 * halves[0].shape[0], halves[0].shape[1]
    return kernel_call(
        functools.partial(pool_kernel, part),
        jax.ShapeDtypeStruct((slots // pools, 2, pools, width), jnp.bfloat16),
        (2 * slots * row_dev * width, 2 * row_dev * width + 2 * slots * width),
        [
            pltpu.VMEM((slots, row_dev), jnp.bfloat16),
            pltpu.VMEM((slots // pools, pools, width), jnp.bfloat16),
            pltpu.SemaphoreType.DMA,
        ],
        flags=1,
        operands=3,
        left=len(given),
        left_out=(0,),
        aliases={4: 0} if given else None,
        room=12,
    )(swap, ids, *halves, *given)


def row_grad_kernel(swap_ref, ids_ref, grads_ref, kept_ref, sent_ref, counts_ref, sums_ref):
    sources, _, emb = grads_ref.shape
    row_dev, slots = counts_ref.shape
    pools = slots // sources
    half = row_dev // 2
    per_block = HOT * SLOTS
    tile = 64
    choice = lookup_choice()
    position = lax.broadcasted_iota(jnp.int32, (tile, SLOTS), 0).astype(jnp.int16)
    for part in range(2):
        lanes = slice(part * per_block, (part + 1) * per_block)
        ids = ids_ref[:, 0, lanes] if len(ids_ref.shape) == 3 else ids_ref[:, lanes]
        high, low = split_ids(ids)
        lines = joined((rows_dot(high, choice), rows_dot(low, choice)))
        for block in range(slots // SLOTS):
            spread = []
            for lookup in range(HOT):
                line = lines[block : block + 1, lookup * SLOTS : (lookup + 1) * SLOTS]
                spread.append(jnp.broadcast_to(line, (tile, SLOTS)).astype(jnp.int16))
            for start in range(0, row_dev, tile):
                counts = None
                for lookup in range(HOT):
                    found = ones_where(spread[lookup] - jnp.asarray(start, jnp.int16) == position)
                    counts = found if counts is None else counts + found
                counts_ref[start : start + tile, block * SLOTS : (block + 1) * SLOTS] = counts
        grads = grads_ref[:, part * pools : (part + 1) * pools].reshape(slots, emb)
        where = slice(part * emb, (part + 1) * emb)
        sums_ref[:, where] = matmul(counts_ref[...], grads).astype(jnp.bfloat16)
    for out_ref, into_half in ((kept_ref, swap_ref[0]), (sent_ref, 1 - swap_ref[0])):
        out_ref[...] = sums_ref[pl.ds(pl.multiple_of(into_half * half, half), half), :]


def row_grads(swap, ids, slot_grads, pools, row_dev):
    sources, _, emb = slot_grads.shape
    slots = sources * pools
    half = jax.ShapeDtypeStruct((row_dev // 2, 2 * emb), jnp.bfloat16)
    return kernel_call(
        row_grad_kernel,
        (half, half),
        (4 * row_dev * slots * emb, 2 * slot_grads.size + 4 * row_dev * emb),
        [
            pltpu.VMEM((row_dev, slots), jnp.bfloat16),
            pltpu.VMEM((row_dev, 2 * emb), jnp.bfloat16),
        ],
        flags=1,
        operands=2,
        room=12,
    )(swap, ids, slot_grads)


def diagonal(size):
    row = lax.broadcasted_iota(jnp.int32, (size, size), 0)
    return row == lax.broadcasted_iota(jnp.int32, (size, size), 1)


def as_column(line):
    return jnp.sum(jnp.where(diagonal(line.shape[1]), line, 0.0), axis=1, keepdims=True)


def as_line(column):
    return jnp.sum(jnp.where(diagonal(column.shape[0]), column, 0.0), axis=0, keepdims=True)


def return_kernel(goals_ref, grads_ref, out_ref, pick_ref):
    blocks = goals_ref.shape[0]
    bags = grads_ref.shape[0]
    samples = bags // FEAT
    high, low = split_ids(goals_ref[...])
    unit = ones_where(diagonal(SLOTS))
    columns = joined((rows_dot(unit, high), rows_dot(unit, low))).astype(jnp.int16)
    place = lax.broadcasted_iota(jnp.int32, (SLOTS, bags), 1)
    order = ((place % samples) * FEAT + place // samples).astype(jnp.int16)
    for block in range(blocks):
        pick_ref[block * SLOTS : (block + 1) * SLOTS, :] = ones_where(
            columns[:, block : block + 1] == order
        )
    out_ref[...] = matmul(pick_ref[...], grads_ref[...]).astype(jnp.bfloat16)


def return_grads(goals, grads):
    bags, emb = grads.shape
    slot_count = goals.size
    return kernel_call(
        return_kernel,
        jax.ShapeDtypeStruct((slot_count, emb), jnp.bfloat16),
        (2 * slot_count * bags * emb, 2 * grads.size + 2 * slot_count * emb),
        [pltpu.VMEM((slot_count, bags), jnp.bfloat16)],
        operands=2,
        room=12,
    )(goals.reshape(slot_count // SLOTS, SLOTS), grads)


def dense_kernel(
    swap_ref,
    goals_ref,
    bias_ref,
    weight_ref,
    target_ref,
    arrived_ref,
    down_ref,
    up_ref,
    logits_ref,
    grads_ref,
    kept_ref,
    sent_ref,
    place_ref,
    wide_ref,
    dcross_ref,
    shifted_ref,
):
    samples = target_ref.shape[1]
    width, rank = down_ref.shape
    emb = width // FEAT
    half = width // 2
    chunk = 512
    first_bag = lax.broadcasted_iota(jnp.int32, (samples, chunk), 0) * FEAT
    for start in range(0, goals_ref.shape[1], chunk):
        line = goals_ref[:, start : start + chunk]
        nth = (jnp.broadcast_to(line, (samples, chunk)) - first_bag).astype(jnp.int16)
        for f in range(FEAT):
            place_ref[f * samples : (f + 1) * samples, start : start + chunk] = ones_where(
                nth == jnp.asarray(f, jnp.int16)
            )
    features = [slice(f * emb, (f + 1) * emb) for f in range(FEAT)]
    for f, part in enumerate(features):
        spot = slice(f * samples, (f + 1) * samples)
        wide_ref[:, part] = matmul(place_ref[spot, :], arrived_ref[...]).astype(jnp.bfloat16)
    hidden = matmul(wide_ref[...], down_ref[...]).astype(jnp.bfloat16)
    summed = jnp.zeros((samples, emb), jnp.float32)
    for part in features:
        shifted = rows_dot(hidden, up_ref[part, :]) + bias_ref[:, part]
        shifted_ref[:, part] = shifted
        feats = wide_ref[:, part].astype(jnp.float32)
        summed = summed + (feats * shifted + feats) * weight_ref[:, part].astype(jnp.float32)
    logits = jnp.sum(summed, axis=1, keepdims=True)
    logits_ref[...] = as_line(logits)
    dlogit = LOSS_SCALE * (jax.nn.sigmoid(logits) - as_column(target_ref[...]))
    for part in features:
        dmixed = dlogit * weight_ref[:, part].astype(jnp.float32)
        feats = wide_ref[:, part].astype(jnp.float32)
        dcross_ref[:, part] = (dmixed * feats).astype(jnp.bfloat16)
    dhidden = matmul(dcross_ref[...], up_ref[...]).astype(jnp.bfloat16)
    for f, part in enumerate(features):
        dmixed = dlogit * weight_ref[:, part].astype(jnp.float32)
        back_term = rows_dot(dhidden, down_ref[part, :])
        grads = dmixed * (shifted_ref[:, part] + 1.0) + back_term
        grads_ref[f * samples : (f + 1) * samples, :] = grads.astype(jnp.bfloat16)
    for step in range(FEAT):
        into_half = swap_ref[0] if step * emb < half else 1 - swap_ref[0]
        spot = (step * emb) % half
        part = pl.ds(pl.multiple_of(into_half * half + spot, emb), emb)
        out_ref = kept_ref if step * emb < half else sent_ref
        down_term = transposed_dot(wide_ref[:, part], dhidden)
        up_term = transposed_dot(dcross_ref[:, part], hidden)
        out_ref[spot : spot + emb, :rank] = down_term.astype(jnp.bfloat16)
        out_ref[spot : spot + emb, rank:] = up_term.astype(jnp.bfloat16)


def dense_step(swap, goals, arrived, down_full, up_full, bias, weight, target):
    samples = target.shape[0]
    slots, emb = arrived.shape
    width, rank = down_full.shape
    flops = 2 * slots * samples * width + 12 * samples * width * rank
    logits, grads, kept, sent = kernel_call(
        dense_kernel,
        (
            jax.ShapeDtypeStruct((1, samples), jnp.float32),
            jax.ShapeDtypeStruct((samples * FEAT, emb), jnp.bfloat16),
            jax.ShapeDtypeStruct((width // 2, 2 * rank), jnp.bfloat16),
            jax.ShapeDtypeStruct((width // 2, 2 * rank), jnp.bfloat16),
        ),
        (flops, 2 * arrived.size + 8 * width * rank),
        [
            pltpu.VMEM((samples * FEAT, slots), jnp.bfloat16),
            pltpu.VMEM((samples, width), jnp.bfloat16),
            pltpu.VMEM((samples, width), jnp.bfloat16),
            pltpu.VMEM((samples, width), jnp.float32),
        ],
        flags=1,
        operands=7,
        room=20,
    )(
        swap,
        goals.reshape(1, slots),
        bias.reshape(1, width),
        weight.reshape(1, width),
        target.reshape(1, samples),
        arrived,
        down_full,
        up_full,
    )
    return logits.reshape(samples), grads, kept, sent


def spread_kernel(count, scale, aliased, spots_ref, *refs):
    piece_refs = refs[:count]
    down_out_ref, up_out_ref, down_ref, up_ref, sems = refs[count + aliased :]
    rows = piece_refs[0].shape[0]
    rank = down_ref.shape[1]
    stores = []
    for i, piece_ref in enumerate(piece_refs):
        here = slice(i * rows, (i + 1) * rows)
        spot = pl.ds(pl.multiple_of(spots_ref[i] * rows, rows), rows)
        for half, (from_ref, to_ref) in enumerate(((down_ref, down_out_ref), (up_ref, up_out_ref))):
            part = slice(half * rank, (half + 1) * rank)
            from_ref[here, :] = piece_ref[:, part].astype(jnp.float32) * scale
            stores.append(
                pltpu.make_async_copy(from_ref.at[here, :], to_ref.at[spot, :], sems.at[len(stores)])
            )
            stores[-1].start()
    for store in stores:
        store.wait()


def spread_pieces(pieces, scale, rows, given=()):
    count = len(pieces)
    spots = jnp.stack([spot for spot, _ in pieces]).astype(jnp.int32)
    arrays = [piece for _, piece in pieces]
    step, both = arrays[0].shape
    rank = both // 2
    shape = jax.ShapeDtypeStruct((rows, rank), jnp.float32)
    block = pltpu.VMEM((count * step, rank), jnp.float32)
    return kernel_call(
        functools.partial(spread_kernel, count, scale, len(given)),
        (shape, shape),
        (count * step * both, 6 * count * step * both),
        [block, block, pltpu.SemaphoreType.DMA((2 * count,))],
        flags=1,
        operands=count,
        left=len(given),
        left_out=(0, 1),
        aliases={1 + count + i: i for i in range(len(given))},
    )(spots, *arrays, *given)


def update_kernel(rows_ref, far_ref, accum_ref, *refs):
    near_refs = refs[:-2]
    rows_out_ref, accum_out_ref = refs[-2:]
    emb = rows_ref.shape[1]
    for chunk in range(accum_ref.shape[0]):
        part = slice(chunk * SLOTS, (chunk + 1) * SLOTS)
        row_grad = far_ref[part, :].astype(jnp.float32)
        for near_ref in near_refs:
            row_grad = row_grad + near_ref[part, :emb].astype(jnp.float32)
        squares = jnp.mean(row_grad * row_grad, axis=1, keepdims=True)
        accum = as_column(accum_ref[chunk : chunk + 1, :]) + squares
        step = LEARN_RATE * row_grad * lax.rsqrt(accum + ADA_EPS)
        rows_out_ref[part, :] = (rows_ref[part, :].astype(jnp.float32) - step).astype(jnp.bfloat16)
        accum_out_ref[chunk : chunk + 1, :] = as_line(accum)


def update_rows(rows, far, accum, nears):
    share, emb = rows.shape
    chunks = share // SLOTS
    new_rows, new_accum = kernel_call(
        update_kernel,
        (
            jax.ShapeDtypeStruct((share, emb), jnp.bfloat16),
            jax.ShapeDtypeStruct((chunks, SLOTS), jnp.float32),
        ),
        (8 * rows.size, 8 * rows.size),
        operands=3 + len(nears),
    )(rows, far, accum.reshape(chunks, SLOTS), *nears)
    return new_rows, new_accum.reshape(share)


def join_kernel(swap_ref, mine_ref, other_ref, out_ref, sems):
    half = mine_ref.shape[0]
    copies = []
    for i, (from_ref, at) in enumerate(((mine_ref, swap_ref[0]), (other_ref, 1 - swap_ref[0]))):
        spot = pl.ds(pl.multiple_of(at * half, half), half)
        copies.append(pltpu.make_async_copy(from_ref, out_ref.at[spot, :], sems.at[i]))
        copies[-1].start()
    for copy in copies:
        copy.wait()


def join_halves(swap, mine, other):
    return kernel_call(
        join_kernel,
        jax.ShapeDtypeStruct((2 * mine.shape[0], mine.shape[1]), mine.dtype),
        (0, 8 * mine.size),
        [pltpu.SemaphoreType.DMA((2,))],
        flags=1,
        operands=2,
        left_out=(0,),
    )(swap, mine, other)


def group_levels(size):
    levels = []
    stride = 1
    while size % 4 == 0:
        levels.append((stride, 4))
        stride, size = stride * 4, size // 4
    if size > 1:
        levels.append((stride, size))
    return levels


def partner_index(index, stride, group, step):
    place = (index // stride) % group
    if group & (group - 1) == 0:
        other = place ^ step
    else:
        other = (place + step) % group
    return index + (other - place) * stride


def sent_from(axis, stride, group, step):
    size = lax.axis_size(axis)
    return [(partner_index(i, stride, group, step), i) for i in range(size)]


def scattered_pieces(blocks, axis, level):
    stride, group = level
    rows = blocks.shape[0] // group
    place = (lax.axis_index(axis) // stride) % group
    pieces = [lax.dynamic_slice_in_dim(blocks, place * rows, rows, 0)]
    for step in range(1, group):
        pairs = sent_from(axis, stride, group, step)
        if group & (group - 1) == 0:
            goal = place ^ step
        else:
            goal = (place + group - step) % group
        outgoing = lax.dynamic_slice_in_dim(blocks, goal * rows, rows, 0)
        pieces.append(lax.ppermute(outgoing, axis, pairs))
    return pieces


def summed(pieces):
    total = pieces[0].astype(jnp.float32)
    for piece in pieces[1:]:
        total = total + piece.astype(jnp.float32)
    return total.astype(jnp.bfloat16)


def scatter_sum(blocks, axis, levels):
    for level in levels:
        blocks = summed(scattered_pieces(blocks, axis, level))
    return blocks


def gathered_pieces(block, axis, level):
    stride, group = level
    index = lax.axis_index(axis)
    pieces = [((index // stride) % group, block)]
    for step in range(1, group):
        origin = partner_index(index, stride, group, step)
        came = lax.ppermute(block, axis, sent_from(axis, stride, group, step))
        pieces.append(((origin // stride) % group, came))
    return pieces


def gather_blocks(block, axis, levels):
    for level in reversed(levels):
        rows = block.shape[0]
        pieces = gathered_pieces(block, axis, level)
        block = jnp.zeros((len(pieces) * rows,) + block.shape[1:], block.dtype)
        for place, piece in pieces:
            block = lax.dynamic_update_slice_in_dim(block, piece, place * rows, 0)
    return block


def local(
    table_rows, accum, factor_down, factor_up, cross_bias, out_weight, target, bag_rows, slot_target
):
    tables = lax.axis_size("table")
    narrows = lax.axis_size("narrow")
    row_dev, emb_width = table_rows.shape
    pools_per = slot_target.shape[1]
    samples = target.shape[0]
    bag_count = samples * FEAT
    slot_count = tables * pools_per
    narrow_levels = group_levels(narrows)
    table_index = lax.axis_index("table")
    narrow_index = lax.axis_index("narrow")
    near_count = tables // 2
    half_levels = group_levels(near_count)
    far_half = table_index // near_count
    halves = [list(range(near_count)), list(range(near_count, tables))]
    across = [(i, (i + near_count) % tables) for i in range(tables)]
    paired = narrows == 2
    swap = (narrow_index if paired else narrow_index * 0).reshape(1)

    def near_and_far(rows):
        return tuple(
            lax.dynamic_slice_in_dim(rows, half * near_count, near_count, 0)
            for half in (far_half, 1 - far_half)
        )

    def in_order(near, far):
        return jnp.where(
            far_half == 0, jnp.concatenate([near, far]), jnp.concatenate([far, near])
        )

    def narrow_whole(block):
        if not paired:
            return gather_blocks(block, "narrow", narrow_levels)
        came = lax.ppermute(block, "narrow", sent_from("narrow", 1, 2, 1))
        first = jnp.where(narrow_index == 0, block, came)
        second = jnp.where(narrow_index == 0, came, block)
        return jnp.concatenate([first, second], axis=0)

    share_rows = row_dev // narrows
    own_halves = tuple(
        lax.dynamic_slice_in_dim(table_rows, half * (row_dev // 2), row_dev // 2, 0)
        for half in (swap[0], 1 - swap[0])
    )
    own_share = lax.dynamic_slice_in_dim(table_rows, narrow_index * share_rows, share_rows, 0)
    far_share = lax.ppermute(own_share, "table", across)
    down_full = narrow_whole(factor_down)
    up_full = narrow_whole(factor_up)

    per_window = bag_rows.shape[1]
    asked = jnp.concatenate(near_and_far(bag_rows), axis=1)[:, None, :]
    asked = lax.all_to_all(
        asked, "table", split_axis=0, concat_axis=0, tiled=True, axis_index_groups=halves
    )
    asked, far_share = lax.optimization_barrier((asked, far_share))
    if paired:
        came = lax.ppermute(far_share, "narrow", sent_from("narrow", 1, 2, 1))
        far_halves = (far_share, came)
    else:
        far_halves = tuple(jnp.split(narrow_whole(far_share), 2, axis=0))
    near_ids, far_ids = asked[:, 0, :per_window], asked[:, 0, per_window:]
    if per_window != SLOTS * HOT:
        by_block = (ids.reshape(-1, SLOTS * HOT) for ids in (near_ids, far_ids))
        asked = jnp.concatenate(tuple(by_block), axis=1)
    sums = pool_lookups(0, swap, asked, own_halves, pools_per)
    far_halves = lax.optimization_barrier((sums, *far_halves))
    sums, far_halves = far_halves[0], far_halves[1:]
    sums = pool_lookups(1, swap, asked, far_halves, pools_per, (sums,))
    arrived = lax.all_to_all(
        sums, "table", split_axis=0, concat_axis=0, tiled=True, axis_index_groups=halves
    )
    goals = jnp.stack(near_and_far(slot_target), axis=1)
    arrived, down_full, up_full, goals = lax.optimization_barrier(
        (arrived, down_full, up_full, goals)
    )
    logits, bag_grads, kept, sent = dense_step(
        swap,
        goals,
        arrived.reshape(slot_count, emb_width),
        down_full,
        up_full,
        cross_bias,
        out_weight,
        target,
    )
    if paired:
        came = lax.ppermute(sent, "narrow", sent_from("narrow", 1, 2, 1))
        narrow_sum = (kept.astype(jnp.float32) + came.astype(jnp.float32)).astype(jnp.bfloat16)
    else:
        narrow_sum = scatter_sum(jnp.concatenate([kept, sent], axis=0), "narrow", narrow_levels)
    slot_grads = return_grads(goals, bag_grads)
    groups = [group for _, group in half_levels]
    share_terms = narrow_sum.reshape(*groups, -1, narrow_sum.shape[1])
    order = list(range(len(groups)))[::-1] + [len(groups), len(groups) + 1]
    share_terms = share_terms.transpose(order).reshape(near_count, -1, narrow_sum.shape[1])
    rank = factor_down.shape[1]
    outgoing = [slot_grads.reshape(near_count, 2 * pools_per, emb_width)]
    outgoing += [share_terms[:, :, :rank], share_terms[:, :, rank:]]
    returned = lax.all_to_all(
        jnp.concatenate(outgoing, axis=1),
        "table",
        split_axis=0,
        concat_axis=0,
        tiled=True,
        axis_index_groups=halves,
    )
    terms = jnp.sum(returned[:, 2 * pools_per :].astype(jnp.float32), axis=0)
    half_sum = jnp.concatenate(jnp.split(terms, 2, axis=0), axis=1).astype(jnp.bfloat16)
    other_sum = lax.ppermute(half_sum, "table", across)
    mine, passed = row_grads(swap, asked, returned, pools_per, row_dev)
    other_sum, mine, passed = lax.optimization_barrier((other_sum, mine, passed))
    table_sum = summed([half_sum, other_sum])
    if paired:
        nears = [mine, lax.ppermute(passed, "narrow", sent_from("narrow", 1, 2, 1))]
    else:
        nears = [scatter_sum(jnp.concatenate([mine, passed], axis=0), "narrow", narrow_levels)]
    far_term = summed([term[:, emb_width:] for term in nears])
    inner = gather_blocks(table_sum, "table", half_levels[2:])
    blocks, fan = [(0, inner)], 1
    if len(half_levels) > 1:
        blocks, fan = gathered_pieces(inner, "table", half_levels[1]), half_levels[1][1]
    early, late = [], []
    for i, (place, block) in enumerate(blocks):
        pieces = gathered_pieces(block, "table", half_levels[0])
        pieces = [(spot * fan + place, piece) for spot, piece in pieces]
        early += pieces if i == 0 else pieces[:1]
        late += [] if i == 0 else pieces[1:]
    far_term = lax.ppermute(far_term, "table", across)
    spots, came = zip(*early, *late)
    far_term, *came = lax.optimization_barrier((far_term, *came))
    pieces = list(zip(spots, came))
    own_accum = lax.dynamic_slice_in_dim(accum, narrow_index * share_rows, share_rows, 0)
    new_share, new_accum = update_rows(own_share, far_term, own_accum, nears)
    if paired:
        other_share = lax.ppermute(new_share, "narrow", sent_from("narrow", 1, 2, 1))
        new_rows = join_halves(swap, new_share, other_share)
    else:
        new_rows = gather_blocks(new_share, "narrow", narrow_levels)
    scale = 1.0 / math.sqrt(samples * tables * narrows)
    down_grad, up_grad = spread_pieces(pieces, scale, factor_down.shape[0])
    return (logits, down_grad, up_grad, new_rows, new_accum)


def solution(mesh):
    in_specs = (
        P("table", None),
        P("table"),
        P("narrow", None),
        P("narrow", None),
        P(),
        P(),
        P(("table", "narrow")),
        P(("table", "narrow"), None),
        P(("table", "narrow"), None),
    )
    out_specs = (
        P(("table", "narrow")),
        P("narrow", None),
        P("narrow", None),
        P("table", None),
        P(("table", "narrow")),
    )
    return jax.shard_map(local, mesh=mesh, in_specs=in_specs, out_specs=out_specs, check_vma=False)
```

```python
import functools
import math

import jax
import jax.numpy as jnp
from jax import lax
from jax.experimental import pallas as pl
from jax.experimental.pallas import tpu as pltpu
from jax.sharding import PartitionSpec as P

FEAT = 8
HOT = 4


LEARN_RATE = 0.2
LOSS_SCALE = 32.0
ADA_EPS = 1e-06


SLOTS = 128
MIB = 1024 * 1024


def matmul(left, right):
    return jnp.dot(left, right, preferred_element_type=jnp.float32)


def transposed_dot(left, right):
    return lax.dot_general(
        left, right, (((0,), (0,)), ((), ())), preferred_element_type=jnp.float32
    )


def rows_dot(left, right):
    return lax.dot_general(
        left, right, (((1,), (1,)), ((), ())), preferred_element_type=jnp.float32
    )


def kernel_call(
    kernel, out_shape, cost, scratch=(), flags=0, operands=0, left=0, left_out=(), aliases=None, room=8
):
    flops, moved = cost
    smem = pl.BlockSpec(memory_space=pltpu.SMEM)
    vmem = pl.BlockSpec(memory_space=pltpu.VMEM)
    hbm = pl.BlockSpec(memory_space=pltpu.HBM)
    if isinstance(out_shape, tuple):
        out_specs = tuple(hbm if i in left_out else vmem for i in range(len(out_shape)))
    else:
        out_specs = hbm if left_out else vmem
    return pl.pallas_call(
        kernel,
        in_specs=[smem] * flags + [vmem] * operands + [hbm] * left,
        out_specs=out_specs,
        input_output_aliases=aliases or {},
        out_shape=out_shape,
        scratch_shapes=scratch,
        compiler_params=pltpu.CompilerParams(vmem_limit_bytes=room * MIB),
        cost_estimate=pl.CostEstimate(flops=flops, bytes_accessed=moved, transcendentals=0),
    )


def split_ids(ids):
    shifted = ids + 1
    high = lax.shift_right_logical(shifted, 5).astype(jnp.float32).astype(jnp.bfloat16)
    low = (shifted & 31).astype(jnp.float32).astype(jnp.bfloat16)
    return high, low


def lookup_choice():
    shape = (HOT * SLOTS, HOT * SLOTS)
    row = lax.broadcasted_iota(jnp.int32, shape, 0)
    column = lax.broadcasted_iota(jnp.int32, shape, 1)
    wanted = (row & (SLOTS - 1)) * HOT + lax.shift_right_logical(row, 7)
    return jnp.where(wanted == column, 1.0, 0.0).astype(jnp.bfloat16)


def joined(digits):
    high, low = digits
    return (high * 32.0 + low - 1.0).astype(jnp.int32)


def ones_where(mask):
    return jnp.where(mask, jnp.asarray(1, jnp.bfloat16), jnp.asarray(0, jnp.bfloat16))


def pool_kernel(part, swap_ref, ids_ref, first_ref, second_ref, *refs):
    out_ref, counts_ref, sums_ref, sem = refs[-4:]
    slots = counts_ref.shape[0]
    sources, _, pools, _ = out_ref.shape
    per_block = HOT * SLOTS
    if len(ids_ref.shape) == 3:
        ids = ids_ref[:, 0, part * per_block : (part + 1) * per_block]
    else:
        ids = ids_ref[:, part * per_block : (part + 1) * per_block]
    choice = lookup_choice()
    high, low = split_ids(ids)
    columns = joined((rows_dot(choice, high), rows_dot(choice, low))).astype(jnp.int16)
    half = first_ref.shape[0]
    position = lax.broadcasted_iota(jnp.int32, (SLOTS, 2 * half), 1) + swap_ref[0] * half
    position = jnp.where(position >= 2 * half, position - 2 * half, position).astype(jnp.int16)
    chunk = 2 * SLOTS
    for start in range(0, slots, chunk):
        for block in range(start // SLOTS, (start + chunk) // SLOTS):
            counts = None
            for lookup in range(HOT):
                column = columns[lookup * SLOTS : (lookup + 1) * SLOTS, block : block + 1]
                found = ones_where(column == position)
                counts = found if counts is None else counts + found
            counts_ref[block * SLOTS : (block + 1) * SLOTS, :] = counts
        here = slice(start, start + chunk)
        sums = matmul(counts_ref[here, :half], first_ref[...])
        sums = (sums + matmul(counts_ref[here, half:], second_ref[...])).astype(jnp.bfloat16)
        for source in range(start // pools, (start + chunk) // pools):
            at = source * pools - start
            sums_ref[source] = sums[at : at + pools]
    store = pltpu.make_async_copy(sums_ref, out_ref.at[:, part], sem)
    store.start()
    store.wait()


def pool_lookups(part, swap, ids, halves, pools, given=()):
    slots = ids.shape[0] * SLOTS
    row_dev, width = 2 * halves[0].shape[0], halves[0].shape[1]
    return kernel_call(
        functools.partial(pool_kernel, part),
        jax.ShapeDtypeStruct((slots // pools, 2, pools, width), jnp.bfloat16),
        (2 * slots * row_dev * width, 2 * row_dev * width + 2 * slots * width),
        [
            pltpu.VMEM((slots, row_dev), jnp.bfloat16),
            pltpu.VMEM((slots // pools, pools, width), jnp.bfloat16),
            pltpu.SemaphoreType.DMA,
        ],
        flags=1,
        operands=3,
        left=len(given),
        left_out=(0,),
        aliases={4: 0} if given else None,
        room=12,
    )(swap, ids, *halves, *given)


def row_grad_kernel(swap_ref, ids_ref, grads_ref, kept_ref, sent_ref, counts_ref, sums_ref):
    sources, _, emb = grads_ref.shape
    row_dev, slots = counts_ref.shape
    pools = slots // sources
    half = row_dev // 2
    per_block = HOT * SLOTS
    tile = 64
    choice = lookup_choice()
    position = lax.broadcasted_iota(jnp.int32, (tile, SLOTS), 0).astype(jnp.int16)
    for part in range(2):
        lanes = slice(part * per_block, (part + 1) * per_block)
        ids = ids_ref[:, 0, lanes] if len(ids_ref.shape) == 3 else ids_ref[:, lanes]
        high, low = split_ids(ids)
        lines = joined((rows_dot(high, choice), rows_dot(low, choice)))
        for block in range(slots // SLOTS):
            spread = []
            for lookup in range(HOT):
                line = lines[block : block + 1, lookup * SLOTS : (lookup + 1) * SLOTS]
                spread.append(jnp.broadcast_to(line, (tile, SLOTS)).astype(jnp.int16))
            for start in range(0, row_dev, tile):
                counts = None
                for lookup in range(HOT):
                    found = ones_where(spread[lookup] - jnp.asarray(start, jnp.int16) == position)
                    counts = found if counts is None else counts + found
                counts_ref[start : start + tile, block * SLOTS : (block + 1) * SLOTS] = counts
        grads = grads_ref[:, part * pools : (part + 1) * pools].reshape(slots, emb)
        where = slice(part * emb, (part + 1) * emb)
        sums_ref[:, where] = matmul(counts_ref[...], grads).astype(jnp.bfloat16)
    for out_ref, into_half in ((kept_ref, swap_ref[0]), (sent_ref, 1 - swap_ref[0])):
        out_ref[...] = sums_ref[pl.ds(pl.multiple_of(into_half * half, half), half), :]


def row_grads(swap, ids, slot_grads, pools, row_dev):
    sources, _, emb = slot_grads.shape
    slots = sources * pools
    half = jax.ShapeDtypeStruct((row_dev // 2, 2 * emb), jnp.bfloat16)
    return kernel_call(
        row_grad_kernel,
        (half, half),
        (4 * row_dev * slots * emb, 2 * slot_grads.size + 4 * row_dev * emb),
        [
            pltpu.VMEM((row_dev, slots), jnp.bfloat16),
            pltpu.VMEM((row_dev, 2 * emb), jnp.bfloat16),
        ],
        flags=1,
        operands=2,
        room=12,
    )(swap, ids, slot_grads)


def diagonal(size):
    row = lax.broadcasted_iota(jnp.int32, (size, size), 0)
    return row == lax.broadcasted_iota(jnp.int32, (size, size), 1)


def as_column(line):
    return jnp.sum(jnp.where(diagonal(line.shape[1]), line, 0.0), axis=1, keepdims=True)


def as_line(column):
    return jnp.sum(jnp.where(diagonal(column.shape[0]), column, 0.0), axis=0, keepdims=True)


def return_kernel(goals_ref, direct_ref, dhidden_ref, down_ref, out_ref, pick_ref, grads_ref):
    blocks = goals_ref.shape[0]
    bags, emb = grads_ref.shape
    samples = bags // FEAT
    for f in range(FEAT):
        part = slice(f * emb, (f + 1) * emb)
        back_term = rows_dot(dhidden_ref[...], down_ref[part, :])
        grads = direct_ref[:, part] + back_term
        grads_ref[f * samples : (f + 1) * samples, :] = grads.astype(jnp.bfloat16)
    high, low = split_ids(goals_ref[...])
    unit = ones_where(diagonal(SLOTS))
    columns = joined((rows_dot(unit, high), rows_dot(unit, low))).astype(jnp.int16)
    place = lax.broadcasted_iota(jnp.int32, (SLOTS, bags), 1)
    order = ((place % samples) * FEAT + place // samples).astype(jnp.int16)
    for block in range(0, blocks, 2):
        for one in (block, block + 1):
            pick_ref[one * SLOTS : (one + 1) * SLOTS, :] = ones_where(
                columns[:, one : one + 1] == order
            )
        here = slice(block * SLOTS, (block + 2) * SLOTS)
        out_ref[here, :] = matmul(pick_ref[here, :], grads_ref[...]).astype(jnp.bfloat16)


def return_grads(goals, direct, dhidden, down_full):
    samples, width = direct.shape
    emb = width // FEAT
    slot_count = goals.size
    return kernel_call(
        return_kernel,
        jax.ShapeDtypeStruct((slot_count, emb), jnp.bfloat16),
        (2 * slot_count * samples * width, 4 * direct.size + 2 * slot_count * emb),
        [
            pltpu.VMEM((slot_count, samples * FEAT), jnp.bfloat16),
            pltpu.VMEM((samples * FEAT, emb), jnp.bfloat16),
        ],
        operands=4,
        room=16,
    )(goals.reshape(slot_count // SLOTS, SLOTS), direct, dhidden, down_full)


def dense_kernel(
    swap_ref,
    goals_ref,
    bias_ref,
    weight_ref,
    target_ref,
    arrived_ref,
    down_ref,
    up_ref,
    logits_ref,
    direct_ref,
    dhidden_ref,
    kept_ref,
    sent_ref,
    place_ref,
    wide_ref,
    dcross_ref,
    shifted_ref,
):
    samples = target_ref.shape[1]
    width, rank = down_ref.shape
    emb = width // FEAT
    half = width // 2
    chunk = 512
    first_bag = lax.broadcasted_iota(jnp.int32, (samples, chunk), 0) * FEAT
    for start in range(0, goals_ref.shape[1], chunk):
        line = goals_ref[:, start : start + chunk]
        nth = (jnp.broadcast_to(line, (samples, chunk)) - first_bag).astype(jnp.int16)
        for f in range(FEAT):
            place_ref[f * samples : (f + 1) * samples, start : start + chunk] = ones_where(
                nth == jnp.asarray(f, jnp.int16)
            )
    features = [slice(f * emb, (f + 1) * emb) for f in range(FEAT)]
    for f, part in enumerate(features):
        spot = slice(f * samples, (f + 1) * samples)
        wide_ref[:, part] = matmul(place_ref[spot, :], arrived_ref[...]).astype(jnp.bfloat16)
    hidden = matmul(wide_ref[...], down_ref[...]).astype(jnp.bfloat16)
    summed = jnp.zeros((samples, emb), jnp.float32)
    for part in features:
        shifted = rows_dot(hidden, up_ref[part, :]) + bias_ref[:, part]
        shifted_ref[:, part] = shifted
        feats = wide_ref[:, part].astype(jnp.float32)
        summed = summed + (feats * shifted + feats) * weight_ref[:, part].astype(jnp.float32)
    logits = jnp.sum(summed, axis=1, keepdims=True)
    logits_ref[...] = as_line(logits)
    dlogit = LOSS_SCALE * (jax.nn.sigmoid(logits) - as_column(target_ref[...]))
    for part in features:
        dmixed = dlogit * weight_ref[:, part].astype(jnp.float32)
        feats = wide_ref[:, part].astype(jnp.float32)
        dcross_ref[:, part] = (dmixed * feats).astype(jnp.bfloat16)
        direct_ref[:, part] = dmixed * (shifted_ref[:, part] + 1.0)
    dhidden = matmul(dcross_ref[...], up_ref[...]).astype(jnp.bfloat16)
    dhidden_ref[...] = dhidden
    for step in range(FEAT):
        into_half = swap_ref[0] if step * emb < half else 1 - swap_ref[0]
        spot = (step * emb) % half
        part = pl.ds(pl.multiple_of(into_half * half + spot, emb), emb)
        out_ref = kept_ref if step * emb < half else sent_ref
        down_term = transposed_dot(wide_ref[:, part], dhidden)
        up_term = transposed_dot(dcross_ref[:, part], hidden)
        out_ref[spot : spot + emb, :rank] = down_term.astype(jnp.bfloat16)
        out_ref[spot : spot + emb, rank:] = up_term.astype(jnp.bfloat16)


def dense_step(swap, goals, arrived, down_full, up_full, bias, weight, target):
    samples = target.shape[0]
    slots, emb = arrived.shape
    width, rank = down_full.shape
    flops = 2 * slots * samples * width + 12 * samples * width * rank
    logits, direct, dhidden, kept, sent = kernel_call(
        dense_kernel,
        (
            jax.ShapeDtypeStruct((1, samples), jnp.float32),
            jax.ShapeDtypeStruct((samples, width), jnp.float32),
            jax.ShapeDtypeStruct((samples, rank), jnp.bfloat16),
            jax.ShapeDtypeStruct((width // 2, 2 * rank), jnp.bfloat16),
            jax.ShapeDtypeStruct((width // 2, 2 * rank), jnp.bfloat16),
        ),
        (flops, 2 * arrived.size + 8 * width * rank),
        [
            pltpu.VMEM((samples * FEAT, slots), jnp.bfloat16),
            pltpu.VMEM((samples, width), jnp.bfloat16),
            pltpu.VMEM((samples, width), jnp.bfloat16),
            pltpu.VMEM((samples, width), jnp.float32),
        ],
        flags=1,
        operands=7,
        room=20,
    )(
        swap,
        goals.reshape(1, slots),
        bias.reshape(1, width),
        weight.reshape(1, width),
        target.reshape(1, samples),
        arrived,
        down_full,
        up_full,
    )
    return logits.reshape(samples), direct, dhidden, kept, sent


def spread_kernel(count, scale, aliased, spots_ref, *refs):
    piece_refs = refs[:count]
    down_out_ref, up_out_ref, down_ref, up_ref, sems = refs[count + aliased :]
    rows = piece_refs[0].shape[0]
    rank = down_ref.shape[1]
    stores = []
    for i, piece_ref in enumerate(piece_refs):
        here = slice(i * rows, (i + 1) * rows)
        spot = pl.ds(pl.multiple_of(spots_ref[i] * rows, rows), rows)
        for half, (from_ref, to_ref) in enumerate(((down_ref, down_out_ref), (up_ref, up_out_ref))):
            part = slice(half * rank, (half + 1) * rank)
            from_ref[here, :] = piece_ref[:, part].astype(jnp.float32) * scale
            stores.append(
                pltpu.make_async_copy(from_ref.at[here, :], to_ref.at[spot, :], sems.at[len(stores)])
            )
            stores[-1].start()
    for store in stores:
        store.wait()


def spread_pieces(pieces, scale, rows, given=()):
    count = len(pieces)
    spots = jnp.stack([spot for spot, _ in pieces]).astype(jnp.int32)
    arrays = [piece for _, piece in pieces]
    step, both = arrays[0].shape
    rank = both // 2
    shape = jax.ShapeDtypeStruct((rows, rank), jnp.float32)
    block = pltpu.VMEM((count * step, rank), jnp.float32)
    return kernel_call(
        functools.partial(spread_kernel, count, scale, len(given)),
        (shape, shape),
        (count * step * both, 6 * count * step * both),
        [block, block, pltpu.SemaphoreType.DMA((2 * count,))],
        flags=1,
        operands=count,
        left=len(given),
        left_out=(0, 1),
        aliases={1 + count + i: i for i in range(len(given))},
    )(spots, *arrays, *given)


def update_kernel(rows_ref, far_ref, accum_ref, *refs):
    near_refs = refs[:-2]
    rows_out_ref, accum_out_ref = refs[-2:]
    emb = rows_ref.shape[1]
    for chunk in range(accum_ref.shape[0]):
        part = slice(chunk * SLOTS, (chunk + 1) * SLOTS)
        row_grad = far_ref[part, :].astype(jnp.float32)
        for near_ref in near_refs:
            row_grad = row_grad + near_ref[part, :emb].astype(jnp.float32)
        squares = jnp.mean(row_grad * row_grad, axis=1, keepdims=True)
        accum = as_column(accum_ref[chunk : chunk + 1, :]) + squares
        step = LEARN_RATE * row_grad * lax.rsqrt(accum + ADA_EPS)
        rows_out_ref[part, :] = (rows_ref[part, :].astype(jnp.float32) - step).astype(jnp.bfloat16)
        accum_out_ref[chunk : chunk + 1, :] = as_line(accum)


def update_rows(rows, far, accum, nears):
    share, emb = rows.shape
    chunks = share // SLOTS
    new_rows, new_accum = kernel_call(
        update_kernel,
        (
            jax.ShapeDtypeStruct((share, emb), jnp.bfloat16),
            jax.ShapeDtypeStruct((chunks, SLOTS), jnp.float32),
        ),
        (8 * rows.size, 8 * rows.size),
        operands=3 + len(nears),
    )(rows, far, accum.reshape(chunks, SLOTS), *nears)
    return new_rows, new_accum.reshape(share)


def join_kernel(swap_ref, mine_ref, other_ref, out_ref, sems):
    half = mine_ref.shape[0]
    copies = []
    for i, (from_ref, at) in enumerate(((mine_ref, swap_ref[0]), (other_ref, 1 - swap_ref[0]))):
        spot = pl.ds(pl.multiple_of(at * half, half), half)
        copies.append(pltpu.make_async_copy(from_ref, out_ref.at[spot, :], sems.at[i]))
        copies[-1].start()
    for copy in copies:
        copy.wait()


def join_halves(swap, mine, other):
    return kernel_call(
        join_kernel,
        jax.ShapeDtypeStruct((2 * mine.shape[0], mine.shape[1]), mine.dtype),
        (0, 8 * mine.size),
        [pltpu.SemaphoreType.DMA((2,))],
        flags=1,
        operands=2,
        left_out=(0,),
    )(swap, mine, other)


def group_levels(size):
    levels = []
    stride = 1
    while size % 4 == 0:
        levels.append((stride, 4))
        stride, size = stride * 4, size // 4
    if size > 1:
        levels.append((stride, size))
    return levels


def partner_index(index, stride, group, step):
    place = (index // stride) % group
    if group & (group - 1) == 0:
        other = place ^ step
    else:
        other = (place + step) % group
    return index + (other - place) * stride


def sent_from(axis, stride, group, step):
    size = lax.axis_size(axis)
    return [(partner_index(i, stride, group, step), i) for i in range(size)]


def scattered_pieces(blocks, axis, level):
    stride, group = level
    rows = blocks.shape[0] // group
    place = (lax.axis_index(axis) // stride) % group
    pieces = [lax.dynamic_slice_in_dim(blocks, place * rows, rows, 0)]
    for step in range(1, group):
        pairs = sent_from(axis, stride, group, step)
        if group & (group - 1) == 0:
            goal = place ^ step
        else:
            goal = (place + group - step) % group
        outgoing = lax.dynamic_slice_in_dim(blocks, goal * rows, rows, 0)
        pieces.append(lax.ppermute(outgoing, axis, pairs))
    return pieces


def summed(pieces):
    total = pieces[0].astype(jnp.float32)
    for piece in pieces[1:]:
        total = total + piece.astype(jnp.float32)
    return total.astype(jnp.bfloat16)


def scatter_sum(blocks, axis, levels):
    for level in levels:
        blocks = summed(scattered_pieces(blocks, axis, level))
    return blocks


def gathered_pieces(block, axis, level):
    stride, group = level
    index = lax.axis_index(axis)
    pieces = [((index // stride) % group, block)]
    for step in range(1, group):
        origin = partner_index(index, stride, group, step)
        came = lax.ppermute(block, axis, sent_from(axis, stride, group, step))
        pieces.append(((origin // stride) % group, came))
    return pieces


def gather_blocks(block, axis, levels):
    for level in reversed(levels):
        rows = block.shape[0]
        pieces = gathered_pieces(block, axis, level)
        block = jnp.zeros((len(pieces) * rows,) + block.shape[1:], block.dtype)
        for place, piece in pieces:
            block = lax.dynamic_update_slice_in_dim(block, piece, place * rows, 0)
    return block


def local(
    table_rows, accum, factor_down, factor_up, cross_bias, out_weight, target, bag_rows, slot_target
):
    tables = lax.axis_size("table")
    narrows = lax.axis_size("narrow")
    row_dev, emb_width = table_rows.shape
    pools_per = slot_target.shape[1]
    samples = target.shape[0]
    bag_count = samples * FEAT
    slot_count = tables * pools_per
    narrow_levels = group_levels(narrows)
    table_index = lax.axis_index("table")
    narrow_index = lax.axis_index("narrow")
    near_count = tables // 2
    half_levels = group_levels(near_count)
    far_half = table_index // near_count
    halves = [list(range(near_count)), list(range(near_count, tables))]
    across = [(i, (i + near_count) % tables) for i in range(tables)]
    paired = narrows == 2
    swap = (narrow_index if paired else narrow_index * 0).reshape(1)

    def near_and_far(rows):
        return tuple(
            lax.dynamic_slice_in_dim(rows, half * near_count, near_count, 0)
            for half in (far_half, 1 - far_half)
        )

    def in_order(near, far):
        return jnp.where(
            far_half == 0, jnp.concatenate([near, far]), jnp.concatenate([far, near])
        )

    def narrow_whole(block):
        if not paired:
            return gather_blocks(block, "narrow", narrow_levels)
        came = lax.ppermute(block, "narrow", sent_from("narrow", 1, 2, 1))
        first = jnp.where(narrow_index == 0, block, came)
        second = jnp.where(narrow_index == 0, came, block)
        return jnp.concatenate([first, second], axis=0)

    share_rows = row_dev // narrows
    own_halves = tuple(
        lax.dynamic_slice_in_dim(table_rows, half * (row_dev // 2), row_dev // 2, 0)
        for half in (swap[0], 1 - swap[0])
    )
    own_share = lax.dynamic_slice_in_dim(table_rows, narrow_index * share_rows, share_rows, 0)
    far_share = lax.ppermute(own_share, "table", across)
    down_full = narrow_whole(factor_down)
    up_full = narrow_whole(factor_up)

    per_window = bag_rows.shape[1]
    asked = jnp.concatenate(near_and_far(bag_rows), axis=1)[:, None, :]
    asked = lax.all_to_all(
        asked, "table", split_axis=0, concat_axis=0, tiled=True, axis_index_groups=halves
    )
    asked, far_share = lax.optimization_barrier((asked, far_share))
    if paired:
        came = lax.ppermute(far_share, "narrow", sent_from("narrow", 1, 2, 1))
        far_halves = (far_share, came)
    else:
        far_halves = tuple(jnp.split(narrow_whole(far_share), 2, axis=0))
    near_ids, far_ids = asked[:, 0, :per_window], asked[:, 0, per_window:]
    if per_window != SLOTS * HOT:
        by_block = (ids.reshape(-1, SLOTS * HOT) for ids in (near_ids, far_ids))
        asked = jnp.concatenate(tuple(by_block), axis=1)
    sums = pool_lookups(0, swap, asked, own_halves, pools_per)
    far_halves = lax.optimization_barrier((sums, *far_halves))
    sums, far_halves = far_halves[0], far_halves[1:]
    sums = pool_lookups(1, swap, asked, far_halves, pools_per, (sums,))
    arrived = lax.all_to_all(
        sums, "table", split_axis=0, concat_axis=0, tiled=True, axis_index_groups=halves
    )
    goals = jnp.stack(near_and_far(slot_target), axis=1)
    arrived, down_full, up_full, goals = lax.optimization_barrier(
        (arrived, down_full, up_full, goals)
    )
    logits, direct, dhidden, kept, sent = dense_step(
        swap,
        goals,
        arrived.reshape(slot_count, emb_width),
        down_full,
        up_full,
        cross_bias,
        out_weight,
        target,
    )
    if paired:
        came = lax.ppermute(sent, "narrow", sent_from("narrow", 1, 2, 1))
        narrow_sum = (kept.astype(jnp.float32) + came.astype(jnp.float32)).astype(jnp.bfloat16)
    else:
        narrow_sum = scatter_sum(jnp.concatenate([kept, sent], axis=0), "narrow", narrow_levels)
    slot_grads = return_grads(goals, direct, dhidden, down_full)
    groups = [group for _, group in half_levels]
    share_terms = narrow_sum.reshape(*groups, -1, narrow_sum.shape[1])
    order = list(range(len(groups)))[::-1] + [len(groups), len(groups) + 1]
    share_terms = share_terms.transpose(order).reshape(near_count, -1, narrow_sum.shape[1])
    rank = factor_down.shape[1]
    outgoing = [slot_grads.reshape(near_count, 2 * pools_per, emb_width)]
    outgoing += [share_terms[:, :, :rank], share_terms[:, :, rank:]]
    returned = lax.all_to_all(
        jnp.concatenate(outgoing, axis=1),
        "table",
        split_axis=0,
        concat_axis=0,
        tiled=True,
        axis_index_groups=halves,
    )
    terms = jnp.sum(returned[:, 2 * pools_per :].astype(jnp.float32), axis=0)
    half_sum = jnp.concatenate(jnp.split(terms, 2, axis=0), axis=1).astype(jnp.bfloat16)
    other_sum = lax.ppermute(half_sum, "table", across)
    mine, passed = row_grads(swap, asked, returned, pools_per, row_dev)
    other_sum, mine, passed = lax.optimization_barrier((other_sum, mine, passed))
    table_sum = summed([half_sum, other_sum])
    if paired:
        nears = [mine, lax.ppermute(passed, "narrow", sent_from("narrow", 1, 2, 1))]
    else:
        nears = [scatter_sum(jnp.concatenate([mine, passed], axis=0), "narrow", narrow_levels)]
    far_term = summed([term[:, emb_width:] for term in nears])
    inner = gather_blocks(table_sum, "table", half_levels[2:])
    blocks, fan = [(0, inner)], 1
    if len(half_levels) > 1:
        blocks, fan = gathered_pieces(inner, "table", half_levels[1]), half_levels[1][1]
    early, late = [], []
    for i, (place, block) in enumerate(blocks):
        pieces = gathered_pieces(block, "table", half_levels[0])
        pieces = [(spot * fan + place, piece) for spot, piece in pieces]
        early += pieces if i == 0 else pieces[:1]
        late += [] if i == 0 else pieces[1:]
    far_term = lax.ppermute(far_term, "table", across)
    spots, came = zip(*early, *late)
    far_term, *came = lax.optimization_barrier((far_term, *came))
    pieces = list(zip(spots, came))
    own_accum = lax.dynamic_slice_in_dim(accum, narrow_index * share_rows, share_rows, 0)
    new_share, new_accum = update_rows(own_share, far_term, own_accum, nears)
    if paired:
        other_share = lax.ppermute(new_share, "narrow", sent_from("narrow", 1, 2, 1))
        new_rows = join_halves(swap, new_share, other_share)
    else:
        new_rows = gather_blocks(new_share, "narrow", narrow_levels)
    scale = 1.0 / math.sqrt(samples * tables * narrows)
    down_grad, up_grad = spread_pieces(pieces, scale, factor_down.shape[0])
    return (logits, down_grad, up_grad, new_rows, new_accum)


def solution(mesh):
    in_specs = (
        P("table", None),
        P("table"),
        P("narrow", None),
        P("narrow", None),
        P(),
        P(),
        P(("table", "narrow")),
        P(("table", "narrow"), None),
        P(("table", "narrow"), None),
    )
    out_specs = (
        P(("table", "narrow")),
        P("narrow", None),
        P("narrow", None),
        P("table", None),
        P(("table", "narrow")),
    )
    return jax.shard_map(local, mesh=mesh, in_specs=in_specs, out_specs=out_specs, check_vma=False)
```

```python
import functools
import math

import jax
import jax.numpy as jnp
from jax import lax
from jax.experimental import pallas as pl
from jax.experimental.pallas import tpu as pltpu
from jax.sharding import PartitionSpec as P

FEAT = 8
HOT = 4


LEARN_RATE = 0.2
LOSS_SCALE = 32.0
ADA_EPS = 1e-06


SLOTS = 128
MIB = 1024 * 1024


def matmul(left, right):
    return jnp.dot(left, right, preferred_element_type=jnp.float32)


def transposed_dot(left, right):
    return lax.dot_general(
        left, right, (((0,), (0,)), ((), ())), preferred_element_type=jnp.float32
    )


def rows_dot(left, right):
    return lax.dot_general(
        left, right, (((1,), (1,)), ((), ())), preferred_element_type=jnp.float32
    )


def kernel_call(
    kernel, out_shape, cost, scratch=(), flags=0, operands=0, left=0, left_out=(), aliases=None, room=8
):
    flops, moved = cost
    smem = pl.BlockSpec(memory_space=pltpu.SMEM)
    vmem = pl.BlockSpec(memory_space=pltpu.VMEM)
    hbm = pl.BlockSpec(memory_space=pltpu.HBM)
    if isinstance(out_shape, tuple):
        out_specs = tuple(hbm if i in left_out else vmem for i in range(len(out_shape)))
    else:
        out_specs = hbm if left_out else vmem
    return pl.pallas_call(
        kernel,
        in_specs=[smem] * flags + [vmem] * operands + [hbm] * left,
        out_specs=out_specs,
        input_output_aliases=aliases or {},
        out_shape=out_shape,
        scratch_shapes=scratch,
        compiler_params=pltpu.CompilerParams(vmem_limit_bytes=room * MIB),
        cost_estimate=pl.CostEstimate(flops=flops, bytes_accessed=moved, transcendentals=0),
    )


def split_ids(ids):
    shifted = ids + 1
    high = lax.shift_right_logical(shifted, 5).astype(jnp.float32).astype(jnp.bfloat16)
    low = (shifted & 31).astype(jnp.float32).astype(jnp.bfloat16)
    return high, low


def lookup_choice():
    shape = (HOT * SLOTS, HOT * SLOTS)
    row = lax.broadcasted_iota(jnp.int32, shape, 0)
    column = lax.broadcasted_iota(jnp.int32, shape, 1)
    wanted = (row & (SLOTS - 1)) * HOT + lax.shift_right_logical(row, 7)
    return jnp.where(wanted == column, 1.0, 0.0).astype(jnp.bfloat16)


def joined(digits):
    high, low = digits
    return (high * 32.0 + low - 1.0).astype(jnp.int32)


def ones_where(mask):
    return jnp.where(mask, jnp.asarray(1, jnp.bfloat16), jnp.asarray(0, jnp.bfloat16))


def pool_kernel(part, swap_ref, ids_ref, first_ref, second_ref, *refs):
    out_ref, counts_ref, sums_ref, sem = refs[-4:]
    slots = counts_ref.shape[0]
    sources, _, pools, _ = out_ref.shape
    per_block = HOT * SLOTS
    if len(ids_ref.shape) == 3:
        ids = ids_ref[:, 0, part * per_block : (part + 1) * per_block]
    else:
        ids = ids_ref[:, part * per_block : (part + 1) * per_block]
    choice = lookup_choice()
    high, low = split_ids(ids)
    columns = joined((rows_dot(choice, high), rows_dot(choice, low))).astype(jnp.int16)
    half = first_ref.shape[0]
    position = lax.broadcasted_iota(jnp.int32, (SLOTS, 2 * half), 1) + swap_ref[0] * half
    position = jnp.where(position >= 2 * half, position - 2 * half, position).astype(jnp.int16)
    chunk = 2 * SLOTS
    for start in range(0, slots, chunk):
        for block in range(start // SLOTS, (start + chunk) // SLOTS):
            counts = None
            for lookup in range(HOT):
                column = columns[lookup * SLOTS : (lookup + 1) * SLOTS, block : block + 1]
                found = ones_where(column == position)
                counts = found if counts is None else counts + found
            counts_ref[block * SLOTS : (block + 1) * SLOTS, :] = counts
        here = slice(start, start + chunk)
        sums = matmul(counts_ref[here, :half], first_ref[...])
        sums = (sums + matmul(counts_ref[here, half:], second_ref[...])).astype(jnp.bfloat16)
        for source in range(start // pools, (start + chunk) // pools):
            at = source * pools - start
            sums_ref[source] = sums[at : at + pools]
    store = pltpu.make_async_copy(sums_ref, out_ref.at[:, part], sem)
    store.start()
    store.wait()


def pool_lookups(part, swap, ids, halves, pools, given=()):
    slots = ids.shape[0] * SLOTS
    row_dev, width = 2 * halves[0].shape[0], halves[0].shape[1]
    return kernel_call(
        functools.partial(pool_kernel, part),
        jax.ShapeDtypeStruct((slots // pools, 2, pools, width), jnp.bfloat16),
        (2 * slots * row_dev * width, 2 * row_dev * width + 2 * slots * width),
        [
            pltpu.VMEM((slots, row_dev), jnp.bfloat16),
            pltpu.VMEM((slots // pools, pools, width), jnp.bfloat16),
            pltpu.SemaphoreType.DMA,
        ],
        flags=1,
        operands=3,
        left=len(given),
        left_out=(0,),
        aliases={4: 0} if given else None,
        room=12,
    )(swap, ids, *halves, *given)


def row_grad_kernel(swap_ref, ids_ref, grads_ref, kept_ref, sent_ref, counts_ref, sums_ref):
    sources, _, emb = grads_ref.shape
    row_dev, slots = counts_ref.shape
    pools = slots // sources
    half = row_dev // 2
    per_block = HOT * SLOTS
    tile = 64
    choice = lookup_choice()
    position = lax.broadcasted_iota(jnp.int32, (tile, SLOTS), 0).astype(jnp.int16)
    for part in range(2):
        lanes = slice(part * per_block, (part + 1) * per_block)
        ids = ids_ref[:, 0, lanes] if len(ids_ref.shape) == 3 else ids_ref[:, lanes]
        high, low = split_ids(ids)
        lines = joined((rows_dot(high, choice), rows_dot(low, choice)))
        for block in range(slots // SLOTS):
            spread = []
            for lookup in range(HOT):
                line = lines[block : block + 1, lookup * SLOTS : (lookup + 1) * SLOTS]
                spread.append(jnp.broadcast_to(line, (tile, SLOTS)).astype(jnp.int16))
            for start in range(0, row_dev, tile):
                counts = None
                for lookup in range(HOT):
                    found = ones_where(spread[lookup] - jnp.asarray(start, jnp.int16) == position)
                    counts = found if counts is None else counts + found
                counts_ref[start : start + tile, block * SLOTS : (block + 1) * SLOTS] = counts
        grads = grads_ref[:, part * pools : (part + 1) * pools].reshape(slots, emb)
        where = slice(part * emb, (part + 1) * emb)
        sums_ref[:, where] = matmul(counts_ref[...], grads).astype(jnp.bfloat16)
    for out_ref, into_half in ((kept_ref, swap_ref[0]), (sent_ref, 1 - swap_ref[0])):
        out_ref[...] = sums_ref[pl.ds(pl.multiple_of(into_half * half, half), half), :]


def row_grads(swap, ids, slot_grads, pools, row_dev):
    sources, _, emb = slot_grads.shape
    slots = sources * pools
    half = jax.ShapeDtypeStruct((row_dev // 2, 2 * emb), jnp.bfloat16)
    return kernel_call(
        row_grad_kernel,
        (half, half),
        (4 * row_dev * slots * emb, 2 * slot_grads.size + 4 * row_dev * emb),
        [
            pltpu.VMEM((row_dev, slots), jnp.bfloat16),
            pltpu.VMEM((row_dev, 2 * emb), jnp.bfloat16),
        ],
        flags=1,
        operands=2,
        room=12,
    )(swap, ids, slot_grads)


def diagonal(size):
    row = lax.broadcasted_iota(jnp.int32, (size, size), 0)
    return row == lax.broadcasted_iota(jnp.int32, (size, size), 1)


def as_column(line):
    return jnp.sum(jnp.where(diagonal(line.shape[1]), line, 0.0), axis=1, keepdims=True)


def as_line(column):
    return jnp.sum(jnp.where(diagonal(column.shape[0]), column, 0.0), axis=0, keepdims=True)


def return_kernel(goals_ref, direct_ref, dhidden_ref, down_ref, out_ref, pick_ref, grads_ref):
    blocks = goals_ref.shape[0]
    bags, emb = grads_ref.shape
    samples = bags // FEAT
    for f in range(FEAT):
        part = slice(f * emb, (f + 1) * emb)
        back_term = rows_dot(dhidden_ref[...], down_ref[part, :])
        grads = direct_ref[:, part] + back_term
        grads_ref[f * samples : (f + 1) * samples, :] = grads.astype(jnp.bfloat16)
    high, low = split_ids(goals_ref[...])
    unit = ones_where(diagonal(SLOTS))
    columns = joined((rows_dot(unit, high), rows_dot(unit, low))).astype(jnp.int16)
    place = lax.broadcasted_iota(jnp.int32, (SLOTS, bags), 1)
    order = ((place % samples) * FEAT + place // samples).astype(jnp.int16)
    for block in range(0, blocks, 2):
        for one in (block, block + 1):
            pick_ref[one * SLOTS : (one + 1) * SLOTS, :] = ones_where(
                columns[:, one : one + 1] == order
            )
        here = slice(block * SLOTS, (block + 2) * SLOTS)
        out_ref[here, :] = matmul(pick_ref[here, :], grads_ref[...]).astype(jnp.bfloat16)


def return_grads(goals, direct, dhidden, down_full):
    samples, width = direct.shape
    emb = width // FEAT
    slot_count = goals.size
    return kernel_call(
        return_kernel,
        jax.ShapeDtypeStruct((slot_count, emb), jnp.bfloat16),
        (2 * slot_count * samples * width, 4 * direct.size + 2 * slot_count * emb),
        [
            pltpu.VMEM((slot_count, samples * FEAT), jnp.bfloat16),
            pltpu.VMEM((samples * FEAT, emb), jnp.bfloat16),
        ],
        operands=4,
        room=16,
    )(goals.reshape(slot_count // SLOTS, SLOTS), direct, dhidden, down_full)


def dense_kernel(
    swap_ref,
    goals_ref,
    bias_ref,
    weight_ref,
    target_ref,
    arrived_ref,
    down_ref,
    up_ref,
    logits_ref,
    direct_ref,
    dhidden_ref,
    kept_ref,
    sent_ref,
    place_ref,
    wide_ref,
    dcross_ref,
    shifted_ref,
):
    samples = target_ref.shape[1]
    width, rank = down_ref.shape
    emb = width // FEAT
    half = width // 2
    chunk = 512
    first_bag = lax.broadcasted_iota(jnp.int32, (samples, chunk), 0) * FEAT
    for start in range(0, goals_ref.shape[1], chunk):
        line = goals_ref[:, start : start + chunk]
        nth = (jnp.broadcast_to(line, (samples, chunk)) - first_bag).astype(jnp.int16)
        for f in range(FEAT):
            place_ref[f * samples : (f + 1) * samples, start : start + chunk] = ones_where(
                nth == jnp.asarray(f, jnp.int16)
            )
    features = [slice(f * emb, (f + 1) * emb) for f in range(FEAT)]
    for f, part in enumerate(features):
        spot = slice(f * samples, (f + 1) * samples)
        wide_ref[:, part] = matmul(place_ref[spot, :], arrived_ref[...]).astype(jnp.bfloat16)
    hidden = matmul(wide_ref[...], down_ref[...]).astype(jnp.bfloat16)
    summed = jnp.zeros((samples, emb), jnp.float32)
    for part in features:
        shifted = rows_dot(hidden, up_ref[part, :]) + bias_ref[:, part]
        shifted_ref[:, part] = shifted
        feats = wide_ref[:, part].astype(jnp.float32)
        summed = summed + (feats * shifted + feats) * weight_ref[:, part].astype(jnp.float32)
    logits = jnp.sum(summed, axis=1, keepdims=True)
    logits_ref[...] = as_line(logits)
    dlogit = LOSS_SCALE * (jax.nn.sigmoid(logits) - as_column(target_ref[...]))
    for part in features:
        dmixed = dlogit * weight_ref[:, part].astype(jnp.float32)
        feats = wide_ref[:, part].astype(jnp.float32)
        dcross_ref[:, part] = (dmixed * feats).astype(jnp.bfloat16)
        direct_ref[:, part] = dmixed * (shifted_ref[:, part] + 1.0)
    dhidden = matmul(dcross_ref[...], up_ref[...]).astype(jnp.bfloat16)
    dhidden_ref[...] = dhidden
    for step in range(FEAT):
        into_half = swap_ref[0] if step * emb < half else 1 - swap_ref[0]
        spot = (step * emb) % half
        part = pl.ds(pl.multiple_of(into_half * half + spot, emb), emb)
        out_ref = kept_ref if step * emb < half else sent_ref
        down_term = transposed_dot(wide_ref[:, part], dhidden)
        up_term = transposed_dot(dcross_ref[:, part], hidden)
        out_ref[spot : spot + emb, :rank] = down_term.astype(jnp.bfloat16)
        out_ref[spot : spot + emb, rank:] = up_term.astype(jnp.bfloat16)


def dense_step(swap, goals, arrived, down_full, up_full, bias, weight, target):
    samples = target.shape[0]
    slots, emb = arrived.shape
    width, rank = down_full.shape
    flops = 2 * slots * samples * width + 12 * samples * width * rank
    logits, direct, dhidden, kept, sent = kernel_call(
        dense_kernel,
        (
            jax.ShapeDtypeStruct((1, samples), jnp.float32),
            jax.ShapeDtypeStruct((samples, width), jnp.float32),
            jax.ShapeDtypeStruct((samples, rank), jnp.bfloat16),
            jax.ShapeDtypeStruct((width // 2, 2 * rank), jnp.bfloat16),
            jax.ShapeDtypeStruct((width // 2, 2 * rank), jnp.bfloat16),
        ),
        (flops, 2 * arrived.size + 8 * width * rank),
        [
            pltpu.VMEM((samples * FEAT, slots), jnp.bfloat16),
            pltpu.VMEM((samples, width), jnp.bfloat16),
            pltpu.VMEM((samples, width), jnp.bfloat16),
            pltpu.VMEM((samples, width), jnp.float32),
        ],
        flags=1,
        operands=7,
        room=20,
    )(
        swap,
        goals.reshape(1, slots),
        bias.reshape(1, width),
        weight.reshape(1, width),
        target.reshape(1, samples),
        arrived,
        down_full,
        up_full,
    )
    return logits.reshape(samples), direct, dhidden, kept, sent


def spread_kernel(count, scale, aliased, spots_ref, *refs):
    piece_refs = refs[:count]
    down_out_ref, up_out_ref, down_ref, up_ref, sems = refs[count + aliased :]
    rows = piece_refs[0].shape[0]
    rank = down_ref.shape[1]
    stores = []
    for i, piece_ref in enumerate(piece_refs):
        here = slice(i * rows, (i + 1) * rows)
        spot = pl.ds(pl.multiple_of(spots_ref[i] * rows, rows), rows)
        for half, (from_ref, to_ref) in enumerate(((down_ref, down_out_ref), (up_ref, up_out_ref))):
            part = slice(half * rank, (half + 1) * rank)
            from_ref[here, :] = piece_ref[:, part].astype(jnp.float32) * scale
            stores.append(
                pltpu.make_async_copy(from_ref.at[here, :], to_ref.at[spot, :], sems.at[len(stores)])
            )
            stores[-1].start()
    for store in stores:
        store.wait()


def spread_pieces(pieces, scale, rows, given=()):
    count = len(pieces)
    spots = jnp.stack([spot for spot, _ in pieces]).astype(jnp.int32)
    arrays = [piece for _, piece in pieces]
    step, both = arrays[0].shape
    rank = both // 2
    shape = jax.ShapeDtypeStruct((rows, rank), jnp.float32)
    block = pltpu.VMEM((count * step, rank), jnp.float32)
    return kernel_call(
        functools.partial(spread_kernel, count, scale, len(given)),
        (shape, shape),
        (count * step * both, 6 * count * step * both),
        [block, block, pltpu.SemaphoreType.DMA((2 * count,))],
        flags=1,
        operands=count,
        left=len(given),
        left_out=(0, 1),
        aliases={1 + count + i: i for i in range(len(given))},
    )(spots, *arrays, *given)


def update_kernel(rows_ref, far_ref, accum_ref, *refs):
    near_refs = refs[:-2]
    rows_out_ref, accum_out_ref = refs[-2:]
    emb = rows_ref.shape[1]
    for chunk in range(accum_ref.shape[0]):
        part = slice(chunk * SLOTS, (chunk + 1) * SLOTS)
        row_grad = far_ref[part, :].astype(jnp.float32)
        for near_ref in near_refs:
            row_grad = row_grad + near_ref[part, :emb].astype(jnp.float32)
        squares = jnp.mean(row_grad * row_grad, axis=1, keepdims=True)
        accum = as_column(accum_ref[chunk : chunk + 1, :]) + squares
        step = LEARN_RATE * row_grad * lax.rsqrt(accum + ADA_EPS)
        rows_out_ref[part, :] = (rows_ref[part, :].astype(jnp.float32) - step).astype(jnp.bfloat16)
        accum_out_ref[chunk : chunk + 1, :] = as_line(accum)


def update_rows(rows, far, accum, nears):
    share, emb = rows.shape
    chunks = share // SLOTS
    new_rows, new_accum = kernel_call(
        update_kernel,
        (
            jax.ShapeDtypeStruct((share, emb), jnp.bfloat16),
            jax.ShapeDtypeStruct((chunks, SLOTS), jnp.float32),
        ),
        (8 * rows.size, 8 * rows.size),
        operands=3 + len(nears),
    )(rows, far, accum.reshape(chunks, SLOTS), *nears)
    return new_rows, new_accum.reshape(share)


def join_kernel(swap_ref, mine_ref, other_ref, out_ref, sems):
    half = mine_ref.shape[0]
    copies = []
    for i, (from_ref, at) in enumerate(((mine_ref, swap_ref[0]), (other_ref, 1 - swap_ref[0]))):
        spot = pl.ds(pl.multiple_of(at * half, half), half)
        copies.append(pltpu.make_async_copy(from_ref, out_ref.at[spot, :], sems.at[i]))
        copies[-1].start()
    for copy in copies:
        copy.wait()


def join_halves(swap, mine, other):
    return kernel_call(
        join_kernel,
        jax.ShapeDtypeStruct((2 * mine.shape[0], mine.shape[1]), mine.dtype),
        (0, 8 * mine.size),
        [pltpu.SemaphoreType.DMA((2,))],
        flags=1,
        operands=2,
        left_out=(0,),
    )(swap, mine, other)


def group_levels(size):
    levels = []
    stride = 1
    while size % 4 == 0:
        levels.append((stride, 4))
        stride, size = stride * 4, size // 4
    if size > 1:
        levels.append((stride, size))
    return levels


def partner_index(index, stride, group, step):
    place = (index // stride) % group
    if group & (group - 1) == 0:
        other = place ^ step
    else:
        other = (place + step) % group
    return index + (other - place) * stride


def sent_from(axis, stride, group, step):
    size = lax.axis_size(axis)
    return [(partner_index(i, stride, group, step), i) for i in range(size)]


def scattered_pieces(blocks, axis, level):
    stride, group = level
    rows = blocks.shape[0] // group
    place = (lax.axis_index(axis) // stride) % group
    pieces = [lax.dynamic_slice_in_dim(blocks, place * rows, rows, 0)]
    for step in range(1, group):
        pairs = sent_from(axis, stride, group, step)
        if group & (group - 1) == 0:
            goal = place ^ step
        else:
            goal = (place + group - step) % group
        outgoing = lax.dynamic_slice_in_dim(blocks, goal * rows, rows, 0)
        pieces.append(lax.ppermute(outgoing, axis, pairs))
    return pieces


def summed(pieces):
    total = pieces[0].astype(jnp.float32)
    for piece in pieces[1:]:
        total = total + piece.astype(jnp.float32)
    return total.astype(jnp.bfloat16)


def scatter_sum(blocks, axis, levels):
    for level in levels:
        blocks = summed(scattered_pieces(blocks, axis, level))
    return blocks


def gathered_pieces(block, axis, level):
    stride, group = level
    index = lax.axis_index(axis)
    pieces = [((index // stride) % group, block)]
    for step in range(1, group):
        origin = partner_index(index, stride, group, step)
        came = lax.ppermute(block, axis, sent_from(axis, stride, group, step))
        pieces.append(((origin // stride) % group, came))
    return pieces


def gather_blocks(block, axis, levels):
    for level in reversed(levels):
        rows = block.shape[0]
        pieces = gathered_pieces(block, axis, level)
        block = jnp.zeros((len(pieces) * rows,) + block.shape[1:], block.dtype)
        for place, piece in pieces:
            block = lax.dynamic_update_slice_in_dim(block, piece, place * rows, 0)
    return block


def local(
    table_rows, accum, factor_down, factor_up, cross_bias, out_weight, target, bag_rows, slot_target
):
    tables = lax.axis_size("table")
    narrows = lax.axis_size("narrow")
    row_dev, emb_width = table_rows.shape
    pools_per = slot_target.shape[1]
    samples = target.shape[0]
    bag_count = samples * FEAT
    slot_count = tables * pools_per
    narrow_levels = group_levels(narrows)
    table_index = lax.axis_index("table")
    narrow_index = lax.axis_index("narrow")
    near_count = tables // 2
    half_levels = group_levels(near_count)
    far_half = table_index // near_count
    halves = [list(range(near_count)), list(range(near_count, tables))]
    across = [(i, (i + near_count) % tables) for i in range(tables)]
    paired = narrows == 2
    swap = (narrow_index if paired else narrow_index * 0).reshape(1)

    def near_and_far(rows):
        return tuple(
            lax.dynamic_slice_in_dim(rows, half * near_count, near_count, 0)
            for half in (far_half, 1 - far_half)
        )

    def in_order(near, far):
        return jnp.where(
            far_half == 0, jnp.concatenate([near, far]), jnp.concatenate([far, near])
        )

    def narrow_whole(block):
        if not paired:
            return gather_blocks(block, "narrow", narrow_levels)
        came = lax.ppermute(block, "narrow", sent_from("narrow", 1, 2, 1))
        first = jnp.where(narrow_index == 0, block, came)
        second = jnp.where(narrow_index == 0, came, block)
        return jnp.concatenate([first, second], axis=0)

    share_rows = row_dev // narrows
    own_halves = tuple(
        lax.dynamic_slice_in_dim(table_rows, half * (row_dev // 2), row_dev // 2, 0)
        for half in (swap[0], 1 - swap[0])
    )
    own_share = lax.dynamic_slice_in_dim(table_rows, narrow_index * share_rows, share_rows, 0)
    far_share = lax.ppermute(own_share, "table", across)
    down_full = narrow_whole(factor_down)
    up_full = narrow_whole(factor_up)

    per_window = bag_rows.shape[1]
    asked = jnp.concatenate(near_and_far(bag_rows), axis=1)[:, None, :]
    asked = lax.all_to_all(
        asked, "table", split_axis=0, concat_axis=0, tiled=True, axis_index_groups=halves
    )
    asked, far_share = lax.optimization_barrier((asked, far_share))
    if paired:
        came = lax.ppermute(far_share, "narrow", sent_from("narrow", 1, 2, 1))
        far_halves = (far_share, came)
    else:
        far_halves = tuple(jnp.split(narrow_whole(far_share), 2, axis=0))
    near_ids, far_ids = asked[:, 0, :per_window], asked[:, 0, per_window:]
    if per_window != SLOTS * HOT:
        by_block = (ids.reshape(-1, SLOTS * HOT) for ids in (near_ids, far_ids))
        asked = jnp.concatenate(tuple(by_block), axis=1)
    sums = pool_lookups(0, swap, asked, own_halves, pools_per)
    far_halves = lax.optimization_barrier((sums, *far_halves))
    sums, far_halves = far_halves[0], far_halves[1:]
    sums = pool_lookups(1, swap, asked, far_halves, pools_per, (sums,))
    arrived = lax.all_to_all(
        sums, "table", split_axis=0, concat_axis=0, tiled=True, axis_index_groups=halves
    )
    goals = jnp.stack(near_and_far(slot_target), axis=1)
    arrived, down_full, up_full, goals = lax.optimization_barrier(
        (arrived, down_full, up_full, goals)
    )
    logits, direct, dhidden, kept, sent = dense_step(
        swap,
        goals,
        arrived.reshape(slot_count, emb_width),
        down_full,
        up_full,
        cross_bias,
        out_weight,
        target,
    )
    if paired:
        came = lax.ppermute(sent, "narrow", sent_from("narrow", 1, 2, 1))
        narrow_sum = (kept.astype(jnp.float32) + came.astype(jnp.float32)).astype(jnp.bfloat16)
    else:
        narrow_sum = scatter_sum(jnp.concatenate([kept, sent], axis=0), "narrow", narrow_levels)
    slot_grads = return_grads(goals, direct, dhidden, down_full)
    groups = [group for _, group in half_levels]
    share_terms = narrow_sum.reshape(*groups, -1, narrow_sum.shape[1])
    order = list(range(len(groups)))[::-1] + [len(groups), len(groups) + 1]
    share_terms = share_terms.transpose(order).reshape(near_count, -1, narrow_sum.shape[1])

    def within_half(blocks):
        return lax.all_to_all(
            blocks, "table", split_axis=0, concat_axis=0, tiled=True, axis_index_groups=halves
        )

    returned = within_half(slot_grads.reshape(near_count, 2 * pools_per, emb_width))
    returned, share_terms = lax.optimization_barrier((returned, share_terms))
    terms = within_half(share_terms)
    mine, passed = row_grads(swap, asked, returned, pools_per, row_dev)
    if paired:
        nears = [mine, lax.ppermute(passed, "narrow", sent_from("narrow", 1, 2, 1))]
    else:
        nears = [scatter_sum(jnp.concatenate([mine, passed], axis=0), "narrow", narrow_levels)]
    far_term = summed([term[:, emb_width:] for term in nears])
    far_term = lax.ppermute(far_term, "table", across)
    terms, mine = lax.optimization_barrier((terms, mine))
    half_sum = jnp.sum(terms.astype(jnp.float32), axis=0).astype(jnp.bfloat16)
    other_sum = lax.ppermute(half_sum, "table", across)
    other_sum, far_term = lax.optimization_barrier((other_sum, far_term))
    table_sum = summed([half_sum, other_sum])
    inner = gather_blocks(table_sum, "table", half_levels[2:])
    blocks, fan = [(0, inner)], 1
    if len(half_levels) > 1:
        blocks, fan = gathered_pieces(inner, "table", half_levels[1]), half_levels[1][1]
    early, late = [], []
    for i, (place, block) in enumerate(blocks):
        pieces = gathered_pieces(block, "table", half_levels[0])
        pieces = [(spot * fan + place, piece) for spot, piece in pieces]
        early += pieces if i == 0 else pieces[:1]
        late += [] if i == 0 else pieces[1:]
    own_accum = lax.dynamic_slice_in_dim(accum, narrow_index * share_rows, share_rows, 0)
    new_share, new_accum = update_rows(own_share, far_term, own_accum, nears)
    if paired:
        other_share = lax.ppermute(new_share, "narrow", sent_from("narrow", 1, 2, 1))
        new_rows = join_halves(swap, new_share, other_share)
    else:
        new_rows = gather_blocks(new_share, "narrow", narrow_levels)
    scale = 1.0 / math.sqrt(samples * tables * narrows)
    down_grad, up_grad = spread_pieces(early, scale, factor_down.shape[0])
    if late:
        spots, last = zip(*late)
        new_rows, down_grad, up_grad, *last = lax.optimization_barrier(
            (new_rows, down_grad, up_grad, *last)
        )
        down_grad, up_grad = spread_pieces(
            list(zip(spots, last)), scale, factor_down.shape[0], (down_grad, up_grad)
        )
    return (logits, down_grad, up_grad, new_rows, new_accum)


def solution(mesh):
    in_specs = (
        P("table", None),
        P("table"),
        P("narrow", None),
        P("narrow", None),
        P(),
        P(),
        P(("table", "narrow")),
        P(("table", "narrow"), None),
        P(("table", "narrow"), None),
    )
    out_specs = (
        P(("table", "narrow")),
        P("narrow", None),
        P("narrow", None),
        P("table", None),
        P(("table", "narrow")),
    )
    return jax.shard_map(local, mesh=mesh, in_specs=in_specs, out_specs=out_specs, check_vma=False)
```

```python
import functools
import math

import jax
import jax.numpy as jnp
from jax import lax
from jax.experimental import pallas as pl
from jax.experimental.pallas import tpu as pltpu
from jax.sharding import PartitionSpec as P

FEAT = 8
HOT = 4


LEARN_RATE = 0.2
LOSS_SCALE = 32.0
ADA_EPS = 1e-06


SLOTS = 128
MIB = 1024 * 1024


def matmul(left, right):
    return jnp.dot(left, right, preferred_element_type=jnp.float32)


def transposed_dot(left, right):
    return lax.dot_general(
        left, right, (((0,), (0,)), ((), ())), preferred_element_type=jnp.float32
    )


def rows_dot(left, right):
    return lax.dot_general(
        left, right, (((1,), (1,)), ((), ())), preferred_element_type=jnp.float32
    )


def kernel_call(
    kernel, out_shape, cost, scratch=(), flags=0, operands=0, left=0, left_out=(), aliases=None, room=8
):
    flops, moved = cost
    smem = pl.BlockSpec(memory_space=pltpu.SMEM)
    vmem = pl.BlockSpec(memory_space=pltpu.VMEM)
    hbm = pl.BlockSpec(memory_space=pltpu.HBM)
    if isinstance(out_shape, tuple):
        out_specs = tuple(hbm if i in left_out else vmem for i in range(len(out_shape)))
    else:
        out_specs = hbm if left_out else vmem
    return pl.pallas_call(
        kernel,
        in_specs=[smem] * flags + [vmem] * operands + [hbm] * left,
        out_specs=out_specs,
        input_output_aliases=aliases or {},
        out_shape=out_shape,
        scratch_shapes=scratch,
        compiler_params=pltpu.CompilerParams(vmem_limit_bytes=room * MIB),
        cost_estimate=pl.CostEstimate(flops=flops, bytes_accessed=moved, transcendentals=0),
    )


def split_ids(ids):
    shifted = ids + 1
    high = lax.shift_right_logical(shifted, 5).astype(jnp.float32).astype(jnp.bfloat16)
    low = (shifted & 31).astype(jnp.float32).astype(jnp.bfloat16)
    return high, low


def lookup_choice():
    shape = (HOT * SLOTS, HOT * SLOTS)
    row = lax.broadcasted_iota(jnp.int32, shape, 0)
    column = lax.broadcasted_iota(jnp.int32, shape, 1)
    wanted = (row & (SLOTS - 1)) * HOT + lax.shift_right_logical(row, 7)
    return jnp.where(wanted == column, 1.0, 0.0).astype(jnp.bfloat16)


def joined(digits):
    high, low = digits
    return (high * 32.0 + low - 1.0).astype(jnp.int32)


def ones_where(mask):
    return jnp.where(mask, jnp.asarray(1, jnp.bfloat16), jnp.asarray(0, jnp.bfloat16))


def pool_kernel(part, swap_ref, ids_ref, first_ref, second_ref, *refs):
    out_ref, counts_ref, sums_ref, sem = refs[-4:]
    slots = counts_ref.shape[0]
    sources, _, pools, _ = out_ref.shape
    per_block = HOT * SLOTS
    if len(ids_ref.shape) == 3:
        ids = ids_ref[:, 0, part * per_block : (part + 1) * per_block]
    else:
        ids = ids_ref[:, part * per_block : (part + 1) * per_block]
    choice = lookup_choice()
    high, low = split_ids(ids)
    columns = joined((rows_dot(choice, high), rows_dot(choice, low))).astype(jnp.int16)
    half = first_ref.shape[0]
    position = lax.broadcasted_iota(jnp.int32, (SLOTS, 2 * half), 1) + swap_ref[0] * half
    position = jnp.where(position >= 2 * half, position - 2 * half, position).astype(jnp.int16)
    chunk = 2 * SLOTS
    for start in range(0, slots, chunk):
        for block in range(start // SLOTS, (start + chunk) // SLOTS):
            counts = None
            for lookup in range(HOT):
                column = columns[lookup * SLOTS : (lookup + 1) * SLOTS, block : block + 1]
                found = ones_where(column == position)
                counts = found if counts is None else counts + found
            counts_ref[block * SLOTS : (block + 1) * SLOTS, :] = counts
        here = slice(start, start + chunk)
        sums = matmul(counts_ref[here, :half], first_ref[...])
        sums = (sums + matmul(counts_ref[here, half:], second_ref[...])).astype(jnp.bfloat16)
        for source in range(start // pools, (start + chunk) // pools):
            at = source * pools - start
            sums_ref[source] = sums[at : at + pools]
    store = pltpu.make_async_copy(sums_ref, out_ref.at[:, part], sem)
    store.start()
    store.wait()


def pool_lookups(part, swap, ids, halves, pools, given=()):
    slots = ids.shape[0] * SLOTS
    row_dev, width = 2 * halves[0].shape[0], halves[0].shape[1]
    return kernel_call(
        functools.partial(pool_kernel, part),
        jax.ShapeDtypeStruct((slots // pools, 2, pools, width), jnp.bfloat16),
        (2 * slots * row_dev * width, 2 * row_dev * width + 2 * slots * width),
        [
            pltpu.VMEM((slots, row_dev), jnp.bfloat16),
            pltpu.VMEM((slots // pools, pools, width), jnp.bfloat16),
            pltpu.SemaphoreType.DMA,
        ],
        flags=1,
        operands=3,
        left=len(given),
        left_out=(0,),
        aliases={4: 0} if given else None,
        room=12,
    )(swap, ids, *halves, *given)


def row_grad_kernel(swap_ref, ids_ref, grads_ref, kept_ref, sent_ref, counts_ref, sums_ref):
    sources, _, emb = grads_ref.shape
    row_dev, slots = counts_ref.shape
    pools = slots // sources
    half = row_dev // 2
    per_block = HOT * SLOTS
    tile = 64
    choice = lookup_choice()
    position = lax.broadcasted_iota(jnp.int32, (tile, SLOTS), 0).astype(jnp.int16)
    for part in range(2):
        lanes = slice(part * per_block, (part + 1) * per_block)
        ids = ids_ref[:, 0, lanes] if len(ids_ref.shape) == 3 else ids_ref[:, lanes]
        high, low = split_ids(ids)
        lines = joined((rows_dot(high, choice), rows_dot(low, choice)))
        for block in range(slots // SLOTS):
            spread = []
            for lookup in range(HOT):
                line = lines[block : block + 1, lookup * SLOTS : (lookup + 1) * SLOTS]
                spread.append(jnp.broadcast_to(line, (tile, SLOTS)).astype(jnp.int16))
            for start in range(0, row_dev, tile):
                counts = None
                for lookup in range(HOT):
                    found = ones_where(spread[lookup] - jnp.asarray(start, jnp.int16) == position)
                    counts = found if counts is None else counts + found
                counts_ref[start : start + tile, block * SLOTS : (block + 1) * SLOTS] = counts
        grads = grads_ref[:, part * pools : (part + 1) * pools].reshape(slots, emb)
        where = slice(part * emb, (part + 1) * emb)
        sums_ref[:, where] = matmul(counts_ref[...], grads).astype(jnp.bfloat16)
    for out_ref, into_half in ((kept_ref, swap_ref[0]), (sent_ref, 1 - swap_ref[0])):
        out_ref[...] = sums_ref[pl.ds(pl.multiple_of(into_half * half, half), half), :]


def row_grads(swap, ids, slot_grads, pools, row_dev):
    sources, _, emb = slot_grads.shape
    slots = sources * pools
    half = jax.ShapeDtypeStruct((row_dev // 2, 2 * emb), jnp.bfloat16)
    return kernel_call(
        row_grad_kernel,
        (half, half),
        (4 * row_dev * slots * emb, 2 * slot_grads.size + 4 * row_dev * emb),
        [
            pltpu.VMEM((row_dev, slots), jnp.bfloat16),
            pltpu.VMEM((row_dev, 2 * emb), jnp.bfloat16),
        ],
        flags=1,
        operands=2,
        room=12,
    )(swap, ids, slot_grads)


def diagonal(size):
    row = lax.broadcasted_iota(jnp.int32, (size, size), 0)
    return row == lax.broadcasted_iota(jnp.int32, (size, size), 1)


def as_column(line):
    return jnp.sum(jnp.where(diagonal(line.shape[1]), line, 0.0), axis=1, keepdims=True)


def as_line(column):
    return jnp.sum(jnp.where(diagonal(column.shape[0]), column, 0.0), axis=0, keepdims=True)


def return_kernel(goals_ref, direct_ref, dhidden_ref, down_ref, out_ref, pick_ref, grads_ref):
    blocks = goals_ref.shape[0]
    bags, emb = grads_ref.shape
    samples = bags // FEAT
    for f in range(FEAT):
        part = slice(f * emb, (f + 1) * emb)
        back_term = rows_dot(dhidden_ref[...], down_ref[part, :])
        grads = direct_ref[:, part] + back_term
        grads_ref[f * samples : (f + 1) * samples, :] = grads.astype(jnp.bfloat16)
    high, low = split_ids(goals_ref[...])
    unit = ones_where(diagonal(SLOTS))
    columns = joined((rows_dot(unit, high), rows_dot(unit, low))).astype(jnp.int16)
    place = lax.broadcasted_iota(jnp.int32, (SLOTS, bags), 1)
    order = ((place % samples) * FEAT + place // samples).astype(jnp.int16)
    for block in range(0, blocks, 2):
        for one in (block, block + 1):
            pick_ref[one * SLOTS : (one + 1) * SLOTS, :] = ones_where(
                columns[:, one : one + 1] == order
            )
        here = slice(block * SLOTS, (block + 2) * SLOTS)
        out_ref[here, :] = matmul(pick_ref[here, :], grads_ref[...]).astype(jnp.bfloat16)


def return_grads(goals, direct, dhidden, down_full):
    samples, width = direct.shape
    emb = width // FEAT
    slot_count = goals.size
    return kernel_call(
        return_kernel,
        jax.ShapeDtypeStruct((slot_count, emb), jnp.bfloat16),
        (2 * slot_count * samples * width, 4 * direct.size + 2 * slot_count * emb),
        [
            pltpu.VMEM((slot_count, samples * FEAT), jnp.bfloat16),
            pltpu.VMEM((samples * FEAT, emb), jnp.bfloat16),
        ],
        operands=4,
        room=16,
    )(goals.reshape(slot_count // SLOTS, SLOTS), direct, dhidden, down_full)


def dense_kernel(
    swap_ref,
    goals_ref,
    bias_ref,
    weight_ref,
    target_ref,
    arrived_ref,
    down_ref,
    up_ref,
    logits_ref,
    direct_ref,
    dhidden_ref,
    kept_ref,
    sent_ref,
    place_ref,
    wide_ref,
    dcross_ref,
    shifted_ref,
):
    samples = target_ref.shape[1]
    width, rank = down_ref.shape
    emb = width // FEAT
    half = width // 2
    chunk = 512
    first_bag = lax.broadcasted_iota(jnp.int32, (samples, chunk), 0) * FEAT
    for start in range(0, goals_ref.shape[1], chunk):
        line = goals_ref[:, start : start + chunk]
        nth = (jnp.broadcast_to(line, (samples, chunk)) - first_bag).astype(jnp.int16)
        for f in range(FEAT):
            place_ref[f * samples : (f + 1) * samples, start : start + chunk] = ones_where(
                nth == jnp.asarray(f, jnp.int16)
            )
    features = [slice(f * emb, (f + 1) * emb) for f in range(FEAT)]
    for f, part in enumerate(features):
        spot = slice(f * samples, (f + 1) * samples)
        wide_ref[:, part] = matmul(place_ref[spot, :], arrived_ref[...]).astype(jnp.bfloat16)
    hidden = matmul(wide_ref[...], down_ref[...]).astype(jnp.bfloat16)
    summed = jnp.zeros((samples, emb), jnp.float32)
    for part in features:
        shifted = rows_dot(hidden, up_ref[part, :]) + bias_ref[:, part]
        shifted_ref[:, part] = shifted
        feats = wide_ref[:, part].astype(jnp.float32)
        summed = summed + (feats * shifted + feats) * weight_ref[:, part].astype(jnp.float32)
    logits = jnp.sum(summed, axis=1, keepdims=True)
    logits_ref[...] = as_line(logits)
    dlogit = LOSS_SCALE * (jax.nn.sigmoid(logits) - as_column(target_ref[...]))
    for part in features:
        dmixed = dlogit * weight_ref[:, part].astype(jnp.float32)
        feats = wide_ref[:, part].astype(jnp.float32)
        dcross_ref[:, part] = (dmixed * feats).astype(jnp.bfloat16)
        direct_ref[:, part] = dmixed * (shifted_ref[:, part] + 1.0)
    dhidden = matmul(dcross_ref[...], up_ref[...]).astype(jnp.bfloat16)
    dhidden_ref[...] = dhidden
    for step in range(FEAT):
        into_half = swap_ref[0] if step * emb < half else 1 - swap_ref[0]
        spot = (step * emb) % half
        part = pl.ds(pl.multiple_of(into_half * half + spot, emb), emb)
        out_ref = kept_ref if step * emb < half else sent_ref
        down_term = transposed_dot(wide_ref[:, part], dhidden)
        up_term = transposed_dot(dcross_ref[:, part], hidden)
        out_ref[spot : spot + emb, :rank] = down_term.astype(jnp.bfloat16)
        out_ref[spot : spot + emb, rank:] = up_term.astype(jnp.bfloat16)


def dense_step(swap, goals, arrived, down_full, up_full, bias, weight, target):
    samples = target.shape[0]
    slots, emb = arrived.shape
    width, rank = down_full.shape
    flops = 2 * slots * samples * width + 12 * samples * width * rank
    logits, direct, dhidden, kept, sent = kernel_call(
        dense_kernel,
        (
            jax.ShapeDtypeStruct((1, samples), jnp.float32),
            jax.ShapeDtypeStruct((samples, width), jnp.float32),
            jax.ShapeDtypeStruct((samples, rank), jnp.bfloat16),
            jax.ShapeDtypeStruct((width // 2, 2 * rank), jnp.bfloat16),
            jax.ShapeDtypeStruct((width // 2, 2 * rank), jnp.bfloat16),
        ),
        (flops, 2 * arrived.size + 8 * width * rank),
        [
            pltpu.VMEM((samples * FEAT, slots), jnp.bfloat16),
            pltpu.VMEM((samples, width), jnp.bfloat16),
            pltpu.VMEM((samples, width), jnp.bfloat16),
            pltpu.VMEM((samples, width), jnp.float32),
        ],
        flags=1,
        operands=7,
        room=20,
    )(
        swap,
        goals.reshape(1, slots),
        bias.reshape(1, width),
        weight.reshape(1, width),
        target.reshape(1, samples),
        arrived,
        down_full,
        up_full,
    )
    return logits.reshape(samples), direct, dhidden, kept, sent


def spread_kernel(count, scale, aliased, spots_ref, *refs):
    piece_refs = refs[:count]
    down_out_ref, up_out_ref, down_ref, up_ref, sems = refs[count + aliased :]
    rows = piece_refs[0].shape[0]
    rank = down_ref.shape[1]
    stores = []
    for i, piece_ref in enumerate(piece_refs):
        here = slice(i * rows, (i + 1) * rows)
        spot = pl.ds(pl.multiple_of(spots_ref[i] * rows, rows), rows)
        for half, (from_ref, to_ref) in enumerate(((down_ref, down_out_ref), (up_ref, up_out_ref))):
            part = slice(half * rank, (half + 1) * rank)
            from_ref[here, :] = piece_ref[:, part].astype(jnp.float32) * scale
            stores.append(
                pltpu.make_async_copy(from_ref.at[here, :], to_ref.at[spot, :], sems.at[len(stores)])
            )
            stores[-1].start()
    for store in stores:
        store.wait()


def spread_pieces(pieces, scale, rows, given=()):
    count = len(pieces)
    spots = jnp.stack([spot for spot, _ in pieces]).astype(jnp.int32)
    arrays = [piece for _, piece in pieces]
    step, both = arrays[0].shape
    rank = both // 2
    shape = jax.ShapeDtypeStruct((rows, rank), jnp.float32)
    block = pltpu.VMEM((count * step, rank), jnp.float32)
    return kernel_call(
        functools.partial(spread_kernel, count, scale, len(given)),
        (shape, shape),
        (count * step * both, 6 * count * step * both),
        [block, block, pltpu.SemaphoreType.DMA((2 * count,))],
        flags=1,
        operands=count,
        left=len(given),
        left_out=(0, 1),
        aliases={1 + count + i: i for i in range(len(given))},
    )(spots, *arrays, *given)


def update_kernel(rows_ref, far_ref, accum_ref, *refs):
    near_refs = refs[:-2]
    rows_out_ref, accum_out_ref = refs[-2:]
    emb = rows_ref.shape[1]
    for chunk in range(accum_ref.shape[0]):
        part = slice(chunk * SLOTS, (chunk + 1) * SLOTS)
        row_grad = far_ref[part, :].astype(jnp.float32)
        for near_ref in near_refs:
            row_grad = row_grad + near_ref[part, :emb].astype(jnp.float32)
        squares = jnp.mean(row_grad * row_grad, axis=1, keepdims=True)
        accum = as_column(accum_ref[chunk : chunk + 1, :]) + squares
        step = LEARN_RATE * row_grad * lax.rsqrt(accum + ADA_EPS)
        rows_out_ref[part, :] = (rows_ref[part, :].astype(jnp.float32) - step).astype(jnp.bfloat16)
        accum_out_ref[chunk : chunk + 1, :] = as_line(accum)


def update_rows(rows, far, accum, nears):
    share, emb = rows.shape
    chunks = share // SLOTS
    new_rows, new_accum = kernel_call(
        update_kernel,
        (
            jax.ShapeDtypeStruct((share, emb), jnp.bfloat16),
            jax.ShapeDtypeStruct((chunks, SLOTS), jnp.float32),
        ),
        (8 * rows.size, 8 * rows.size),
        operands=3 + len(nears),
    )(rows, far, accum.reshape(chunks, SLOTS), *nears)
    return new_rows, new_accum.reshape(share)


def join_kernel(swap_ref, mine_ref, other_ref, out_ref, sems):
    half = mine_ref.shape[0]
    copies = []
    for i, (from_ref, at) in enumerate(((mine_ref, swap_ref[0]), (other_ref, 1 - swap_ref[0]))):
        spot = pl.ds(pl.multiple_of(at * half, half), half)
        copies.append(pltpu.make_async_copy(from_ref, out_ref.at[spot, :], sems.at[i]))
        copies[-1].start()
    for copy in copies:
        copy.wait()


def join_halves(swap, mine, other):
    return kernel_call(
        join_kernel,
        jax.ShapeDtypeStruct((2 * mine.shape[0], mine.shape[1]), mine.dtype),
        (0, 8 * mine.size),
        [pltpu.SemaphoreType.DMA((2,))],
        flags=1,
        operands=2,
        left_out=(0,),
    )(swap, mine, other)


def group_levels(size):
    levels = []
    stride = 1
    while size % 4 == 0:
        levels.append((stride, 4))
        stride, size = stride * 4, size // 4
    if size > 1:
        levels.append((stride, size))
    return levels


def partner_index(index, stride, group, step):
    place = (index // stride) % group
    if group & (group - 1) == 0:
        other = place ^ step
    else:
        other = (place + step) % group
    return index + (other - place) * stride


def sent_from(axis, stride, group, step):
    size = lax.axis_size(axis)
    return [(partner_index(i, stride, group, step), i) for i in range(size)]


def scattered_pieces(blocks, axis, level):
    stride, group = level
    rows = blocks.shape[0] // group
    place = (lax.axis_index(axis) // stride) % group
    pieces = [lax.dynamic_slice_in_dim(blocks, place * rows, rows, 0)]
    for step in range(1, group):
        pairs = sent_from(axis, stride, group, step)
        if group & (group - 1) == 0:
            goal = place ^ step
        else:
            goal = (place + group - step) % group
        outgoing = lax.dynamic_slice_in_dim(blocks, goal * rows, rows, 0)
        pieces.append(lax.ppermute(outgoing, axis, pairs))
    return pieces


def summed(pieces):
    total = pieces[0].astype(jnp.float32)
    for piece in pieces[1:]:
        total = total + piece.astype(jnp.float32)
    return total.astype(jnp.bfloat16)


def scatter_sum(blocks, axis, levels):
    for level in levels:
        blocks = summed(scattered_pieces(blocks, axis, level))
    return blocks


def gathered_pieces(block, axis, level):
    stride, group = level
    index = lax.axis_index(axis)
    pieces = [((index // stride) % group, block)]
    for step in range(1, group):
        origin = partner_index(index, stride, group, step)
        came = lax.ppermute(block, axis, sent_from(axis, stride, group, step))
        pieces.append(((origin // stride) % group, came))
    return pieces


def gather_blocks(block, axis, levels):
    for level in levels:
        rows = block.shape[0]
        pieces = gathered_pieces(block, axis, level)
        block = jnp.zeros((len(pieces) * rows,) + block.shape[1:], block.dtype)
        for place, piece in pieces:
            block = lax.dynamic_update_slice_in_dim(block, piece, place * rows, 0)
    return block


def local(
    table_rows, accum, factor_down, factor_up, cross_bias, out_weight, target, bag_rows, slot_target
):
    tables = lax.axis_size("table")
    narrows = lax.axis_size("narrow")
    row_dev, emb_width = table_rows.shape
    pools_per = slot_target.shape[1]
    samples = target.shape[0]
    bag_count = samples * FEAT
    slot_count = tables * pools_per
    narrow_levels = group_levels(narrows)
    table_index = lax.axis_index("table")
    narrow_index = lax.axis_index("narrow")
    near_count = tables // 2
    half_levels = group_levels(near_count)
    far_half = table_index // near_count
    halves = [list(range(near_count)), list(range(near_count, tables))]
    across = [(i, (i + near_count) % tables) for i in range(tables)]
    paired = narrows == 2
    swap = (narrow_index if paired else narrow_index * 0).reshape(1)

    def near_and_far(rows):
        return tuple(
            lax.dynamic_slice_in_dim(rows, half * near_count, near_count, 0)
            for half in (far_half, 1 - far_half)
        )

    def in_order(near, far):
        return jnp.where(
            far_half == 0, jnp.concatenate([near, far]), jnp.concatenate([far, near])
        )

    def narrow_whole(block):
        if not paired:
            return gather_blocks(block, "narrow", narrow_levels)
        came = lax.ppermute(block, "narrow", sent_from("narrow", 1, 2, 1))
        first = jnp.where(narrow_index == 0, block, came)
        second = jnp.where(narrow_index == 0, came, block)
        return jnp.concatenate([first, second], axis=0)

    share_rows = row_dev // narrows
    own_halves = tuple(
        lax.dynamic_slice_in_dim(table_rows, half * (row_dev // 2), row_dev // 2, 0)
        for half in (swap[0], 1 - swap[0])
    )
    own_share = lax.dynamic_slice_in_dim(table_rows, narrow_index * share_rows, share_rows, 0)
    far_share = lax.ppermute(own_share, "table", across)
    down_full = narrow_whole(factor_down)
    up_full = narrow_whole(factor_up)

    per_window = bag_rows.shape[1]
    asked = jnp.concatenate(near_and_far(bag_rows), axis=1)[:, None, :]
    asked = lax.all_to_all(
        asked, "table", split_axis=0, concat_axis=0, tiled=True, axis_index_groups=halves
    )
    asked, far_share = lax.optimization_barrier((asked, far_share))
    if paired:
        came = lax.ppermute(far_share, "narrow", sent_from("narrow", 1, 2, 1))
        far_halves = (far_share, came)
    else:
        far_halves = tuple(jnp.split(narrow_whole(far_share), 2, axis=0))
    near_ids, far_ids = asked[:, 0, :per_window], asked[:, 0, per_window:]
    if per_window != SLOTS * HOT:
        by_block = (ids.reshape(-1, SLOTS * HOT) for ids in (near_ids, far_ids))
        asked = jnp.concatenate(tuple(by_block), axis=1)
    sums = pool_lookups(0, swap, asked, own_halves, pools_per)
    far_halves = lax.optimization_barrier((sums, *far_halves))
    sums, far_halves = far_halves[0], far_halves[1:]
    sums = pool_lookups(1, swap, asked, far_halves, pools_per, (sums,))
    arrived = lax.all_to_all(
        sums, "table", split_axis=0, concat_axis=0, tiled=True, axis_index_groups=halves
    )
    goals = jnp.stack(near_and_far(slot_target), axis=1)
    arrived, down_full, up_full, goals = lax.optimization_barrier(
        (arrived, down_full, up_full, goals)
    )
    logits, direct, dhidden, kept, sent = dense_step(
        swap,
        goals,
        arrived.reshape(slot_count, emb_width),
        down_full,
        up_full,
        cross_bias,
        out_weight,
        target,
    )
    if paired:
        came = lax.ppermute(sent, "narrow", sent_from("narrow", 1, 2, 1))
        narrow_sum = (kept.astype(jnp.float32) + came.astype(jnp.float32)).astype(jnp.bfloat16)
    else:
        narrow_sum = scatter_sum(jnp.concatenate([kept, sent], axis=0), "narrow", narrow_levels[::-1])
    slot_grads = return_grads(goals, direct, dhidden, down_full)
    groups = [group for _, group in half_levels]
    share_terms = narrow_sum.reshape(*groups, -1, narrow_sum.shape[1])
    order = list(range(len(groups)))[::-1] + [len(groups), len(groups) + 1]
    share_terms = share_terms.transpose(order).reshape(near_count, -1, narrow_sum.shape[1])
    rank = factor_down.shape[1]
    outgoing = [slot_grads.reshape(near_count, 2 * pools_per, emb_width)]
    outgoing += [share_terms[:, :, :rank], share_terms[:, :, rank:]]
    returned = lax.all_to_all(
        jnp.concatenate(outgoing, axis=1),
        "table",
        split_axis=0,
        concat_axis=0,
        tiled=True,
        axis_index_groups=halves,
    )
    terms = jnp.sum(returned[:, 2 * pools_per :].astype(jnp.float32), axis=0)
    half_sum = jnp.concatenate(jnp.split(terms, 2, axis=0), axis=1).astype(jnp.bfloat16)
    other_sum = lax.ppermute(half_sum, "table", across)
    mine, passed = row_grads(swap, asked, returned, pools_per, row_dev)
    other_sum, mine, passed = lax.optimization_barrier((other_sum, mine, passed))
    table_sum = summed([half_sum, other_sum])
    if paired:
        nears = [mine, lax.ppermute(passed, "narrow", sent_from("narrow", 1, 2, 1))]
    else:
        nears = [scatter_sum(jnp.concatenate([mine, passed], axis=0), "narrow", narrow_levels[::-1])]
    far_term = summed([term[:, emb_width:] for term in nears])
    inner = gather_blocks(table_sum, "table", half_levels[2:][::-1])
    blocks, fan = [(0, inner)], 1
    if len(half_levels) > 1:
        blocks, fan = gathered_pieces(inner, "table", half_levels[1]), half_levels[1][1]
    early, late = [], []
    for i, (place, block) in enumerate(blocks):
        pieces = gathered_pieces(block, "table", half_levels[0])
        pieces = [(spot * fan + place, piece) for spot, piece in pieces]
        early += pieces if i == 0 else pieces[:1]
        late += [] if i == 0 else pieces[1:]
    far_term = lax.ppermute(far_term, "table", across)
    spots, came = zip(*early, *late)
    far_term, *came = lax.optimization_barrier((far_term, *came))
    pieces = list(zip(spots, came))
    own_accum = lax.dynamic_slice_in_dim(accum, narrow_index * share_rows, share_rows, 0)
    new_share, new_accum = update_rows(own_share, far_term, own_accum, nears)
    if paired:
        other_share = lax.ppermute(new_share, "narrow", sent_from("narrow", 1, 2, 1))
        new_rows = join_halves(swap, new_share, other_share)
    else:
        new_rows = gather_blocks(new_share, "narrow", narrow_levels)
    scale = 1.0 / math.sqrt(samples * tables * narrows)
    down_grad, up_grad = spread_pieces(pieces, scale, factor_down.shape[0])
    return (logits, down_grad, up_grad, new_rows, new_accum)


def solution(mesh):
    in_specs = (
        P("table", None),
        P("table"),
        P("narrow", None),
        P("narrow", None),
        P(),
        P(),
        P(("table", "narrow")),
        P(("table", "narrow"), None),
        P(("table", "narrow"), None),
    )
    out_specs = (
        P(("table", "narrow")),
        P("narrow", None),
        P("narrow", None),
        P("table", None),
        P(("table", "narrow")),
    )
    return jax.shard_map(local, mesh=mesh, in_specs=in_specs, out_specs=out_specs, check_vma=False)
```

```python
import functools
import math

import jax
import jax.numpy as jnp
from jax import lax
from jax.experimental import pallas as pl
from jax.experimental.pallas import tpu as pltpu
from jax.sharding import PartitionSpec as P

FEAT = 8
HOT = 4


LEARN_RATE = 0.2
LOSS_SCALE = 32.0
ADA_EPS = 1e-06


SLOTS = 128
MIB = 1024 * 1024


def matmul(left, right):
    return jnp.dot(left, right, preferred_element_type=jnp.float32)


def transposed_dot(left, right):
    return lax.dot_general(
        left, right, (((0,), (0,)), ((), ())), preferred_element_type=jnp.float32
    )


def rows_dot(left, right):
    return lax.dot_general(
        left, right, (((1,), (1,)), ((), ())), preferred_element_type=jnp.float32
    )


def kernel_call(
    kernel, out_shape, cost, scratch=(), flags=0, operands=0, left=0, left_out=(), aliases=None, room=8
):
    flops, moved = cost
    smem = pl.BlockSpec(memory_space=pltpu.SMEM)
    vmem = pl.BlockSpec(memory_space=pltpu.VMEM)
    hbm = pl.BlockSpec(memory_space=pltpu.HBM)
    if isinstance(out_shape, tuple):
        out_specs = tuple(hbm if i in left_out else vmem for i in range(len(out_shape)))
    else:
        out_specs = hbm if left_out else vmem
    return pl.pallas_call(
        kernel,
        in_specs=[smem] * flags + [vmem] * operands + [hbm] * left,
        out_specs=out_specs,
        input_output_aliases=aliases or {},
        out_shape=out_shape,
        scratch_shapes=scratch,
        compiler_params=pltpu.CompilerParams(vmem_limit_bytes=room * MIB),
        cost_estimate=pl.CostEstimate(flops=flops, bytes_accessed=moved, transcendentals=0),
    )


def split_ids(ids):
    shifted = ids + 1
    high = lax.shift_right_logical(shifted, 5).astype(jnp.float32).astype(jnp.bfloat16)
    low = (shifted & 31).astype(jnp.float32).astype(jnp.bfloat16)
    return high, low


def lookup_choice():
    shape = (HOT * SLOTS, HOT * SLOTS)
    row = lax.broadcasted_iota(jnp.int32, shape, 0)
    column = lax.broadcasted_iota(jnp.int32, shape, 1)
    wanted = (row & (SLOTS - 1)) * HOT + lax.shift_right_logical(row, 7)
    return jnp.where(wanted == column, 1.0, 0.0).astype(jnp.bfloat16)


def joined(digits):
    high, low = digits
    return (high * 32.0 + low - 1.0).astype(jnp.int32)


def ones_where(mask):
    return jnp.where(mask, jnp.asarray(1, jnp.bfloat16), jnp.asarray(0, jnp.bfloat16))


def pool_kernel(part, swap_ref, ids_ref, first_ref, second_ref, *refs):
    out_ref, counts_ref, sums_ref, sem = refs[-4:]
    slots = counts_ref.shape[0]
    sources, _, pools, _ = out_ref.shape
    per_block = HOT * SLOTS
    if len(ids_ref.shape) == 3:
        ids = ids_ref[:, 0, part * per_block : (part + 1) * per_block]
    else:
        ids = ids_ref[:, part * per_block : (part + 1) * per_block]
    choice = lookup_choice()
    high, low = split_ids(ids)
    columns = joined((rows_dot(choice, high), rows_dot(choice, low))).astype(jnp.int16)
    half = first_ref.shape[0]
    position = lax.broadcasted_iota(jnp.int32, (SLOTS, 2 * half), 1) + swap_ref[0] * half
    position = jnp.where(position >= 2 * half, position - 2 * half, position).astype(jnp.int16)
    chunk = 2 * SLOTS
    for start in range(0, slots, chunk):
        for block in range(start // SLOTS, (start + chunk) // SLOTS):
            counts = None
            for lookup in range(HOT):
                column = columns[lookup * SLOTS : (lookup + 1) * SLOTS, block : block + 1]
                found = ones_where(column == position)
                counts = found if counts is None else counts + found
            counts_ref[block * SLOTS : (block + 1) * SLOTS, :] = counts
        here = slice(start, start + chunk)
        sums = matmul(counts_ref[here, :half], first_ref[...])
        sums = (sums + matmul(counts_ref[here, half:], second_ref[...])).astype(jnp.bfloat16)
        for source in range(start // pools, (start + chunk) // pools):
            at = source * pools - start
            sums_ref[source] = sums[at : at + pools]
    store = pltpu.make_async_copy(sums_ref, out_ref.at[:, part], sem)
    store.start()
    store.wait()


def pool_lookups(part, swap, ids, halves, pools, given=()):
    slots = ids.shape[0] * SLOTS
    row_dev, width = 2 * halves[0].shape[0], halves[0].shape[1]
    return kernel_call(
        functools.partial(pool_kernel, part),
        jax.ShapeDtypeStruct((slots // pools, 2, pools, width), jnp.bfloat16),
        (2 * slots * row_dev * width, 2 * row_dev * width + 2 * slots * width),
        [
            pltpu.VMEM((slots, row_dev), jnp.bfloat16),
            pltpu.VMEM((slots // pools, pools, width), jnp.bfloat16),
            pltpu.SemaphoreType.DMA,
        ],
        flags=1,
        operands=3,
        left=len(given),
        left_out=(0,),
        aliases={4: 0} if given else None,
        room=12,
    )(swap, ids, *halves, *given)


def row_grad_kernel(swap_ref, ids_ref, grads_ref, kept_ref, sent_ref, counts_ref, sums_ref):
    sources, _, emb = grads_ref.shape
    row_dev, slots = counts_ref.shape
    pools = slots // sources
    half = row_dev // 2
    per_block = HOT * SLOTS
    tile = 64
    choice = lookup_choice()
    position = lax.broadcasted_iota(jnp.int32, (tile, SLOTS), 0).astype(jnp.int16)
    for part in range(2):
        lanes = slice(part * per_block, (part + 1) * per_block)
        ids = ids_ref[:, 0, lanes] if len(ids_ref.shape) == 3 else ids_ref[:, lanes]
        high, low = split_ids(ids)
        lines = joined((rows_dot(high, choice), rows_dot(low, choice)))
        for block in range(slots // SLOTS):
            spread = []
            for lookup in range(HOT):
                line = lines[block : block + 1, lookup * SLOTS : (lookup + 1) * SLOTS]
                spread.append(jnp.broadcast_to(line, (tile, SLOTS)).astype(jnp.int16))
            for start in range(0, row_dev, tile):
                counts = None
                for lookup in range(HOT):
                    found = ones_where(spread[lookup] - jnp.asarray(start, jnp.int16) == position)
                    counts = found if counts is None else counts + found
                counts_ref[start : start + tile, block * SLOTS : (block + 1) * SLOTS] = counts
        grads = grads_ref[:, part * pools : (part + 1) * pools].reshape(slots, emb)
        where = slice(part * emb, (part + 1) * emb)
        sums_ref[:, where] = matmul(counts_ref[...], grads).astype(jnp.bfloat16)
    for out_ref, into_half in ((kept_ref, swap_ref[0]), (sent_ref, 1 - swap_ref[0])):
        out_ref[...] = sums_ref[pl.ds(pl.multiple_of(into_half * half, half), half), :]


def row_grads(swap, ids, slot_grads, pools, row_dev):
    sources, _, emb = slot_grads.shape
    slots = sources * pools
    half = jax.ShapeDtypeStruct((row_dev // 2, 2 * emb), jnp.bfloat16)
    return kernel_call(
        row_grad_kernel,
        (half, half),
        (4 * row_dev * slots * emb, 2 * slot_grads.size + 4 * row_dev * emb),
        [
            pltpu.VMEM((row_dev, slots), jnp.bfloat16),
            pltpu.VMEM((row_dev, 2 * emb), jnp.bfloat16),
        ],
        flags=1,
        operands=2,
        room=12,
    )(swap, ids, slot_grads)


def diagonal(size):
    row = lax.broadcasted_iota(jnp.int32, (size, size), 0)
    return row == lax.broadcasted_iota(jnp.int32, (size, size), 1)


def as_column(line):
    return jnp.sum(jnp.where(diagonal(line.shape[1]), line, 0.0), axis=1, keepdims=True)


def as_line(column):
    return jnp.sum(jnp.where(diagonal(column.shape[0]), column, 0.0), axis=0, keepdims=True)


def return_kernel(goals_ref, direct_ref, dhidden_ref, down_ref, out_ref, pick_ref, grads_ref):
    blocks = goals_ref.shape[0]
    bags, emb = grads_ref.shape
    samples = bags // FEAT
    for f in range(FEAT):
        part = slice(f * emb, (f + 1) * emb)
        back_term = rows_dot(dhidden_ref[...], down_ref[part, :])
        grads = direct_ref[:, part] + back_term
        grads_ref[f * samples : (f + 1) * samples, :] = grads.astype(jnp.bfloat16)
    high, low = split_ids(goals_ref[...])
    unit = ones_where(diagonal(SLOTS))
    columns = joined((rows_dot(unit, high), rows_dot(unit, low))).astype(jnp.int16)
    place = lax.broadcasted_iota(jnp.int32, (SLOTS, bags), 1)
    order = ((place % samples) * FEAT + place // samples).astype(jnp.int16)
    for block in range(0, blocks, 2):
        for one in (block, block + 1):
            pick_ref[one * SLOTS : (one + 1) * SLOTS, :] = ones_where(
                columns[:, one : one + 1] == order
            )
        here = slice(block * SLOTS, (block + 2) * SLOTS)
        out_ref[here, :] = matmul(pick_ref[here, :], grads_ref[...]).astype(jnp.bfloat16)


def return_grads(goals, direct, dhidden, down_full):
    samples, width = direct.shape
    emb = width // FEAT
    slot_count = goals.size
    return kernel_call(
        return_kernel,
        jax.ShapeDtypeStruct((slot_count, emb), jnp.bfloat16),
        (2 * slot_count * samples * width, 4 * direct.size + 2 * slot_count * emb),
        [
            pltpu.VMEM((slot_count, samples * FEAT), jnp.bfloat16),
            pltpu.VMEM((samples * FEAT, emb), jnp.bfloat16),
        ],
        operands=4,
        room=16,
    )(goals.reshape(slot_count // SLOTS, SLOTS), direct, dhidden, down_full)


def dense_kernel(
    swap_ref,
    goals_ref,
    bias_ref,
    weight_ref,
    target_ref,
    arrived_ref,
    down_ref,
    up_ref,
    logits_ref,
    direct_ref,
    dhidden_ref,
    kept_ref,
    sent_ref,
    place_ref,
    wide_ref,
    dcross_ref,
    shifted_ref,
):
    samples = target_ref.shape[1]
    width, rank = down_ref.shape
    emb = width // FEAT
    half = width // 2
    chunk = 512
    first_bag = lax.broadcasted_iota(jnp.int32, (samples, chunk), 0) * FEAT
    for start in range(0, goals_ref.shape[1], chunk):
        line = goals_ref[:, start : start + chunk]
        nth = (jnp.broadcast_to(line, (samples, chunk)) - first_bag).astype(jnp.int16)
        for f in range(FEAT):
            place_ref[f * samples : (f + 1) * samples, start : start + chunk] = ones_where(
                nth == jnp.asarray(f, jnp.int16)
            )
    features = [slice(f * emb, (f + 1) * emb) for f in range(FEAT)]
    for f, part in enumerate(features):
        spot = slice(f * samples, (f + 1) * samples)
        wide_ref[:, part] = matmul(place_ref[spot, :], arrived_ref[...]).astype(jnp.bfloat16)
    hidden = matmul(wide_ref[...], down_ref[...]).astype(jnp.bfloat16)
    summed = jnp.zeros((samples, emb), jnp.float32)
    for part in features:
        shifted = rows_dot(hidden, up_ref[part, :]) + bias_ref[:, part]
        shifted_ref[:, part] = shifted
        feats = wide_ref[:, part].astype(jnp.float32)
        summed = summed + (feats * shifted + feats) * weight_ref[:, part].astype(jnp.float32)
    logits = jnp.sum(summed, axis=1, keepdims=True)
    logits_ref[...] = as_line(logits)
    dlogit = LOSS_SCALE * (jax.nn.sigmoid(logits) - as_column(target_ref[...]))
    for part in features:
        dmixed = dlogit * weight_ref[:, part].astype(jnp.float32)
        feats = wide_ref[:, part].astype(jnp.float32)
        dcross_ref[:, part] = (dmixed * feats).astype(jnp.bfloat16)
        direct_ref[:, part] = dmixed * (shifted_ref[:, part] + 1.0)
    dhidden = matmul(dcross_ref[...], up_ref[...]).astype(jnp.bfloat16)
    dhidden_ref[...] = dhidden
    for step in range(FEAT):
        into_half = swap_ref[0] if step * emb < half else 1 - swap_ref[0]
        spot = (step * emb) % half
        part = pl.ds(pl.multiple_of(into_half * half + spot, emb), emb)
        out_ref = kept_ref if step * emb < half else sent_ref
        down_term = transposed_dot(wide_ref[:, part], dhidden)
        up_term = transposed_dot(dcross_ref[:, part], hidden)
        out_ref[spot : spot + emb, :rank] = down_term.astype(jnp.bfloat16)
        out_ref[spot : spot + emb, rank:] = up_term.astype(jnp.bfloat16)


def dense_step(swap, goals, arrived, down_full, up_full, bias, weight, target):
    samples = target.shape[0]
    slots, emb = arrived.shape
    width, rank = down_full.shape
    flops = 2 * slots * samples * width + 12 * samples * width * rank
    logits, direct, dhidden, kept, sent = kernel_call(
        dense_kernel,
        (
            jax.ShapeDtypeStruct((1, samples), jnp.float32),
            jax.ShapeDtypeStruct((samples, width), jnp.float32),
            jax.ShapeDtypeStruct((samples, rank), jnp.bfloat16),
            jax.ShapeDtypeStruct((width // 2, 2 * rank), jnp.bfloat16),
            jax.ShapeDtypeStruct((width // 2, 2 * rank), jnp.bfloat16),
        ),
        (flops, 2 * arrived.size + 8 * width * rank),
        [
            pltpu.VMEM((samples * FEAT, slots), jnp.bfloat16),
            pltpu.VMEM((samples, width), jnp.bfloat16),
            pltpu.VMEM((samples, width), jnp.bfloat16),
            pltpu.VMEM((samples, width), jnp.float32),
        ],
        flags=1,
        operands=7,
        room=20,
    )(
        swap,
        goals.reshape(1, slots),
        bias.reshape(1, width),
        weight.reshape(1, width),
        target.reshape(1, samples),
        arrived,
        down_full,
        up_full,
    )
    return logits.reshape(samples), direct, dhidden, kept, sent


def spread_kernel(count, scale, aliased, spots_ref, *refs):
    piece_refs = refs[:count]
    down_out_ref, up_out_ref, down_ref, up_ref, sems = refs[count + aliased :]
    rows = piece_refs[0].shape[0]
    rank = down_ref.shape[1]
    stores = []
    for i, piece_ref in enumerate(piece_refs):
        here = slice(i * rows, (i + 1) * rows)
        spot = pl.ds(pl.multiple_of(spots_ref[i] * rows, rows), rows)
        for half, (from_ref, to_ref) in enumerate(((down_ref, down_out_ref), (up_ref, up_out_ref))):
            part = slice(half * rank, (half + 1) * rank)
            from_ref[here, :] = piece_ref[:, part].astype(jnp.float32) * scale
            stores.append(
                pltpu.make_async_copy(from_ref.at[here, :], to_ref.at[spot, :], sems.at[len(stores)])
            )
            stores[-1].start()
    for store in stores:
        store.wait()


def spread_pieces(pieces, scale, rows, given=()):
    count = len(pieces)
    spots = jnp.stack([spot for spot, _ in pieces]).astype(jnp.int32)
    arrays = [piece for _, piece in pieces]
    step, both = arrays[0].shape
    rank = both // 2
    shape = jax.ShapeDtypeStruct((rows, rank), jnp.float32)
    block = pltpu.VMEM((count * step, rank), jnp.float32)
    return kernel_call(
        functools.partial(spread_kernel, count, scale, len(given)),
        (shape, shape),
        (count * step * both, 6 * count * step * both),
        [block, block, pltpu.SemaphoreType.DMA((2 * count,))],
        flags=1,
        operands=count,
        left=len(given),
        left_out=(0, 1),
        aliases={1 + count + i: i for i in range(len(given))},
    )(spots, *arrays, *given)


def update_kernel(rows_ref, far_ref, accum_ref, *refs):
    near_refs = refs[:-2]
    rows_out_ref, accum_out_ref = refs[-2:]
    emb = rows_ref.shape[1]
    for chunk in range(accum_ref.shape[0]):
        part = slice(chunk * SLOTS, (chunk + 1) * SLOTS)
        row_grad = far_ref[part, :].astype(jnp.float32)
        for near_ref in near_refs:
            row_grad = row_grad + near_ref[part, :emb].astype(jnp.float32)
        squares = jnp.mean(row_grad * row_grad, axis=1, keepdims=True)
        accum = as_column(accum_ref[chunk : chunk + 1, :]) + squares
        step = LEARN_RATE * row_grad * lax.rsqrt(accum + ADA_EPS)
        rows_out_ref[part, :] = (rows_ref[part, :].astype(jnp.float32) - step).astype(jnp.bfloat16)
        accum_out_ref[chunk : chunk + 1, :] = as_line(accum)


def update_rows(rows, far, accum, nears):
    share, emb = rows.shape
    chunks = share // SLOTS
    new_rows, new_accum = kernel_call(
        update_kernel,
        (
            jax.ShapeDtypeStruct((share, emb), jnp.bfloat16),
            jax.ShapeDtypeStruct((chunks, SLOTS), jnp.float32),
        ),
        (8 * rows.size, 8 * rows.size),
        operands=3 + len(nears),
    )(rows, far, accum.reshape(chunks, SLOTS), *nears)
    return new_rows, new_accum.reshape(share)


def join_kernel(swap_ref, mine_ref, other_ref, out_ref, sems):
    half = mine_ref.shape[0]
    copies = []
    for i, (from_ref, at) in enumerate(((mine_ref, swap_ref[0]), (other_ref, 1 - swap_ref[0]))):
        spot = pl.ds(pl.multiple_of(at * half, half), half)
        copies.append(pltpu.make_async_copy(from_ref, out_ref.at[spot, :], sems.at[i]))
        copies[-1].start()
    for copy in copies:
        copy.wait()


def join_halves(swap, mine, other):
    return kernel_call(
        join_kernel,
        jax.ShapeDtypeStruct((2 * mine.shape[0], mine.shape[1]), mine.dtype),
        (0, 8 * mine.size),
        [pltpu.SemaphoreType.DMA((2,))],
        flags=1,
        operands=2,
        left_out=(0,),
    )(swap, mine, other)


def group_levels(size):
    levels = []
    stride = 1
    while size % 4 == 0:
        levels.append((stride, 4))
        stride, size = stride * 4, size // 4
    if size > 1:
        levels.append((stride, size))
    return levels


def partner_index(index, stride, group, step):
    place = (index // stride) % group
    if group & (group - 1) == 0:
        other = place ^ step
    else:
        other = (place + step) % group
    return index + (other - place) * stride


def sent_from(axis, stride, group, step):
    size = lax.axis_size(axis)
    return [(partner_index(i, stride, group, step), i) for i in range(size)]


def scattered_pieces(blocks, axis, level):
    stride, group = level
    rows = blocks.shape[0] // group
    place = (lax.axis_index(axis) // stride) % group
    pieces = [lax.dynamic_slice_in_dim(blocks, place * rows, rows, 0)]
    for step in range(1, group):
        pairs = sent_from(axis, stride, group, step)
        if group & (group - 1) == 0:
            goal = place ^ step
        else:
            goal = (place + group - step) % group
        outgoing = lax.dynamic_slice_in_dim(blocks, goal * rows, rows, 0)
        pieces.append(lax.ppermute(outgoing, axis, pairs))
    return pieces


def summed(pieces):
    total = pieces[0].astype(jnp.float32)
    for piece in pieces[1:]:
        total = total + piece.astype(jnp.float32)
    return total.astype(jnp.bfloat16)


def scatter_sum(blocks, axis, levels):
    for level in levels:
        blocks = summed(scattered_pieces(blocks, axis, level))
    return blocks


def gathered_pieces(block, axis, level):
    stride, group = level
    index = lax.axis_index(axis)
    pieces = [((index // stride) % group, block)]
    for step in range(1, group):
        origin = partner_index(index, stride, group, step)
        came = lax.ppermute(block, axis, sent_from(axis, stride, group, step))
        pieces.append(((origin // stride) % group, came))
    return pieces


def gather_blocks(block, axis, levels):
    for level in levels:
        rows = block.shape[0]
        pieces = gathered_pieces(block, axis, level)
        block = jnp.zeros((len(pieces) * rows,) + block.shape[1:], block.dtype)
        for place, piece in pieces:
            block = lax.dynamic_update_slice_in_dim(block, piece, place * rows, 0)
    return block


def local(
    table_rows, accum, factor_down, factor_up, cross_bias, out_weight, target, bag_rows, slot_target
):
    tables = lax.axis_size("table")
    narrows = lax.axis_size("narrow")
    row_dev, emb_width = table_rows.shape
    pools_per = slot_target.shape[1]
    samples = target.shape[0]
    bag_count = samples * FEAT
    slot_count = tables * pools_per
    narrow_levels = group_levels(narrows)
    table_index = lax.axis_index("table")
    narrow_index = lax.axis_index("narrow")
    near_count = tables // 2
    half_levels = group_levels(near_count)
    far_half = table_index // near_count
    halves = [list(range(near_count)), list(range(near_count, tables))]
    across = [(i, (i + near_count) % tables) for i in range(tables)]
    paired = narrows == 2
    swap = (narrow_index if paired else narrow_index * 0).reshape(1)

    def near_and_far(rows):
        return tuple(
            lax.dynamic_slice_in_dim(rows, half * near_count, near_count, 0)
            for half in (far_half, 1 - far_half)
        )

    def in_order(near, far):
        return jnp.where(
            far_half == 0, jnp.concatenate([near, far]), jnp.concatenate([far, near])
        )

    def narrow_whole(block):
        if not paired:
            return gather_blocks(block, "narrow", narrow_levels)
        came = lax.ppermute(block, "narrow", sent_from("narrow", 1, 2, 1))
        first = jnp.where(narrow_index == 0, block, came)
        second = jnp.where(narrow_index == 0, came, block)
        return jnp.concatenate([first, second], axis=0)

    share_rows = row_dev // narrows
    own_halves = tuple(
        lax.dynamic_slice_in_dim(table_rows, half * (row_dev // 2), row_dev // 2, 0)
        for half in (swap[0], 1 - swap[0])
    )
    own_share = lax.dynamic_slice_in_dim(table_rows, narrow_index * share_rows, share_rows, 0)
    far_share = lax.ppermute(own_share, "table", across)
    down_full = narrow_whole(factor_down)
    up_full = narrow_whole(factor_up)

    per_window = bag_rows.shape[1]
    asked = jnp.concatenate(near_and_far(bag_rows), axis=1)[:, None, :]
    asked = lax.all_to_all(
        asked, "table", split_axis=0, concat_axis=0, tiled=True, axis_index_groups=halves
    )
    asked, far_share = lax.optimization_barrier((asked, far_share))
    if paired:
        came = lax.ppermute(far_share, "narrow", sent_from("narrow", 1, 2, 1))
        far_halves = (far_share, came)
    else:
        far_halves = tuple(jnp.split(narrow_whole(far_share), 2, axis=0))
    near_ids, far_ids = asked[:, 0, :per_window], asked[:, 0, per_window:]
    if per_window != SLOTS * HOT:
        by_block = (ids.reshape(-1, SLOTS * HOT) for ids in (near_ids, far_ids))
        asked = jnp.concatenate(tuple(by_block), axis=1)
    sums = pool_lookups(0, swap, asked, own_halves, pools_per)
    far_halves = lax.optimization_barrier((sums, *far_halves))
    sums, far_halves = far_halves[0], far_halves[1:]
    sums = pool_lookups(1, swap, asked, far_halves, pools_per, (sums,))
    arrived = lax.all_to_all(
        sums, "table", split_axis=0, concat_axis=0, tiled=True, axis_index_groups=halves
    )
    goals = jnp.stack(near_and_far(slot_target), axis=1)
    arrived, down_full, up_full, goals = lax.optimization_barrier(
        (arrived, down_full, up_full, goals)
    )
    logits, direct, dhidden, kept, sent = dense_step(
        swap,
        goals,
        arrived.reshape(slot_count, emb_width),
        down_full,
        up_full,
        cross_bias,
        out_weight,
        target,
    )
    if paired:
        came = lax.ppermute(sent, "narrow", sent_from("narrow", 1, 2, 1))
        narrow_sum = (kept.astype(jnp.float32) + came.astype(jnp.float32)).astype(jnp.bfloat16)
    else:
        narrow_sum = scatter_sum(jnp.concatenate([kept, sent], axis=0), "narrow", narrow_levels[::-1])
    slot_grads = return_grads(goals, direct, dhidden, down_full)
    groups = [group for _, group in half_levels]
    share_terms = narrow_sum.reshape(*groups, -1, narrow_sum.shape[1])
    order = list(range(len(groups)))[::-1] + [len(groups), len(groups) + 1]
    share_terms = share_terms.transpose(order).reshape(near_count, -1, narrow_sum.shape[1])
    rank = factor_down.shape[1]
    outgoing = [slot_grads.reshape(near_count, 2 * pools_per, emb_width)]
    outgoing += [share_terms[:, :, :rank], share_terms[:, :, rank:]]
    returned = lax.all_to_all(
        jnp.concatenate(outgoing, axis=1),
        "table",
        split_axis=0,
        concat_axis=0,
        tiled=True,
        axis_index_groups=halves,
    )
    terms = jnp.sum(returned[:, 2 * pools_per :].astype(jnp.float32), axis=0)
    half_sum = jnp.concatenate(jnp.split(terms, 2, axis=0), axis=1).astype(jnp.bfloat16)
    other_sum = lax.ppermute(half_sum, "table", across)
    mine, passed = row_grads(swap, asked, returned, pools_per, row_dev)
    other_sum, mine, passed = lax.optimization_barrier((other_sum, mine, passed))
    table_sum = summed([half_sum, other_sum])
    if paired:
        nears = [mine, lax.ppermute(passed, "narrow", sent_from("narrow", 1, 2, 1))]
    else:
        nears = [scatter_sum(jnp.concatenate([mine, passed], axis=0), "narrow", narrow_levels[::-1])]
    far_term = summed([term[:, emb_width:] for term in nears])
    inner = gather_blocks(table_sum, "table", half_levels[2:][::-1])
    blocks, fan = [(0, inner)], 1
    if len(half_levels) > 1:
        blocks, fan = gathered_pieces(inner, "table", half_levels[1]), half_levels[1][1]
    early, late = [], []
    for i, (place, block) in enumerate(blocks):
        pieces = gathered_pieces(block, "table", half_levels[0])
        pieces = [(spot * fan + place, piece) for spot, piece in pieces]
        early += pieces if i == 0 else pieces[:1]
        late += [] if i == 0 else pieces[1:]
    far_term = lax.ppermute(far_term, "table", across)
    scale = 1.0 / math.sqrt(samples * tables * narrows)
    grads = spread_pieces(early, scale, factor_down.shape[0])
    spots = [spot for spot, _ in late]
    far_term, down_grad, up_grad, *came = lax.optimization_barrier(
        (far_term, *grads, *(piece for _, piece in late))
    )
    own_accum = lax.dynamic_slice_in_dim(accum, narrow_index * share_rows, share_rows, 0)
    new_share, new_accum = update_rows(own_share, far_term, own_accum, nears)
    if paired:
        other_share = lax.ppermute(new_share, "narrow", sent_from("narrow", 1, 2, 1))
        new_rows = join_halves(swap, new_share, other_share)
    else:
        new_rows = gather_blocks(new_share, "narrow", narrow_levels)
    if late:
        down_grad, up_grad = spread_pieces(
            list(zip(spots, came)), scale, factor_down.shape[0], (down_grad, up_grad)
        )
    return (logits, down_grad, up_grad, new_rows, new_accum)


def solution(mesh):
    in_specs = (
        P("table", None),
        P("table"),
        P("narrow", None),
        P("narrow", None),
        P(),
        P(),
        P(("table", "narrow")),
        P(("table", "narrow"), None),
        P(("table", "narrow"), None),
    )
    out_specs = (
        P(("table", "narrow")),
        P("narrow", None),
        P("narrow", None),
        P("table", None),
        P(("table", "narrow")),
    )
    return jax.shard_map(local, mesh=mesh, in_specs=in_specs, out_specs=out_specs, check_vma=False)
```
